32 devices in a mesh: fsdp: 8 (over z, y), tp: 4 (over x, core).
Axes of the slice: x: 2, y: 2, z: 4, core: 2. Of those that a mesh axis runs over, the one named last changes fastest.
Arguments:
- hidden_in: bfloat16 [10240, 4096], P(('fsdp', 'tp')), may hold values from -6 to 6
- segment_ids: int32 [8, 1280], P('fsdp'), may hold values from 0 to 9, never falling along the last dimension, each value on 1 to 640 neighbouring positions
- qkv_weight: bfloat16 [4096, 3, 4096], P('fsdp', None, 'tp'), may hold values from -0.5 to 0.5
- out_weight: bfloat16 [4096, 4096], P('tp', 'fsdp'), may hold values from -0.375 to 0.375
- up_weight: bfloat16 [4096, 16384], P('fsdp', 'tp'), may hold values from -0.09375 to 0.09375
- down_weight: bfloat16 [16384, 4096], P('tp', 'fsdp'), may hold values from -0.046875 to 0.046875
- norm1_gain: bfloat16 [4096], P('fsdp'), may hold values from 0.25 to 1.75
- norm2_gain: bfloat16 [4096], P('fsdp'), may hold values from 0.25 to 1.75
- out_cotangent: bfloat16 [10240, 4096], P(('fsdp', 'tp')), may hold values from -6 to 6
Outputs:
- block_out: bfloat16 [10240, 4096], P(('fsdp', 'tp'))
- grad_in: float32 [10240, 4096], P(('fsdp', 'tp'))
- grad_norm1: float32 [4096], P(('fsdp', 'tp'))
- grad_norm2: float32 [4096], P(('fsdp', 'tp'))
- grad_qkv: float32 [4096, 3, 4096], P('fsdp', None, 'tp')
- grad_outproj: float32 [4096, 4096], P('tp', 'fsdp')
- grad_up: float32 [4096, 16384], P('fsdp', 'tp')
- grad_down: float32 [16384, 4096], P('tp', 'fsdp')
The draws below stay inside these ranges and needn't reach their ends.
Inputs may be any that keep to these rules, and one draw needn't show every extreme that they name: `segment_ids`: along each sequence the numbers never fall; equal numbers mark one document of 1 to 640 positions, and one document of every sequence has 640.
All inputs are finite; a program needn't handle non-finite values.
Results may differ from the reference program's by a relative error of at most 0.015.
Values may be sent and summed in bfloat16 or wider, within the bound.
No kernel may reach another device: no remote copies, remote signals or barrier semaphores. Data moves between devices by JAX's collectives and lax.ppermute only.
A program may use at most 512 MiB of HBM per device.

```python
import math
import jax
import jax.numpy as jnp
import numpy as np
from jax import lax

D = 4096
H = 32
FF = 16384
SEQ_LEN = 1280
SEQS = 8
TOKENS = 10240


def draw_qkv_weight(key, part):
    weights = jax.random.normal(key, (D, 3, D), jnp.float32) / math.sqrt(D)
    weights = jnp.clip(weights, -0.5, 0.5)
    return weights.astype(jnp.bfloat16)


def shard_levels(stream_key, dims, shards, smallest, largest):
    def one(position, blocks):
        steps = jax.random.uniform(jax.random.fold_in(jax.random.fold_in(stream_key, 6), position), (blocks,), jnp.float32, smallest / len(shards), largest / len(shards))
        return jnp.repeat(jnp.exp(steps), dims[position] // blocks).reshape((-1,) + (1,) * (len(dims) - position - 1))

    loudness = one(*shards[0])
    for cut in shards[1:]:
        loudness = loudness * one(*cut)
    return loudness


def split_up(count, total, bound, skew):
    portions = [(1 << 20) // math.isqrt(rank ** skew) + 1 for rank in range(2, count + 1)]
    surplus, holding = total - bound - (count - 1), [1] * (count - 1)
    while surplus > 0:
        movable = [i for i in range(count - 1) if holding[i] < bound]
        whole, left = sum([portions[i] for i in movable]), surplus
        for i in movable:
            addition = min(bound - holding[i], max(1, left * portions[i] // whole), surplus)
            holding[i] = holding[i] + addition
            surplus = surplus - addition
    return np.array([bound] + holding)


def ragged(key, count, total, reach, skew):
    if count == 2:
        one = jax.random.randint(key, (), max(1, total - reach), min(reach, total - 1) + 1)
        return jnp.stack([one, total - one])
    sizes = jnp.asarray(split_up(count, total, reach, skew), jnp.int32)
    couples = (count - 1) // 2
    giver, taker = sizes[1:1 + 2 * couples:2], sizes[2:2 + 2 * couples:2]
    room = jnp.minimum(giver - 1, reach - taker)
    shifted = jax.random.randint(jax.random.fold_in(key, 1), (couples,), 0, 1 << 20) % (room + 1)
    sizes = sizes.at[1:1 + 2 * couples:2].set(giver - shifted).at[2:2 + 2 * couples:2].set(taker + shifted)
    return sizes[jax.random.permutation(jax.random.fold_in(key, 2), count)]


def normal_values(rng, extent, deviation, most, split=(), kind=jnp.bfloat16):
    entries = jax.random.normal(rng, extent, jnp.float32) * deviation
    if len(split) > 0:
        entries = shard_levels(rng, extent, split, -0.22, 0.18) * entries
    return jnp.clip(entries, min=-most, max=most).astype(kind)


def setup_inputs(seed: int = 0) -> dict:
    arg_keys = jax.random.split(jax.random.key(seed), 10)
    return {
        "hidden_in": normal_values(arg_keys[0], (TOKENS, D), 1.0, 6.0, ((0, 32),)),
        "segment_ids": jax.vmap(lambda own: jnp.searchsorted(jnp.cumsum(ragged(own, max(4, SEQ_LEN // 128), SEQ_LEN, SEQ_LEN // 2, 2)), jnp.arange(SEQ_LEN), side="right"))(jax.random.split(arg_keys[1], SEQS)).reshape((SEQS, SEQ_LEN)).astype(jnp.int32),
        "qkv_weight": draw_qkv_weight(jax.random.fold_in(arg_keys[9], 71), 0),
        "out_weight": normal_values(arg_keys[3], (D, D), (D // 16) ** -0.5, 0.375, ((0, 4), (1, 8))),
        "up_weight": normal_values(arg_keys[4], (D, FF), D ** -0.5, 0.09375, ((0, 8), (1, 4))),
        "down_weight": normal_values(arg_keys[5], (FF, D), FF ** -0.5, 0.046875, ((0, 4), (1, 8))),
        "norm1_gain": jnp.clip(1.0 + 0.15 * jax.random.normal(arg_keys[6], (D,), jnp.float32), 0.25, 1.75).astype(jnp.bfloat16),
        "norm2_gain": jnp.clip(1.0 + 0.15 * jax.random.normal(arg_keys[7], (D,), jnp.float32), 0.25, 1.75).astype(jnp.bfloat16),
        "out_cotangent": normal_values(arg_keys[8], (TOKENS, D), 1.0, 6.0, ((0, 32),)),
    }


NORM_EPSILON = 1e-05
SQRT_HALF = 0.7071067811865476
INV_ROOT_TWO_PI = 0.3989422804014327

def norm_forward(values_in):
    row_mean = lax.optimization_barrier(jnp.mean(values_in, axis=-1, keepdims=True))
    centred = values_in - row_mean
    row_variance = lax.optimization_barrier(jnp.mean(centred * centred, axis=-1, keepdims=True))
    inverse = lax.rsqrt(row_variance + NORM_EPSILON)
    return (centred * inverse, inverse)

def norm_backward(grad_out, normed, inverse, gain):
    grad_gain = lax.optimization_barrier(jnp.sum(grad_out * normed, axis=0))
    scaled = grad_out * gain
    mean_one = lax.optimization_barrier(jnp.mean(scaled, axis=-1, keepdims=True))
    mean_two = lax.optimization_barrier(jnp.mean(scaled * normed, axis=-1, keepdims=True))
    return (inverse * (scaled - mean_one - normed * mean_two), grad_gain)

def gelu_value(pre_act):
    return 0.5 * pre_act * (1.0 + jax.scipy.special.erf(pre_act * SQRT_HALF))

def gelu_slope(pre_act):
    return 0.5 * (1.0 + jax.scipy.special.erf(pre_act * SQRT_HALF)) + pre_act * jnp.exp(-0.5 * pre_act * pre_act) * INV_ROOT_TWO_PI

def attention_scores(queries, keys_all, slopes, positions, document, score_scale):
    scores = jnp.einsum('qhd,khd->hqk', queries.astype(jnp.float32), keys_all.astype(jnp.float32))
    distance = (positions[:, None] - positions[None, :]).astype(jnp.float32)
    scores = scores * score_scale - slopes[:, None, None] * distance[None]
    allowed = (positions[None, :] <= positions[:, None]) & (document[:, None] == document[None, :])
    return jnp.where(allowed[None], scores, -1e+30)

def sequence_layer(hidden, document, cotangent, weights):
    w_qkv, w_out, w_up, w_down, gain_one, gain_two = weights
    head_width = D // H
    score_scale = 1.0 / math.sqrt(head_width)
    slopes = 2.0 ** (-8.0 * jnp.arange(1, H + 1).astype(jnp.float32) / H)
    positions = jnp.arange(SEQ_LEN)
    hidden_f = hidden.astype(jnp.float32)
    normed_one, inverse_one = norm_forward(hidden_f)
    input_one = (normed_one * gain_one).astype(jnp.bfloat16)
    projected = jnp.dot(input_one, w_qkv, preferred_element_type=jnp.float32).astype(jnp.bfloat16)
    projected = projected.reshape(SEQ_LEN, 3, H, head_width)
    queries = projected[:, 0]
    keys_all = projected[:, 1]
    values_all = projected[:, 2]
    scores = attention_scores(queries, keys_all, slopes, positions, document, score_scale)
    row_peak = lax.optimization_barrier(jnp.max(scores, axis=-1, keepdims=True))
    log_total = row_peak + jnp.log(lax.optimization_barrier(jnp.sum(jnp.exp(scores - row_peak), axis=-1, keepdims=True)))
    prob_full = jnp.exp(scores - log_total)
    attn_probs = prob_full.astype(jnp.bfloat16)
    attended = jnp.einsum('hqk,khd->qhd', attn_probs.astype(jnp.float32), values_all.astype(jnp.float32))
    attended = attended.astype(jnp.bfloat16).reshape(SEQ_LEN, D)
    resid_one = hidden_f + jnp.dot(attended, w_out, preferred_element_type=jnp.float32)
    normed_two, inverse_two = norm_forward(resid_one)
    input_two = (normed_two * gain_two).astype(jnp.bfloat16)
    pre_act = jnp.dot(input_two, w_up, preferred_element_type=jnp.float32)
    activated = gelu_value(pre_act).astype(jnp.bfloat16)
    block_out = (resid_one + jnp.dot(activated, w_down, preferred_element_type=jnp.float32)).astype(jnp.bfloat16)
    grad_down = jnp.dot(activated.T, cotangent, preferred_element_type=jnp.float32)
    grad_act = jnp.dot(cotangent, w_down.T, preferred_element_type=jnp.float32)
    grad_pre = (grad_act * gelu_slope(pre_act)).astype(jnp.bfloat16)
    grad_up = jnp.dot(input_two.T, grad_pre, preferred_element_type=jnp.float32)
    grad_in_two = jnp.dot(grad_pre, w_up.T, preferred_element_type=jnp.float32)
    grad_resid_part, grad_gain_two = norm_backward(grad_in_two, normed_two, inverse_two, gain_two)
    grad_resid = cotangent.astype(jnp.float32) + grad_resid_part
    grad_rows = grad_resid.astype(jnp.bfloat16)
    grad_out = jnp.dot(attended.T, grad_rows, preferred_element_type=jnp.float32)
    grad_attended = jnp.dot(grad_rows, w_out.T, preferred_element_type=jnp.float32).astype(jnp.bfloat16)
    grad_attended = grad_attended.reshape(SEQ_LEN, H, head_width)
    grad_probs = jnp.einsum('qhd,khd->hqk', grad_attended.astype(jnp.float32), values_all.astype(jnp.float32))
    row_dot = lax.optimization_barrier(jnp.sum(prob_full * grad_probs, axis=-1, keepdims=True))
    grad_scores = (prob_full * (grad_probs - row_dot) * score_scale).astype(jnp.bfloat16)
    grad_query = jnp.einsum('hqk,khd->qhd', grad_scores.astype(jnp.float32), keys_all.astype(jnp.float32)).astype(jnp.bfloat16)
    grad_key = jnp.einsum('hqk,qhd->khd', grad_scores.astype(jnp.float32), queries.astype(jnp.float32)).astype(jnp.bfloat16)
    grad_value = jnp.einsum('hqk,qhd->khd', attn_probs.astype(jnp.float32), grad_attended.astype(jnp.float32)).astype(jnp.bfloat16)
    grad_proj = jnp.stack([grad_query, grad_key, grad_value], axis=1).reshape(SEQ_LEN, 3 * D)
    grad_qkv = jnp.dot(input_one.T, grad_proj, preferred_element_type=jnp.float32)
    grad_in_one = jnp.dot(grad_proj, w_qkv.T, preferred_element_type=jnp.float32)
    grad_hidden_part, grad_gain_one = norm_backward(grad_in_one, normed_one, inverse_one, gain_one)
    grad_in = grad_resid + grad_hidden_part
    grads = (grad_qkv, grad_out, grad_up, grad_down, grad_gain_one, grad_gain_two)
    return (block_out, grad_in, grads)

def reference(hidden_in, segment_ids, qkv_weight, out_weight, up_weight, down_weight, norm1_gain, norm2_gain, out_cotangent):
    weights = (qkv_weight.reshape(D, 3 * D), out_weight, up_weight, down_weight, norm1_gain.astype(jnp.float32), norm2_gain.astype(jnp.float32))

    def one_sequence(totals, inputs):
        hidden, document, cotangent = inputs
        block_out, grad_in, grads = sequence_layer(hidden, document, cotangent, weights)
        totals = tuple((total + grad for total, grad in zip(totals, grads)))
        return (totals, (block_out, grad_in))
    start = (jnp.zeros((D, 3 * D), jnp.float32), jnp.zeros((D, D), jnp.float32), jnp.zeros((D, FF), jnp.float32), jnp.zeros((FF, D), jnp.float32), jnp.zeros((D,), jnp.float32), jnp.zeros((D,), jnp.float32))
    totals, outputs = lax.scan(one_sequence, start, (hidden_in.reshape(SEQS, SEQ_LEN, D), segment_ids, out_cotangent.reshape(SEQS, SEQ_LEN, D)))
    block_out = outputs[0].reshape(TOKENS, D)
    grad_in = outputs[1].reshape(TOKENS, D)
    return (block_out, grad_in, totals[4], totals[5], totals[0].reshape(D, 3, D), totals[1], totals[2], totals[3])
```

```python
import math

import jax
import jax.numpy as jnp
from jax import lax
from jax.experimental import pallas as pl
from jax.experimental.pallas import tpu as pltpu
from jax.sharding import PartitionSpec as P

D = 4096
H = 32
HEAD = D // H
REACH = 640
NORM_EPSILON = 1e-05
SQRT_HALF = 0.7071067811865476
INV_ROOT_TWO_PI = 0.3989422804014327
BF = jnp.bfloat16
F32 = jnp.float32


def norm_forward(values_in):
    row_mean = jnp.mean(values_in, axis=-1, keepdims=True)
    centred = values_in - row_mean
    row_variance = jnp.mean(centred * centred, axis=-1, keepdims=True)
    inverse = lax.rsqrt(row_variance + NORM_EPSILON)
    return centred * inverse, inverse


def norm_backward(grad_out, normed, inverse, gain):
    grad_gain = jnp.sum(grad_out * normed, axis=0)
    scaled = grad_out * gain
    mean_one = jnp.mean(scaled, axis=-1, keepdims=True)
    mean_two = jnp.mean(scaled * normed, axis=-1, keepdims=True)
    return inverse * (scaled - mean_one - normed * mean_two), grad_gain


def gelu_value(pre_act):
    return 0.5 * pre_act * (1.0 + jax.scipy.special.erf(pre_act * SQRT_HALF))


def gelu_slope(pre_act):
    return (
        0.5 * (1.0 + jax.scipy.special.erf(pre_act * SQRT_HALF))
        + pre_act * jnp.exp(-0.5 * pre_act * pre_act) * INV_ROOT_TWO_PI
    )


def dot(left, right, cl, cr):
    return lax.dot_general(left, right, (((cl,), (cr,)), ((), ())), preferred_element_type=F32)


QB = 256


def window(first):
    low = max(0, first - REACH)
    return low, first + QB - low


def masked_scores(q, k, start, slope, first, low, width, scale):
    scores = dot(q, k, 1, 1)
    row = first + lax.broadcasted_iota(jnp.int32, (QB, width), 0)
    col = low + lax.broadcasted_iota(jnp.int32, (QB, width), 1)
    scores = scores * scale - slope * (row - col).astype(F32)
    return jnp.where((col >= start) & (col <= row), scores, -1e30)


def load_ordered(ref, scratches, turn, piece):
    for i in range(4):
        rel = lax.bitwise_xor(jnp.int32(i), turn)
        block = ref[lax.bitwise_and(rel, 1), 0, lax.shift_right_logical(rel, 1)]
        for j, scratch in enumerate(scratches):
            scratch[i * piece : (i + 1) * piece, :] = block[:, j * HEAD : (j + 1) * HEAD]


def attention_forward(turn_ref, slope_ref, qkv_ref, start_ref, o_ref, lse_ref, q_s, k_s, v_s, o_s):
    turn = turn_ref[0]
    slope = slope_ref[pl.program_id(1)]
    sequence = q_s.shape[0]
    piece = sequence // 4
    scale = 1.0 / math.sqrt(HEAD)
    load_ordered(qkv_ref, (q_s, k_s, v_s), turn, piece)
    for first in range(0, sequence, QB):
        low, width = window(first)
        scores = masked_scores(
            q_s[first : first + QB, :],
            k_s[low : low + width, :],
            start_ref[0, first : first + QB, :],
            slope,
            first,
            low,
            width,
            scale,
        )
        peak = jnp.max(scores, axis=-1, keepdims=True)
        weights = jnp.exp(scores - peak)
        total = jnp.sum(weights, axis=-1, keepdims=True)
        lse_ref[0, 0, first : first + QB, :] = peak + jnp.log(total)
        probs = (weights * (1.0 / total)).astype(BF)
        o_s[first : first + QB, :] = dot(probs, v_s[low : low + width, :], 1, 0).astype(BF)
    for i in range(4):
        rel = lax.bitwise_xor(jnp.int32(i), turn)
        o_ref[lax.bitwise_and(rel, 1), 0, lax.shift_right_logical(rel, 1)] = o_s[
            i * piece : (i + 1) * piece, :
        ]


def attention_backward(
    turn_ref, slope_ref, qkv_ref, do_ref, start_ref, lse_ref, out_ref, q_s, k_s, v_s, do_s, dq_s, dk_s, dv_s
):
    turn = turn_ref[0]
    slope = slope_ref[pl.program_id(1)]
    sequence = q_s.shape[0]
    piece = sequence // 4
    scale = 1.0 / math.sqrt(HEAD)
    load_ordered(qkv_ref, (q_s, k_s, v_s), turn, piece)
    load_ordered(do_ref, (do_s,), turn, piece)
    dk_s[...] = jnp.zeros_like(dk_s)
    dv_s[...] = jnp.zeros_like(dv_s)
    for first in range(0, sequence, QB):
        low, width = window(first)
        keys = k_s[low : low + width, :]
        query = q_s[first : first + QB, :]
        grad = do_s[first : first + QB, :]
        scores = masked_scores(
            query, keys, start_ref[0, first : first + QB, :], slope, first, low, width, scale
        )
        probs = jnp.exp(scores - lse_ref[0, 0, first : first + QB, :])
        grad_probs = dot(grad, v_s[low : low + width, :], 1, 1)
        delta = jnp.sum(probs * grad_probs, axis=-1, keepdims=True)
        grad_scores = (probs * (grad_probs - delta) * scale).astype(BF)
        dq_s[first : first + QB, :] = dot(grad_scores, keys, 1, 0).astype(BF)
        dk_s[low : low + width, :] += dot(grad_scores, query, 0, 0)
        dv_s[low : low + width, :] += dot(probs.astype(BF), grad, 0, 0)
    for i in range(4):
        rel = lax.bitwise_xor(jnp.int32(i), turn)
        rows = slice(i * piece, (i + 1) * piece)
        at = (lax.bitwise_and(rel, 1), 0, lax.shift_right_logical(rel, 1))
        out_ref[(*at, slice(None), slice(0, HEAD))] = dq_s[rows, :]
        out_ref[(*at, slice(None), slice(HEAD, 2 * HEAD))] = dk_s[rows, :].astype(BF)
        out_ref[(*at, slice(None), slice(2 * HEAD, 3 * HEAD))] = dv_s[rows, :].astype(BF)


def on_device(
    hidden_in,
    segment_ids,
    qkv_weight,
    out_weight,
    up_weight,
    down_weight,
    norm1_gain,
    norm2_gain,
    out_cotangent,
):
    n = lax.axis_size("fsdp")
    tp = lax.axis_size("tp")
    ring = n // 4
    f = lax.axis_index("fsdp")
    t = lax.axis_index("tp")
    y, zl, zh = f & 1, (f >> 1) & 1, f >> 2
    low_half = zl == 0
    piece = hidden_in.shape[0]
    sequence = piece * tp
    heads = H // tp // 2
    width = heads * HEAD
    unit = D // n

    def over(axis, to, size):
        return lambda v: lax.ppermute(v, axis, [(i, to(i)) for i in range(size)])

    pp_core = over("tp", lambda i: i ^ 1, tp)
    pp_x = over("tp", lambda i: i ^ 2, tp)
    pp_zl = over("fsdp", lambda i: i ^ 2, n)
    pp_y = over("fsdp", lambda i: i ^ 1, n)
    pp_up = over("fsdp", lambda i: (i + 4) % n, n)
    pp_down = over("fsdp", lambda i: (i - 4) % n, n)

    def to_rel(v):
        cols = [v[..., b * unit : (b + 1) * unit] for b in range(n)]

        def pick(k, j, l):
            chosen = None
            for a in range(ring):
                both = jnp.where(y == j, cols[a * 4 + l * 2], cols[a * 4 + l * 2 + 1])
                chosen = both if chosen is None else jnp.where((zh - k) % ring == a, both, chosen)
            return chosen

        return jnp.concatenate(
            [pick(k, j, l) for k in range(ring) for j in range(2) for l in range(2)], axis=-1
        )

    def from_rel(v):
        cols = [v[..., b * unit : (b + 1) * unit] for b in range(n)]

        def pick(a, l, b):
            chosen = None
            for k in range(ring):
                both = jnp.where(y == b, cols[k * 4 + l], cols[k * 4 + 2 + l])
                chosen = both if chosen is None else jnp.where((zh - k) % ring == a, both, chosen)
            return chosen

        return jnp.concatenate(
            [pick(a, l, b) for a in range(ring) for l in range(2) for b in range(2)], axis=-1
        )

    def gather_blocks(block):
        chain = [block]
        for _ in range(ring - 1):
            chain.append(pp_up(chain[-1]))
        out = []
        for item in chain:
            out += [item, pp_y(item)]
        return out

    def gather_weight(mine, other, axis):
        blocks_mine = gather_blocks(mine)
        blocks_other = gather_blocks(pp_zl(other))
        cols = []
        for a, b in zip(blocks_mine, blocks_other):
            cols += [jnp.where(low_half, a, b), jnp.where(low_half, b, a)]
        return jnp.concatenate(cols, axis=axis)

    def reduce_weight(parts, axis):
        sums = [
            (parts[k][0].astype(F32) + pp_y(parts[k][1]).astype(F32)).astype(BF)
            for k in range(ring)
        ]
        value = sums[ring - 1]
        for k in range(ring - 2, -1, -1):
            value = (pp_down(value).astype(F32) + sums[k].astype(F32)).astype(BF)
        first, second = jnp.split(value, 2, axis=axis)
        keep = jnp.where(low_half, first, second)
        got = pp_zl(jnp.where(low_half, second, first))
        return keep, got

    def gather_rows(a):
        ax, az = pp_x(a), pp_zl(a)
        half = piece // 2
        top = pp_x(az[:half])
        bottom = pp_zl(ax[half:])
        ad = jnp.concatenate([top, bottom], axis=0)
        same = [a, ax, az, ad]
        return jnp.concatenate(same + [pp_core(v) for v in same], axis=0)

    def scatter_rows(near, far):
        e = (near + pp_core(far.astype(BF)).astype(F32)).astype(BF)
        half = piece // 2
        e00 = e[:piece]
        ex = e[piece : 2 * piece]
        ez = e[2 * piece : 3 * piece]
        ed = e[3 * piece :]
        from_x = pp_x(ed[:half])
        from_z = pp_zl(ed[half:])
        x_top = pp_x(ex[:half])
        z_bottom = pp_zl(ez[half:])
        x_bottom = pp_x((ex[half:].astype(F32) + from_z.astype(F32)).astype(BF))
        z_top = pp_zl((ez[:half].astype(F32) + from_x.astype(F32)).astype(BF))
        x_all = jnp.concatenate([x_top, x_bottom], axis=0).astype(F32)
        z_all = jnp.concatenate([z_top, z_bottom], axis=0).astype(F32)
        return e00.astype(F32) + x_all + z_all

    def rows_out(a, b, cl, cr):
        half = a.shape[0] // 2
        far = dot(a[half:], b, cl, cr)
        near = dot(a[:half], b, cl, cr)
        return scatter_rows(near, far)

    def halves(v, axis):
        first, second = jnp.split(v, 2, axis=axis)
        return jnp.where(low_half, first, second), jnp.where(low_half, second, first)

    qkv_heads = (
        qkv_weight.reshape(unit, 3, 2 * heads, HEAD)
        .transpose(0, 2, 1, 3)
        .reshape(unit, 2 * heads * 3 * HEAD)
    )
    w_qkv = gather_weight(*halves(qkv_heads, 1), 0)
    w_out = gather_weight(*halves(out_weight, 0), 1)
    w_up = gather_weight(*halves(up_weight, 1), 0)
    w_down = gather_weight(*halves(down_weight, 0), 1)

    gains = jnp.stack([norm1_gain, norm2_gain])
    gains = gather_weight(gains, gains, 1).astype(F32)
    gain_one, gain_two = gains[0], gains[1]

    documents = jnp.concatenate([segment_ids, pp_zl(segment_ids)], axis=0)
    starts = jnp.sum(
        (documents[:, None, :] < documents[:, :, None]).astype(jnp.int32), axis=-1
    )[:, :, None]
    turn = jnp.full((1,), t, jnp.int32)
    head_index = t * 2 * heads + zl * heads + jnp.arange(heads)
    slopes = 2.0 ** (-8.0 * (head_index + 1).astype(F32) / H)

    x = to_rel(hidden_in).astype(F32)
    cot = to_rel(out_cotangent)
    normed_one, inverse_one = norm_forward(x)
    rows_one = gather_rows((normed_one * gain_one).astype(BF))
    qkv = dot(rows_one, w_qkv, 1, 0).astype(BF).reshape(2, 2, 2, piece, 3 * width)

    def spec(cols):
        return pl.BlockSpec((2, 1, 2, piece, cols), lambda s, h, *_: (0, s, 0, 0, h))

    start_spec = pl.BlockSpec((1, sequence, 1), lambda s, h, *_: (s, 0, 0))
    lse_spec = pl.BlockSpec((1, 1, sequence, 1), lambda s, h, *_: (s, h, 0, 0))
    params = pltpu.CompilerParams(
        dimension_semantics=("arbitrary", "arbitrary"), vmem_limit_bytes=48 << 20
    )
    block = pltpu.VMEM((sequence, HEAD), BF)
    wide = pltpu.VMEM((sequence, HEAD), F32)
    pairs = 2 * heads
    area = sum(QB * window(i)[1] for i in range(0, sequence, QB)) * pairs
    attended, lse = pl.pallas_call(
        attention_forward,
        out_shape=(
            jax.ShapeDtypeStruct((2, 2, 2, piece, width), BF),
            jax.ShapeDtypeStruct((2, heads, sequence, 1), F32),
        ),
        grid_spec=pltpu.PrefetchScalarGridSpec(
            num_scalar_prefetch=2,
            grid=(2, heads),
            in_specs=[spec(3 * HEAD), start_spec],
            out_specs=[spec(HEAD), lse_spec],
            scratch_shapes=[block] * 4,
        ),
        compiler_params=params,
        cost_estimate=pl.CostEstimate(
            flops=4 * HEAD * area, transcendentals=area, bytes_accessed=2 * sequence * HEAD * 4 * pairs
        ),
        name="attention_forward",
    )(turn, slopes, qkv, starts)
    attended = attended.reshape(2 * sequence, width)
    resid = x + rows_out(attended, w_out, 1, 0)
    normed_two, inverse_two = norm_forward(resid)
    rows_two = gather_rows((normed_two * gain_two).astype(BF))
    pre_act = dot(rows_two, w_up, 1, 0)
    activated = gelu_value(pre_act).astype(BF)
    block_out = from_rel((resid + rows_out(activated, w_down, 1, 0)).astype(BF))

    cot_rows = gather_rows(cot)

    def grad_parts(make):
        return [[make(slice((k * 2 + j) * 2 * unit, (k * 2 + j + 1) * 2 * unit)).astype(BF) for j in range(2)] for k in range(ring)]

    keep, got = reduce_weight(grad_parts(lambda c: dot(activated, cot_rows[:, c], 0, 0)), 1)

    def joined(keep, got, axis):
        return jnp.concatenate(
            [jnp.where(low_half, keep, got), jnp.where(low_half, got, keep)], axis=axis
        ).astype(F32)

    grad_down = joined(keep, got, 0)
    grad_act = dot(cot_rows, w_down, 1, 1)
    grad_pre = (grad_act * gelu_slope(pre_act)).astype(BF)
    grad_up = joined(*reduce_weight(grad_parts(lambda c: dot(rows_two[:, c], grad_pre, 0, 0)), 0), 1)
    grad_in_two = rows_out(grad_pre, w_up, 1, 1)
    grad_part, grad_gain_two = norm_backward(grad_in_two, normed_two, inverse_two, gain_two)
    grad_resid = cot.astype(F32) + grad_part
    grad_rows = gather_rows(grad_resid.astype(BF))
    grad_attended = dot(grad_rows, w_out, 1, 1).astype(BF).reshape(2, 2, 2, piece, width)
    grad_out = joined(*reduce_weight(grad_parts(lambda c: dot(attended, grad_rows[:, c], 0, 0)), 1), 0)
    grad_proj = pl.pallas_call(
        attention_backward,
        out_shape=jax.ShapeDtypeStruct((2, 2, 2, piece, 3 * width), BF),
        grid_spec=pltpu.PrefetchScalarGridSpec(
            num_scalar_prefetch=2,
            grid=(2, heads),
            in_specs=[spec(3 * HEAD), spec(HEAD), start_spec, lse_spec],
            out_specs=spec(3 * HEAD),
            scratch_shapes=[block] * 5 + [wide] * 2,
        ),
        compiler_params=params,
        cost_estimate=pl.CostEstimate(
            flops=10 * HEAD * area, transcendentals=area, bytes_accessed=2 * sequence * HEAD * 7 * pairs
        ),
        name="attention_backward",
    )(turn, slopes, qkv, grad_attended, starts, lse)
    grad_proj = grad_proj.reshape(2 * sequence, 3 * width)
    keep, got = reduce_weight(grad_parts(lambda c: dot(rows_one[:, c], grad_proj, 0, 0)), 0)

    def parts_first(v):
        return v.reshape(unit, heads, 3, HEAD).transpose(0, 2, 1, 3).reshape(unit, 3, width)

    grad_qkv = joined(parts_first(keep), parts_first(got), 2)
    grad_in_one = rows_out(grad_proj, w_qkv, 1, 1)
    grad_part, grad_gain_one = norm_backward(grad_in_one, normed_one, inverse_one, gain_one)
    grad_in = from_rel(grad_resid + grad_part)

    def total(v):
        v = from_rel(v)
        for step in (pp_core, pp_x, pp_zl, pp_y):
            v = v + step(v)
        moving = v
        for _ in range(ring - 1):
            moving = pp_up(moving)
            v = v + moving
        size = D // (n * tp)
        return lax.dynamic_slice_in_dim(v, (f * tp + t) * size, size)

    return (
        block_out,
        grad_in,
        total(grad_gain_one),
        total(grad_gain_two),
        grad_qkv,
        grad_out,
        grad_up,
        grad_down,
    )


def solution(mesh):
    return jax.shard_map(
        on_device,
        mesh=mesh,
        in_specs=(
            P(("fsdp", "tp"), None),
            P("fsdp", None),
            P("fsdp", None, "tp"),
            P("tp", "fsdp"),
            P("fsdp", "tp"),
            P("tp", "fsdp"),
            P("fsdp"),
            P("fsdp"),
            P(("fsdp", "tp"), None),
        ),
        out_specs=(
            P(("fsdp", "tp"), None),
            P(("fsdp", "tp"), None),
            P(("fsdp", "tp")),
            P(("fsdp", "tp")),
            P("fsdp", None, "tp"),
            P("tp", "fsdp"),
            P("fsdp", "tp"),
            P("tp", "fsdp"),
        ),
        check_vma=False,
    )
```

```python
import functools
import math

import jax
import jax.numpy as jnp
from jax import lax
from jax.experimental import pallas as pl
from jax.experimental.pallas import tpu as pltpu
from jax.sharding import PartitionSpec as P

D = 4096
H = 32
HEAD = D // H
REACH = 640
NORM_EPSILON = 1e-05
SQRT_HALF = 0.7071067811865476
INV_ROOT_TWO_PI = 0.3989422804014327
BF = jnp.bfloat16
F32 = jnp.float32
COVER = 0.05
VMEM = 56 << 20


def norm_forward(values_in):
    row_mean = jnp.mean(values_in, axis=-1, keepdims=True)
    centred = values_in - row_mean
    row_variance = jnp.mean(centred * centred, axis=-1, keepdims=True)
    inverse = lax.rsqrt(row_variance + NORM_EPSILON)
    return centred * inverse, inverse


def norm_backward(grad_out, normed, inverse, gain):
    grad_gain = jnp.sum(grad_out * normed, axis=0)
    scaled = grad_out * gain
    mean_one = jnp.mean(scaled, axis=-1, keepdims=True)
    mean_two = jnp.mean(scaled * normed, axis=-1, keepdims=True)
    return inverse * (scaled - mean_one - normed * mean_two), grad_gain


def gelu_and_slope(pre_act):
    part = 0.5 * (1.0 + lax.erf(pre_act * SQRT_HALF))
    slope = part + pre_act * jnp.exp(-0.5 * pre_act * pre_act) * INV_ROOT_TWO_PI
    return pre_act * part, slope


def dot(left, right, cl, cr):
    return lax.dot_general(left, right, (((cl,), (cr,)), ((), ())), preferred_element_type=F32)


class Steps:
    def __init__(self):
        self.token = jnp.zeros((1,), F32)
        self.pending = []
        self.first = True

    def begin(self, value):
        if self.first:
            return value
        return lax.optimization_barrier((value, self.token))[0]

    def move(self, how, value):
        out = how(self.begin(value))
        self.pending.append(out)
        return out

    def run(self, how, value, *more, **named):
        out = how(self.begin(value), *more, **named)
        self.pending += jax.tree.leaves(out)
        return out

    def close(self):
        self.token = lax.optimization_barrier((self.token, *self.pending))[0]
        self.pending = []
        self.first = False


def params(grid_dims):
    return pltpu.CompilerParams(
        dimension_semantics=("arbitrary",) * grid_dims, vmem_limit_bytes=VMEM
    )


def cost(m, n, k):
    return pl.CostEstimate(
        flops=int(2 * m * n * k * COVER), transcendentals=0, bytes_accessed=2 * (m * k + k * n + m * n)
    )


def tile(size, most):
    if size <= most:
        return size
    while size % most:
        most -= 128
    return most


def stack_rows(*pieces):
    rows = math.gcd(*(v.shape[0] for v in pieces))
    cols = pieces[0].shape[1]
    sizes = [v.shape[0] // rows for v in pieces]
    firsts = [sum(sizes[:i]) for i in range(len(pieces))]

    def body(*refs):
        step = pl.program_id(0)
        for ref, first, size in zip(refs, firsts, sizes):

            @pl.when((step >= first) & (step < first + size))
            def _(ref=ref):
                refs[-1][...] = ref[...]

    def spec(first, size):
        return pl.BlockSpec((rows, cols), lambda g: (jnp.clip(g - first, 0, size - 1), 0))

    return pl.pallas_call(
        body,
        out_shape=jax.ShapeDtypeStruct((sum(sizes) * rows, cols), pieces[0].dtype),
        grid=(sum(sizes),),
        in_specs=[spec(f, s) for f, s in zip(firsts, sizes)],
        out_specs=pl.BlockSpec((rows, cols), lambda g: (g, 0)),
        compiler_params=params(1),
        name="stack_rows",
    )(*pieces)


def gram(a_pair, b_pair, blocks, side):
    rows = a_pair[0].shape[0]
    width = blocks[0][1]
    m = width if side == 0 else a_pair[0].shape[1]
    n = width if side == 1 else b_pair[0].shape[1]
    tm, tn = tile(m, 1024), tile(n, 1024)
    grid_m, grid_n = m // tm, n // tn
    count = len(blocks)
    per = grid_m * grid_n

    def at(g):
        p, r = g // per, g % per
        return p, r // grid_m, r % grid_m

    def body(index_ref, a0, a1, b0, b1, *outs):
        total = (dot(a0[...], b0[...], 0, 0) + dot(a1[...], b1[...], 0, 0)).astype(BF)
        p = pl.program_id(0) // per
        for q in range(count):

            @pl.when(p == q)
            def _(q=q):
                outs[q][...] = total

    def a_map(g, index):
        p, _, i = at(g)
        return 0, (index[p] * grid_m + i if side == 0 else i)

    def b_map(g, index):
        p, j, _ = at(g)
        return 0, (index[p] * grid_n + j if side == 1 else j)

    def out_map(q):
        def at_q(g, index):
            r = jnp.clip(g - q * per, 0, per - 1)
            return r % grid_m, r // grid_m

        return at_q

    return pl.pallas_call(
        body,
        out_shape=[jax.ShapeDtypeStruct((m, n), BF)] * count,
        grid_spec=pltpu.PrefetchScalarGridSpec(
            num_scalar_prefetch=1,
            grid=(count * per,),
            in_specs=[pl.BlockSpec((rows, tm), a_map)] * 2 + [pl.BlockSpec((rows, tn), b_map)] * 2,
            out_specs=[pl.BlockSpec((tm, tn), out_map(q)) for q in range(count)],
        ),
        compiler_params=params(1),
        cost_estimate=cost(m, n * count, 2 * rows),
        name="gram",
    )(jnp.array([b[0] for b in blocks], jnp.int32), *a_pair, *b_pair)


def deep(a, blocks, starts, cr, finish=None, extra=(), outs=1, tm=640, tn=512, parts=1):
    m = a.shape[0]
    n = blocks[0].shape[1 - cr]
    count = len(blocks)
    tm, tn = tile(m, tm), tile(n, tn)
    rows = tm // parts

    def body(starts_ref, a_ref, *rest):
        def part(r):
            total = None
            for p in range(count):
                size = blocks[p].shape[cr]
                at = pl.multiple_of(starts_ref[p] * 128, 128)
                term = dot(a_ref[r * rows : (r + 1) * rows, pl.ds(at, size)], rest[p][...], 1, cr)
                total = term if total is None else total + term
            return total

        def store(r, total):
            at = slice(r * rows, (r + 1) * rows)
            values = (total,) if finish is None else finish(total, *(v[at, :] for v in rest[count:-outs]))
            for ref, value in zip(rest[-outs:], values):
                ref[at, :] = value.astype(BF)

        before = None
        for r in range(parts):
            total = part(r)
            if before is not None:
                store(r - 1, before)
            before = total
        store(parts - 1, before)

    def w_spec(w):
        size = w.shape[cr]
        if cr == 0:
            return pl.BlockSpec((size, tn), lambda j, i, *_: (0, j))
        return pl.BlockSpec((tn, size), lambda j, i, *_: (j, 0))

    out = pl.BlockSpec((tm, tn), lambda j, i, *_: (i, j))
    result = pl.pallas_call(
        body,
        out_shape=[jax.ShapeDtypeStruct((m, n), BF)] * outs,
        grid_spec=pltpu.PrefetchScalarGridSpec(
            num_scalar_prefetch=1,
            grid=(n // tn, m // tm),
            in_specs=[pl.BlockSpec((tm, a.shape[1]), lambda j, i, *_: (i, 0))]
            + [w_spec(w) for w in blocks]
            + [out] * len(extra),
            out_specs=[out] * outs,
        ),
        compiler_params=params(2),
        cost_estimate=cost(m, n, a.shape[1]),
        name="deep",
    )(starts, a, *blocks, *extra)
    return result[0] if outs == 1 else result


def broad(a, blocks, starts, cr, add=None):
    m, k = a.shape
    n = sum(w.shape[1 - cr] for w in blocks)
    count = len(blocks)
    tm = tile(m, 320)

    def body(starts_ref, a_ref, *rest):
        for p in range(count):
            size = blocks[p].shape[1 - cr]
            at = pl.multiple_of(starts_ref[p] * 128, 128)
            part = dot(a_ref[...], rest[p][...], 1, cr)
            if add is not None:
                part = part + rest[count][:, pl.ds(at, size)].astype(F32)
            rest[-1][:, pl.ds(at, size)] = part.astype(BF)

    out = pl.BlockSpec((tm, n), lambda i, *_: (i, 0))
    return pl.pallas_call(
        body,
        out_shape=jax.ShapeDtypeStruct((m, n), BF),
        grid_spec=pltpu.PrefetchScalarGridSpec(
            num_scalar_prefetch=1,
            grid=(m // tm,),
            in_specs=[pl.BlockSpec((tm, k), lambda i, *_: (i, 0))]
            + [pl.BlockSpec(w.shape, lambda i, *_: (0, 0), pipeline_mode=pl.Buffered(1)) for w in blocks]
            + ([out] if add is not None else []),
            out_specs=out,
        ),
        compiler_params=params(1),
        cost_estimate=cost(m, n, k),
        name="broad",
    )(starts, a, *blocks, *(() if add is None else (add,)))


QB = 256


def window(first):
    low = max(0, first - REACH)
    return low, first + QB - low


def masked_scores(q, k, start, slope, first, low, width, scale):
    scores = dot(q, k, 1, 1)
    row = first + lax.broadcasted_iota(jnp.int32, (QB, width), 0)
    col = low + lax.broadcasted_iota(jnp.int32, (QB, width), 1)
    scores = scores * scale - slope * (row - col).astype(F32)
    return jnp.where((col >= start) & (col <= row), scores, -1e30)


def in_order(turn, visit):
    for c in range(2):

        @pl.when(lax.bitwise_and(turn, 1) == c)
        def _(c=c):
            for i in range(4):
                visit(i, (i & 1) ^ c, lax.bitwise_xor(jnp.int32(i >> 1), lax.shift_right_logical(turn, 1)))


def attention_forward(turn_ref, slope_ref, near, far, start_ref, o_near, o_far, lse_ref, q_s, k_s, v_s, o_s):
    turn = turn_ref[0]
    slope = slope_ref[pl.program_id(1)]
    sequence = q_s.shape[0]
    piece = sequence // 4
    scale = 1.0 / math.sqrt(HEAD)

    def load(i, core, x):
        block = (near, far)[core][0, x]
        for j, scratch in enumerate((q_s, k_s, v_s)):
            scratch[i * piece : (i + 1) * piece, :] = block[:, j * HEAD : (j + 1) * HEAD]

    in_order(turn, load)
    for first in range(0, sequence, QB):
        low, width = window(first)
        scores = masked_scores(
            q_s[first : first + QB, :],
            k_s[low : low + width, :],
            start_ref[0, first : first + QB, :],
            slope,
            first,
            low,
            width,
            scale,
        )
        peak = jnp.max(scores, axis=-1, keepdims=True)
        weights = jnp.exp(scores - peak)
        total = jnp.sum(weights, axis=-1, keepdims=True)
        lse_ref[0, 0, first : first + QB, :] = peak + jnp.log(total)
        probs = (weights * (1.0 / total)).astype(BF)
        o_s[first : first + QB, :] = dot(probs, v_s[low : low + width, :], 1, 0).astype(BF)

    def store(i, core, x):
        (o_near, o_far)[core][0, x] = o_s[i * piece : (i + 1) * piece, :]

    in_order(turn, store)


def attention_backward(
    turn_ref,
    slope_ref,
    near,
    far,
    do_near,
    do_far,
    start_ref,
    lse_ref,
    out_near,
    out_far,
    q_s,
    k_s,
    v_s,
    do_s,
    dq_s,
    dk_s,
    dv_s,
):
    turn = turn_ref[0]
    slope = slope_ref[pl.program_id(1)]
    sequence = q_s.shape[0]
    piece = sequence // 4
    scale = 1.0 / math.sqrt(HEAD)

    def load(i, core, x):
        rows = slice(i * piece, (i + 1) * piece)
        block = (near, far)[core][0, x]
        for j, scratch in enumerate((q_s, k_s, v_s)):
            scratch[rows, :] = block[:, j * HEAD : (j + 1) * HEAD]
        do_s[rows, :] = (do_near, do_far)[core][0, x]

    in_order(turn, load)
    dk_s[...] = jnp.zeros_like(dk_s)
    dv_s[...] = jnp.zeros_like(dv_s)
    for first in range(0, sequence, QB):
        low, width = window(first)
        keys = k_s[low : low + width, :]
        query = q_s[first : first + QB, :]
        grad = do_s[first : first + QB, :]
        scores = masked_scores(
            query, keys, start_ref[0, first : first + QB, :], slope, first, low, width, scale
        )
        probs = jnp.exp(scores - lse_ref[0, 0, first : first + QB, :])
        grad_probs = dot(grad, v_s[low : low + width, :], 1, 1)
        delta = jnp.sum(probs * grad_probs, axis=-1, keepdims=True)
        grad_scores = (probs * (grad_probs - delta) * scale).astype(BF)
        dq_s[first : first + QB, :] = dot(grad_scores, keys, 1, 0).astype(BF)
        dk_s[low : low + width, :] += dot(grad_scores, query, 0, 0)
        dv_s[low : low + width, :] += dot(probs.astype(BF), grad, 0, 0)

    def store(i, core, x):
        rows = slice(i * piece, (i + 1) * piece)
        out = (out_near, out_far)[core]
        out[0, x, :, 0:HEAD] = dq_s[rows, :]
        out[0, x, :, HEAD : 2 * HEAD] = dk_s[rows, :].astype(BF)
        out[0, x, :, 2 * HEAD : 3 * HEAD] = dv_s[rows, :].astype(BF)

    in_order(turn, store)


def on_device(
    hidden_in,
    segment_ids,
    qkv_weight,
    out_weight,
    up_weight,
    down_weight,
    norm1_gain,
    norm2_gain,
    out_cotangent,
):
    n = lax.axis_size("fsdp")
    tp = lax.axis_size("tp")
    ring = n // 4
    f = lax.axis_index("fsdp")
    t = lax.axis_index("tp")
    y, zl, zh = f & 1, (f >> 1) & 1, f >> 2
    low_half = zl == 0
    piece = hidden_in.shape[0]
    half = piece // 2
    sequence = piece * tp
    heads = H // tp // 2
    width = heads * HEAD
    unit = D // n
    pairs = [(k, j) for k in range(ring) for j in range(2)]
    far_first = range(ring - 1, -1, -1)
    steps = Steps()
    move, run, close = steps.move, steps.run, steps.close

    def over(axis, to, size):
        return lambda v: lax.ppermute(v, axis, [(i, to(i)) for i in range(size)])

    pp_core = over("tp", lambda i: i ^ 1, tp)
    pp_x = over("tp", lambda i: i ^ 2, tp)
    pp_zl = over("fsdp", lambda i: i ^ 2, n)
    pp_y = over("fsdp", lambda i: i ^ 1, n)
    pp_up = over("fsdp", lambda i: (i + 4) % n, n)
    pp_down = over("fsdp", lambda i: (i - 4) % n, n)

    def to_rel(v):
        cols = [v[..., b * unit : (b + 1) * unit] for b in range(n)]

        def pick(k, j, l):
            chosen = None
            for a in range(ring):
                both = jnp.where(y == j, cols[a * 4 + l * 2], cols[a * 4 + l * 2 + 1])
                chosen = both if chosen is None else jnp.where((zh - k) % ring == a, both, chosen)
            return chosen

        return jnp.concatenate([pick(k, j, l) for k, j in pairs for l in range(2)], axis=-1)

    def from_rel(v):
        cols = [v[..., b * unit : (b + 1) * unit] for b in range(n)]

        def pick(a, l, b):
            chosen = None
            for k in range(ring):
                both = jnp.where(y == b, cols[k * 4 + l], cols[k * 4 + 2 + l])
                chosen = both if chosen is None else jnp.where((zh - k) % ring == a, both, chosen)
            return chosen

        return jnp.concatenate(
            [pick(a, l, b) for a in range(ring) for l in range(2) for b in range(2)], axis=-1
        )

    def mine_of(first, second):
        return jnp.where(low_half, first, second)

    def joined(mine, other, axis):
        return jnp.concatenate(
            [jnp.where(low_half, mine, other), jnp.where(low_half, other, mine)], axis=axis
        )

    def plus(a, b):
        return (a.astype(F32) + b.astype(F32)).astype(BF)

    def ring_up(v):
        chain = [v]
        for _ in range(ring - 1):
            chain.append(pp_up(chain[-1]))
        return chain[1:]

    class Weight:
        def __init__(self):
            self.have = {}

        def zh(self, source, chunk):
            for k, v in enumerate(move(ring_up, self.have[0, 0, source, chunk])):
                self.have[k + 1, 0, source, chunk] = v

        def y(self, source, chunk):
            self.have[0, 1, source, chunk] = move(pp_y, self.have[0, 0, source, chunk])

        def yz(self, source, chunk):
            for k in range(1, ring):
                self.have[k, 1, source, chunk] = move(pp_y, self.have[k, 0, source, chunk])

        def blocks(self, axis):
            found, starts = [], []
            for k, j in pairs:
                for source in range(2):
                    side = zl if source == 0 else 1 - zl
                    base = (2 * (2 * k + j) + side) * unit
                    at = 0
                    for chunk in sorted(c for a, b, s, c in self.have if (a, b, s) == (k, j, source)):
                        v = self.have[k, j, source, chunk]
                        found.append(v)
                        starts.append((base + at) // 128)
                        at += v.shape[axis]
            return found, jnp.stack(starts).astype(jnp.int32)

    gains = jnp.stack([norm1_gain, norm2_gain])
    gain_chain = [joined(gains, pp_zl(gains), 1)]
    gain_chain = jnp.concatenate(gain_chain + ring_up(gain_chain[0]), axis=0)
    gain_other = pp_y(gain_chain)
    gains = jnp.concatenate(
        [(gain_chain, gain_other)[j][2 * k : 2 * k + 2] for k, j in pairs], axis=1
    ).astype(F32)
    gain_one, gain_two = gains[0:1], gains[1:2]
    documents = jnp.concatenate([segment_ids, pp_zl(segment_ids)], axis=0)
    x = to_rel(hidden_in).astype(F32)
    normed_one, inverse_one = norm_forward(x)
    a_one = (normed_one * gain_one).astype(BF)

    qkv_heads = (
        qkv_weight.reshape(unit, 3, 2 * heads, HEAD)
        .transpose(0, 2, 1, 3)
        .reshape(unit, 2 * heads * 3 * HEAD)
    )
    lower, upper = jnp.split(qkv_heads, 2, axis=1)
    mine, other = mine_of(lower, upper), mine_of(upper, lower)
    steps.pending += [a_one, mine, other]
    close()

    def split_rows(v):
        return v[:half], v[half:]

    qkv_w = Weight()
    have = qkv_w.have
    have[0, 0, 0, 0] = mine
    swapped = move(pp_zl, other)
    qkv_w.y(0, 0)
    qkv_w.zh(0, 0)
    ax = move(pp_x, a_one)
    close()
    a_top, a_bottom = split_rows(a_one)
    have[0, 0, 1, 0] = swapped
    swapped_parts = swapped[: unit // 2], swapped[unit // 2 :]

    def qkv_zh(c):
        for k, v in enumerate(move(ring_up, swapped_parts[c])):
            have[k + 1, 0, 1, c] = v

    qkv_zh(0)
    qkv_w.y(1, 0)
    az_top = move(pp_zl, a_top)
    close()
    qkv_zh(1)
    qkv_w.yz(0, 0)
    az_bottom = move(pp_zl, a_bottom)
    ad_top = move(pp_x, az_top)
    close()
    qkv_w.yz(1, 0)
    qkv_w.yz(1, 1)
    ad_bottom = move(pp_x, az_bottom)
    first, second = jnp.split(out_weight, 2, axis=0)
    swap_out = move(pp_zl, mine_of(second, first))
    near_one = stack_rows(a_one, ax, az_top, az_bottom, ad_top, ad_bottom)
    steps.pending.append(near_one)
    close()

    mine_out = joined(mine_of(first, second), swap_out, 1)
    out_w, up_w, down_w = Weight(), Weight(), Weight()
    chunk = unit // 2

    def up_part(side, c):
        rows = up_weight[c * chunk : (c + 1) * chunk]
        lower, upper = jnp.split(rows, 2, axis=1)
        return mine_of(lower, upper) if side == 0 else mine_of(upper, lower)

    def down_part(side, c):
        cols = down_weight[:, c * chunk : (c + 1) * chunk]
        lower, upper = jnp.split(cols, 2, axis=0)
        return mine_of(lower, upper) if side == 0 else mine_of(upper, lower)

    for c in range(2):
        up_w.have[0, 0, 0, c] = up_part(0, c)
        down_w.have[0, 0, 0, c] = down_part(0, c)
    out_w.have[0, 0, 0, 0] = mine_out

    def swap_up(c):
        up_w.have[0, 0, 1, c] = move(pp_zl, up_part(1, c))

    def swap_down(c):
        down_w.have[0, 0, 1, c] = move(pp_zl, down_part(1, c))

    cot = to_rel(out_cotangent)
    cot_top, cot_bottom = split_rows(cot)
    turn = jnp.full((1,), t, jnp.int32)
    head_index = t * 2 * heads + zl * heads + jnp.arange(heads)
    slopes = 2.0 ** (-8.0 * (head_index + 1).astype(F32) / H)
    starts = jnp.sum(
        (documents[:, None, :] < documents[:, :, None]).astype(jnp.int32), axis=-1
    )[:, :, None]

    w_qkv, at_qkv = qkv_w.blocks(0)
    far_one = move(pp_core, near_one)
    out_w.zh(0, 0)
    out_w.y(0, 0)
    swap_up(0)
    qkv = [run(deep, near_one, w_qkv, at_qkv, 0), deep(far_one, w_qkv, at_qkv, 0)]
    qkv = [v.reshape(2, 2, piece, 3 * width) for v in qkv]
    steps.pending += qkv
    close()

    def spec(cols):
        return pl.BlockSpec((1, 2, piece, cols), lambda s, h, *_: (s, 0, 0, h))

    start_spec = pl.BlockSpec((1, sequence, 1), lambda s, h, *_: (s, 0, 0))
    lse_spec = pl.BlockSpec((1, 1, sequence, 1), lambda s, h, *_: (s, h, 0, 0))
    block = pltpu.VMEM((sequence, HEAD), BF)
    wide = pltpu.VMEM((sequence, HEAD), F32)
    halves_shape = jax.ShapeDtypeStruct((2, 2, piece, width), BF)

    def attend(near, far):
        return pl.pallas_call(
            attention_forward,
            out_shape=(halves_shape, halves_shape, jax.ShapeDtypeStruct((2, heads, sequence, 1), F32)),
            grid_spec=pltpu.PrefetchScalarGridSpec(
                num_scalar_prefetch=2,
                grid=(2, heads),
                in_specs=[spec(3 * HEAD), spec(3 * HEAD), start_spec],
                out_specs=[spec(HEAD), spec(HEAD), lse_spec],
                scratch_shapes=[block] * 4,
            ),
            compiler_params=params(2),
            cost_estimate=cost(sequence, sequence, 2 * heads * HEAD * 4),
            name="attention_forward",
        )(turn, slopes, near, far, starts)

    out_w.yz(0, 0)
    up_w.zh(0, 0)
    up_w.y(0, 0)
    swap_up(1)
    cx_top = move(pp_x, cot_top)
    att_near, att_far, lse = run(attend, *qkv)
    att_near, att_far = (v.reshape(4 * piece, width) for v in (att_near, att_far))
    close()

    w_out = [out_w.have[k, j, 0, 0] for k, j in pairs]
    at_out = jnp.arange(len(pairs), dtype=jnp.int32) * (2 * unit // 128)
    far = run(broad, att_far, w_out, at_out, 0)
    got = move(pp_core, far)
    up_w.yz(0, 0)
    cx_bottom = move(pp_x, cot_bottom)
    cz_top = move(pp_zl, cot_top)
    e = run(broad, att_near, w_out, at_out, 0, got)
    close()

    def quarters(v):
        return [v[i * piece : (i + 1) * piece] for i in range(4)]

    e00, ex, ez, ed = quarters(e)
    from_d = move(pp_x, ed)
    up_w.zh(0, 1)
    up_w.y(0, 1)
    swap_down(0)
    close()
    from_x = move(pp_x, ex)
    from_z = move(pp_zl, plus(ez, from_d))
    up_w.zh(1, 0)
    up_w.yz(0, 1)
    up_w.y(1, 0)
    close()
    resid = x + (e00.astype(F32) + from_x.astype(F32) + from_z.astype(F32))
    normed_two, inverse_two = norm_forward(resid)
    a_two = (normed_two * gain_two).astype(BF)
    steps.pending.append(a_two)
    close()

    ax = move(pp_x, a_two)
    az = move(pp_zl, a_two)
    up_w.zh(1, 1)
    up_w.yz(1, 0)
    up_w.y(1, 1)
    close()
    ad = move(pp_x, az)
    up_w.yz(1, 1)
    down_w.zh(0, 0)
    down_w.y(0, 0)
    swap_down(1)
    close()
    near_two = stack_rows(a_two, ax, az, ad)

    w_up, at_up = up_w.blocks(0)

    def lift(rows):
        return deep(
            rows, w_up, at_up, 0, finish=gelu_and_slope, outs=2, tm=1280, parts=5
        )

    far_two = move(pp_core, near_two)
    down_w.zh(0, 1)
    down_w.yz(0, 0)
    down_w.y(0, 1)
    cz_bottom = move(pp_zl, cot_bottom)
    act_near, slope_near = run(lift, near_two)
    close()
    down_w.zh(1, 0)
    down_w.yz(0, 1)
    down_w.y(1, 0)
    cd_top = move(pp_x, cz_top)
    cd_bottom = move(pp_x, cz_bottom)
    act_far, slope_far = run(lift, far_two)
    near_cot = stack_rows(cot, cx_top, cx_bottom, cz_top, cz_bottom, cd_top, cd_bottom)
    steps.pending.append(near_cot)
    close()

    def cuts(j):
        return [((2 * k + j) * 2 + l, unit) for k in far_first for l in range(2)]

    def keys(j):
        return [(k, j, l) for k in far_first for l in range(2)]

    class Sum:
        def __init__(self, axis):
            self.parts = {}
            self.sums = {}
            self.value = {}
            self.axis = axis

        def make(self, j, a_pair, b_pair, first):
            side = self.axis

            def go(v, *_):
                pair = (v, a_pair[1])
                return gram(pair, b_pair, cuts(j), side)

            for key, v in zip(keys(j), run(go, a_pair[0])):
                self.parts[key] = v

        def y_far(self, l):
            for k in range(ring - 1, 0, -1):
                self.sums[k, l] = plus(self.parts[k, 0, l], move(pp_y, self.parts[k, 1, l]))

        def y_own(self, l):
            self.sums[0, l] = plus(self.parts[0, 0, l], move(pp_y, self.parts[0, 1, l]))

        def cut(self, v, r, of):
            size = v.shape[1 - self.axis] // of
            return lax.slice_in_dim(v, r * size, (r + 1) * size, axis=1 - self.axis)

        def zh(self, l, r=0, of=2):
            value = self.cut(self.sums[ring - 1, l], r, of)
            for k in range(ring - 2, 0, -1):
                value = plus(move(pp_down, value), self.cut(self.sums[k, l], r, of))
            self.value[l, r] = move(pp_down, value)

        def zl(self, r=0, of=2):
            first, second = (
                plus(self.value[l, r], self.cut(self.sums[0, l], r, of)) for l in range(2)
            )
            self.value[2, r] = mine_of(first, second)
            self.value[3, r] = move(pp_zl, mine_of(second, first))

        def result(self, of=2):
            mine = [self.value[2, r] for r in range(of)]
            other = [self.value[3, r] for r in range(of)]
            if of == 1:
                return mine[0], other[0]
            return tuple(jnp.concatenate(v, axis=1 - self.axis) for v in (mine, other))

    down_g, up_g, out_g, qkv_g = Sum(1), Sum(0), Sum(1), Sum(0)
    acts = (act_near, act_far)
    far_cot = move(pp_core, near_cot)
    down_w.zh(1, 1)
    down_w.yz(1, 0)
    down_w.y(1, 1)
    down_g.make(1, acts, (near_cot, far_cot), None)
    close()
    down_w.yz(1, 1)
    down_g.make(0, acts, (near_cot, far_cot), None)
    close()

    w_down, at_down = down_w.blocks(1)

    def pull(rows, slope):
        return deep(
            rows, w_down, at_down, 1, finish=lambda total, s: (total * s.astype(F32),), extra=(slope,), tm=640, parts=2
        )

    down_g.y_far(0)
    du_far = run(pull, far_cot, slope_far)
    far = broad(du_far, w_up, at_up, 1)
    steps.pending.append(far)
    close()
    got = move(pp_core, far)
    down_g.y_far(1)
    down_g.zh(0, 0)
    du_near = run(pull, near_cot, slope_near)
    e = broad(du_near, w_up, at_up, 1, got)
    steps.pending.append(e)
    close()

    e00, ex, ez, ed = quarters(e)
    from_d = move(pp_x, ed)
    down_g.y_own(0)
    down_g.zh(0, 1)
    dus = (du_near, du_far)
    up_g.make(1, (near_two, far_two), dus, None)
    up_g.make(0, (near_two, far_two), dus, None)
    close()
    from_x = move(pp_x, ex)
    from_z = move(pp_zl, plus(ez, from_d))
    down_g.y_own(1)
    down_g.zh(1, 0)
    far = run(broad, act_far, w_down, at_down, 0)
    close()
    grad_in_two = e00.astype(F32) + from_x.astype(F32) + from_z.astype(F32)
    grad_part, grad_gain_two = norm_backward(grad_in_two, normed_two, inverse_two, gain_two)
    grad_resid = cot.astype(F32) + grad_part
    grad_rows = grad_resid.astype(BF)
    steps.pending.append(grad_rows)
    close()

    ax = move(pp_x, grad_rows)
    az = move(pp_zl, grad_rows)
    got = move(pp_core, far)
    up_g.y_far(0)
    down_g.zh(1, 1)
    e_out = run(broad, act_near, w_down, at_down, 0, got)
    close()
    ad = move(pp_x, az)
    up_g.y_far(1)
    up_g.zh(0, 0)
    down_g.zl(0)
    close()
    near_grad = stack_rows(grad_rows, ax, az, ad)

    proj_shape = jax.ShapeDtypeStruct((2, 2, piece, 3 * width), BF)

    def attend_back(near, far):
        return pl.pallas_call(
            attention_backward,
            out_shape=(proj_shape, proj_shape),
            grid_spec=pltpu.PrefetchScalarGridSpec(
                num_scalar_prefetch=2,
                grid=(2, heads),
                in_specs=[spec(3 * HEAD), spec(3 * HEAD), spec(HEAD), spec(HEAD), start_spec, lse_spec],
                out_specs=[spec(3 * HEAD), spec(3 * HEAD)],
                scratch_shapes=[block] * 5 + [wide] * 2,
            ),
            compiler_params=params(2),
            cost_estimate=cost(sequence, sequence, 2 * heads * HEAD * 8),
            name="attention_backward",
        )(turn, slopes, *qkv, near, far, starts, lse)

    o00, ox, oz, od = quarters(e_out)
    far_grad = move(pp_core, near_grad)
    from_od = move(pp_x, od)
    up_g.y_own(0)
    up_g.zh(0, 1)
    down_g.zl(1)
    grad_att = [
        v.reshape(2, 2, piece, width)
        for v in (run(deep, near_grad, w_out, at_out, 1), deep(far_grad, w_out, at_out, 1))
    ]
    proj = attend_back(*grad_att)
    proj = tuple(v.reshape(4 * piece, 3 * width) for v in proj)
    steps.pending += proj
    close()

    rows_one = (near_one, far_one)
    up_g.y_own(1)
    up_g.zh(1, 0)
    qkv_g.make(1, rows_one, proj, None)
    qkv_g.make(0, rows_one, proj, None)
    close()

    qkv_g.y_far(0)
    up_g.zh(1, 1)
    from_ox = move(pp_x, ox)
    from_oz = move(pp_zl, plus(oz, from_od))
    far = run(broad, proj[1], w_qkv, at_qkv, 1)
    got = move(pp_core, far)
    e = run(broad, proj[0], w_qkv, at_qkv, 1, got)
    close()
    block_out = from_rel(
        (resid + (o00.astype(F32) + from_ox.astype(F32) + from_oz.astype(F32))).astype(BF)
    )

    e00, ex, ez, ed = quarters(e)
    from_d = move(pp_x, ed)
    qkv_g.y_far(1)
    qkv_g.zh(0, 0, 1)
    up_g.zl(0)
    atts = (att_near, att_far)
    out_g.make(1, atts, (near_grad, far_grad), None)
    out_g.make(0, atts, (near_grad, far_grad), None)
    close()
    from_x = move(pp_x, ex)
    from_z = move(pp_zl, plus(ez, from_d))
    qkv_g.zh(1, 0, 1)
    qkv_g.y_own(0)
    qkv_g.y_own(1)
    close()
    grad_in_one = e00.astype(F32) + from_x.astype(F32) + from_z.astype(F32)
    grad_part, grad_gain_one = norm_backward(grad_in_one, normed_one, inverse_one, gain_one)
    grad_in = from_rel(grad_resid + grad_part)

    out_g.y_far(0)
    out_g.y_far(1)
    up_g.zl(1)
    qkv_g.zl(0, 1)
    close()
    out_g.zh(0, 0, 1)
    out_g.zh(1, 0, 1)
    out_g.y_own(0)
    out_g.y_own(1)
    close()
    out_g.zl(0, 1)

    grad_down = joined(*down_g.result(), 0).astype(F32)
    grad_up = joined(*up_g.result(), 1).astype(F32)
    grad_out = joined(*out_g.result(1), 0).astype(F32)

    def parts_first(v):
        return v.reshape(unit, heads, 3, HEAD).transpose(0, 2, 1, 3).reshape(unit, 3, width)

    mine, other = qkv_g.result(1)
    grad_qkv = joined(parts_first(mine), parts_first(other), 2).astype(F32)

    def total(v):
        v = from_rel(v)
        for step in (pp_core, pp_x, pp_zl, pp_y):
            v = v + step(v)
        moving = v
        for _ in range(ring - 1):
            moving = pp_up(moving)
            v = v + moving
        size = D // (n * tp)
        return lax.dynamic_slice_in_dim(v, (f * tp + t) * size, size)

    return (
        block_out,
        grad_in,
        total(grad_gain_one),
        total(grad_gain_two),
        grad_qkv,
        grad_out,
        grad_up,
        grad_down,
    )


def solution(mesh):
    return jax.shard_map(
        on_device,
        mesh=mesh,
        in_specs=(
            P(("fsdp", "tp"), None),
            P("fsdp", None),
            P("fsdp", None, "tp"),
            P("tp", "fsdp"),
            P("fsdp", "tp"),
            P("tp", "fsdp"),
            P("fsdp"),
            P("fsdp"),
            P(("fsdp", "tp"), None),
        ),
        out_specs=(
            P(("fsdp", "tp"), None),
            P(("fsdp", "tp"), None),
            P(("fsdp", "tp")),
            P(("fsdp", "tp")),
            P("fsdp", None, "tp"),
            P("tp", "fsdp"),
            P("fsdp", "tp"),
            P("tp", "fsdp"),
        ),
        check_vma=False,
    )
```

```python
import functools
import math

import jax
import jax.numpy as jnp
from jax import lax
from jax.experimental import pallas as pl
from jax.experimental.pallas import tpu as pltpu
from jax.sharding import PartitionSpec as P

D = 4096
H = 32
HEAD = D // H
REACH = 640
NORM_EPSILON = 1e-05
SQRT_HALF = 0.7071067811865476
INV_ROOT_TWO_PI = 0.3989422804014327
BF = jnp.bfloat16
F32 = jnp.float32
COVER = 0.05
VMEM = 56 << 20


def norm_forward(values_in):
    row_mean = jnp.mean(values_in, axis=-1, keepdims=True)
    centred = values_in - row_mean
    row_variance = jnp.mean(centred * centred, axis=-1, keepdims=True)
    inverse = lax.rsqrt(row_variance + NORM_EPSILON)
    return centred * inverse, inverse


def norm_backward(grad_out, normed, inverse, gain):
    grad_gain = jnp.sum(grad_out * normed, axis=0)
    scaled = grad_out * gain
    mean_one = jnp.mean(scaled, axis=-1, keepdims=True)
    mean_two = jnp.mean(scaled * normed, axis=-1, keepdims=True)
    return inverse * (scaled - mean_one - normed * mean_two), grad_gain


def gelu_and_slope(pre_act):
    part = 0.5 * (1.0 + lax.erf(pre_act * SQRT_HALF))
    slope = part + pre_act * jnp.exp(-0.5 * pre_act * pre_act) * INV_ROOT_TWO_PI
    return pre_act * part, slope


def dot(left, right, cl, cr):
    return lax.dot_general(left, right, (((cl,), (cr,)), ((), ())), preferred_element_type=F32)


class Steps:
    def __init__(self):
        self.token = jnp.zeros((1,), F32)
        self.pending = []
        self.first = True

    def begin(self, value):
        if self.first:
            return value
        return lax.optimization_barrier((value, self.token))[0]

    def move(self, how, value):
        out = how(self.begin(value))
        self.pending.append(out)
        return out

    def run(self, how, value, *more, **named):
        out = how(self.begin(value), *more, **named)
        self.pending += jax.tree.leaves(out)
        return out

    def close(self):
        self.token = lax.optimization_barrier((self.token, *self.pending))[0]
        self.pending = []
        self.first = False


def params(grid_dims):
    return pltpu.CompilerParams(
        dimension_semantics=("arbitrary",) * grid_dims, vmem_limit_bytes=VMEM
    )


def cost(m, n, k):
    return pl.CostEstimate(
        flops=int(2 * m * n * k * COVER), transcendentals=0, bytes_accessed=2 * (m * k + k * n + m * n)
    )


def tile(size, most):
    if size <= most:
        return size
    while size % most:
        most -= 128
    return most


def stack_rows(*pieces):
    rows = math.gcd(*(v.shape[0] for v in pieces))
    cols = pieces[0].shape[1]
    sizes = [v.shape[0] // rows for v in pieces]
    firsts = [sum(sizes[:i]) for i in range(len(pieces))]

    def body(*refs):
        step = pl.program_id(0)
        for ref, first, size in zip(refs, firsts, sizes):

            @pl.when((step >= first) & (step < first + size))
            def _(ref=ref):
                refs[-1][...] = ref[...]

    def spec(first, size):
        return pl.BlockSpec((rows, cols), lambda g: (jnp.clip(g - first, 0, size - 1), 0))

    return pl.pallas_call(
        body,
        out_shape=jax.ShapeDtypeStruct((sum(sizes) * rows, cols), pieces[0].dtype),
        grid=(sum(sizes),),
        in_specs=[spec(f, s) for f, s in zip(firsts, sizes)],
        out_specs=pl.BlockSpec((rows, cols), lambda g: (g, 0)),
        compiler_params=params(1),
        name="stack_rows",
    )(*pieces)


def gram(a_sides, b_sides, blocks, side):
    width = blocks[0][1]
    m = width if side == 0 else a_sides[0][0][0].shape[1]
    n = width if side == 1 else b_sides[0][0][0].shape[1]
    tm, tn = tile(m, 1024), tile(n, 1024)
    grid_m, grid_n = m // tm, n // tn
    count = len(blocks)
    per = grid_m * grid_n

    def at(g):
        p, r = g // per, g % per
        return p, r // grid_m, r % grid_m

    def a_spec(row, rows):
        def index_map(g, index):
            p, _, i = at(g)
            return row, (index[p] * grid_m + i if side == 0 else i)

        return pl.BlockSpec((rows, tm), index_map)

    def b_spec(row, rows):
        def index_map(g, index):
            p, j, _ = at(g)
            return row, (index[p] * grid_n + j if side == 1 else j)

        return pl.BlockSpec((rows, tn), index_map)

    def out_map(q):
        def at_q(g, index):
            r = jnp.clip(g - q * per, 0, per - 1)
            return r % grid_m, r // grid_m

        return at_q

    def body(index_ref, *refs):
        refs = list(refs)

        def take(batch):
            parts = [refs.pop(0)[...] for _ in batch]
            return parts[0] if len(parts) == 1 else jnp.concatenate(parts, axis=0)

        lefts = [take(batch) for batch in a_sides]
        rights = [take(batch) for batch in b_sides]
        total = None
        for left, right in zip(lefts, rights):
            part = dot(left, right, 0, 0)
            total = part if total is None else total + part
        total = total.astype(BF)
        p = pl.program_id(0) // per
        for q in range(count):

            @pl.when(p == q)
            def _(q=q):
                refs[q][...] = total

    flat_a = [piece for batch in a_sides for piece in batch]
    flat_b = [piece for batch in b_sides for piece in batch]
    depth = sum(piece[2] for piece in flat_a)
    return pl.pallas_call(
        body,
        out_shape=[jax.ShapeDtypeStruct((m, n), BF)] * count,
        grid_spec=pltpu.PrefetchScalarGridSpec(
            num_scalar_prefetch=1,
            grid=(count * per,),
            in_specs=[a_spec(row, rows) for _, row, rows in flat_a]
            + [b_spec(row, rows) for _, row, rows in flat_b],
            out_specs=[pl.BlockSpec((tm, tn), out_map(q)) for q in range(count)],
        ),
        compiler_params=params(1),
        cost_estimate=cost(m, n * count, depth),
        name="gram",
    )(
        jnp.array([b[0] for b in blocks], jnp.int32),
        *(piece[0] for piece in flat_a),
        *(piece[0] for piece in flat_b),
    )


def deep(pieces, blocks, starts, cr, finish=None, extra=(), outs=1, tn=512, cuts=1):
    sizes = [rows for _, _, rows in pieces]
    m, k = sum(sizes), pieces[0][0].shape[1]
    n = blocks[0].shape[1 - cr]
    count, heights = len(blocks), len(pieces)
    tn = tile(n, tn)
    work = []
    for i, rows in enumerate(sizes):
        for c in range(cuts):
            height = rows // cuts
            work.append((i, c * height, sum(sizes[:i]) + c * height, height))

    def body(starts_ref, *refs):
        a_refs, rest = refs[:heights], refs[heights:]

        def part(i, first, height):
            total = None
            for p in range(count):
                size = blocks[p].shape[cr]
                at = pl.multiple_of(starts_ref[p] * 128, 128)
                term = dot(a_refs[i][first : first + height, pl.ds(at, size)], rest[p][...], 1, cr)
                total = term if total is None else total + term
            return total

        def store(first, height, total):
            at = slice(first, first + height)
            values = (total,) if finish is None else finish(total, *(v[at, :] for v in rest[count:-outs]))
            for ref, value in zip(rest[-outs:], values):
                ref[at, :] = value.astype(BF)

        before = None
        for i, first, row, height in work:
            total = part(i, first, height)
            if before is not None:
                store(*before)
            before = (row, height, total)
        store(*before)

    def a_spec(row, rows):
        return pl.BlockSpec((rows, k), lambda j, *_: (row, 0), pipeline_mode=pl.Buffered(1))

    def w_spec(w):
        size = w.shape[cr]
        if cr == 0:
            return pl.BlockSpec((size, tn), lambda j, *_: (0, j))
        return pl.BlockSpec((tn, size), lambda j, *_: (j, 0))

    out = pl.BlockSpec((m, tn), lambda j, *_: (0, j))
    result = pl.pallas_call(
        body,
        out_shape=[jax.ShapeDtypeStruct((m, n), BF)] * outs,
        grid_spec=pltpu.PrefetchScalarGridSpec(
            num_scalar_prefetch=1,
            grid=(n // tn,),
            in_specs=[a_spec(row, rows) for _, row, rows in pieces]
            + [w_spec(w) for w in blocks]
            + [out] * len(extra),
            out_specs=[out] * outs,
        ),
        compiler_params=params(1),
        cost_estimate=cost(m, n, k),
        name="deep",
    )(starts, *(piece[0] for piece in pieces), *blocks, *extra)
    return result[0] if outs == 1 else result


def broad(a, blocks, starts, cr):
    m, k = a.shape
    n = sum(w.shape[1 - cr] for w in blocks)
    count = len(blocks)
    tm = tile(m // 2, 320)
    steps = m // 2 // tm

    def body(starts_ref, a_ref, *rest):
        for which in range(2):

            @pl.when(pl.program_id(0) // steps == which)
            def _(out=rest[count + which]):
                for p in range(count):
                    size = blocks[p].shape[1 - cr]
                    at = pl.multiple_of(starts_ref[p] * 128, 128)
                    out[:, pl.ds(at, size)] = dot(a_ref[...], rest[p][...], 1, cr).astype(BF)

    return pl.pallas_call(
        body,
        out_shape=[jax.ShapeDtypeStruct((m // 2, n), BF)] * 2,
        grid_spec=pltpu.PrefetchScalarGridSpec(
            num_scalar_prefetch=1,
            grid=(2 * steps,),
            in_specs=[pl.BlockSpec((tm, k), lambda i, *_: (i, 0))]
            + [pl.BlockSpec(w.shape, lambda i, *_: (0, 0), pipeline_mode=pl.Buffered(1)) for w in blocks],
            out_specs=[
                pl.BlockSpec((tm, n), lambda i, *_: (jnp.minimum(i, steps - 1), 0)),
                pl.BlockSpec((tm, n), lambda i, *_: (jnp.maximum(i - steps, 0), 0)),
            ],
        ),
        compiler_params=params(1),
        cost_estimate=cost(m, n, k),
        name="broad",
    )(starts, a, *blocks)


QB = 256


def window(first):
    low = max(0, first - REACH)
    return low, first + QB - low


def masked_scores(q, k, start, slope, first, low, width, scale):
    scores = dot(q, k, 1, 1)
    row = first + lax.broadcasted_iota(jnp.int32, (QB, width), 0)
    col = low + lax.broadcasted_iota(jnp.int32, (QB, width), 1)
    scores = scores * scale - slope * (row - col).astype(F32)
    return jnp.where((col >= start) & (col <= row), scores, -1e30)


def in_order(turn, visit):
    for i in range(4):
        rel = lax.bitwise_xor(jnp.int32(i), turn)
        visit(i, lax.bitwise_and(rel, 1), lax.shift_right_logical(rel, 1))


def attention_forward(turn_ref, slope_ref, qkv_ref, start_ref, o_ref, lse_ref, q_s, k_s, v_s, o_s):
    turn = turn_ref[0]
    slope = slope_ref[pl.program_id(0)]
    sequence = q_s.shape[0]
    piece = sequence // 4
    scale = 1.0 / math.sqrt(HEAD)

    def load(i, core, x):
        block = qkv_ref[core, x]
        for j, scratch in enumerate((q_s, k_s, v_s)):
            scratch[i * piece : (i + 1) * piece, :] = block[:, j * HEAD : (j + 1) * HEAD]

    in_order(turn, load)
    for first in range(0, sequence, QB):
        low, width = window(first)
        scores = masked_scores(
            q_s[first : first + QB, :],
            k_s[low : low + width, :],
            start_ref[first : first + QB, :],
            slope,
            first,
            low,
            width,
            scale,
        )
        peak = jnp.max(scores, axis=-1, keepdims=True)
        weights = jnp.exp(scores - peak)
        total = jnp.sum(weights, axis=-1, keepdims=True)
        lse_ref[0, first : first + QB, :] = peak + jnp.log(total)
        probs = (weights * (1.0 / total)).astype(BF)
        o_s[first : first + QB, :] = dot(probs, v_s[low : low + width, :], 1, 0).astype(BF)

    def store(i, core, x):
        o_ref[core, x] = o_s[i * piece : (i + 1) * piece, :]

    in_order(turn, store)


def attention_backward(
    turn_ref, slope_ref, qkv_ref, do_ref, start_ref, lse_ref, out_ref, q_s, k_s, v_s, do_s, dq_s, dk_s, dv_s
):
    turn = turn_ref[0]
    slope = slope_ref[pl.program_id(0)]
    sequence = q_s.shape[0]
    piece = sequence // 4
    scale = 1.0 / math.sqrt(HEAD)

    def load(i, core, x):
        rows = slice(i * piece, (i + 1) * piece)
        block = qkv_ref[core, x]
        for j, scratch in enumerate((q_s, k_s, v_s)):
            scratch[rows, :] = block[:, j * HEAD : (j + 1) * HEAD]
        do_s[rows, :] = do_ref[core, x]

    in_order(turn, load)
    dk_s[...] = jnp.zeros_like(dk_s)
    dv_s[...] = jnp.zeros_like(dv_s)
    for first in range(0, sequence, QB):
        low, width = window(first)
        keys = k_s[low : low + width, :]
        query = q_s[first : first + QB, :]
        grad = do_s[first : first + QB, :]
        scores = masked_scores(
            query, keys, start_ref[first : first + QB, :], slope, first, low, width, scale
        )
        probs = jnp.exp(scores - lse_ref[0, first : first + QB, :])
        grad_probs = dot(grad, v_s[low : low + width, :], 1, 1)
        delta = jnp.sum(probs * grad_probs, axis=-1, keepdims=True)
        grad_scores = (probs * (grad_probs - delta) * scale).astype(BF)
        dq_s[first : first + QB, :] = dot(grad_scores, keys, 1, 0).astype(BF)
        dk_s[low : low + width, :] += dot(grad_scores, query, 0, 0)
        dv_s[low : low + width, :] += dot(probs.astype(BF), grad, 0, 0)

    def store(i, core, x):
        rows = slice(i * piece, (i + 1) * piece)
        out_ref[core, x, :, 0:HEAD] = dq_s[rows, :]
        out_ref[core, x, :, HEAD : 2 * HEAD] = dk_s[rows, :].astype(BF)
        out_ref[core, x, :, 2 * HEAD : 3 * HEAD] = dv_s[rows, :].astype(BF)

    in_order(turn, store)


def on_device(
    hidden_in,
    segment_ids,
    qkv_weight,
    out_weight,
    up_weight,
    down_weight,
    norm1_gain,
    norm2_gain,
    out_cotangent,
):
    n = lax.axis_size("fsdp")
    tp = lax.axis_size("tp")
    ring = n // 4
    f = lax.axis_index("fsdp")
    t = lax.axis_index("tp")
    y, zl, zh = f & 1, (f >> 1) & 1, f >> 2
    low_half = zl == 0
    piece = hidden_in.shape[0]
    half = piece // 2
    sequence = piece * tp
    heads = H // tp // 2
    width = heads * HEAD
    unit = D // n
    pairs = [(k, j) for k in range(ring) for j in range(2)]
    far_first = range(ring - 1, -1, -1)
    steps = Steps()
    move, run, close = steps.move, steps.run, steps.close

    def over(axis, to, size):
        return lambda v: lax.ppermute(v, axis, [(i, to(i)) for i in range(size)])

    pp_core = over("tp", lambda i: i ^ 1, tp)
    pp_x = over("tp", lambda i: i ^ 2, tp)
    pp_zl = over("fsdp", lambda i: i ^ 2, n)
    pp_y = over("fsdp", lambda i: i ^ 1, n)
    pp_up = over("fsdp", lambda i: (i + 4) % n, n)
    pp_down = over("fsdp", lambda i: (i - 4) % n, n)

    def to_rel(v):
        cols = [v[..., b * unit : (b + 1) * unit] for b in range(n)]

        def pick(k, j, l):
            chosen = None
            for a in range(ring):
                both = jnp.where(y == j, cols[a * 4 + l * 2], cols[a * 4 + l * 2 + 1])
                chosen = both if chosen is None else jnp.where((zh - k) % ring == a, both, chosen)
            return chosen

        return jnp.concatenate([pick(k, j, l) for k, j in pairs for l in range(2)], axis=-1)

    def from_rel(v):
        cols = [v[..., b * unit : (b + 1) * unit] for b in range(n)]

        def pick(a, l, b):
            chosen = None
            for k in range(ring):
                both = jnp.where(y == b, cols[k * 4 + l], cols[k * 4 + 2 + l])
                chosen = both if chosen is None else jnp.where((zh - k) % ring == a, both, chosen)
            return chosen

        return jnp.concatenate(
            [pick(a, l, b) for a in range(ring) for l in range(2) for b in range(2)], axis=-1
        )

    def mine_of(first, second):
        return jnp.where(low_half, first, second)

    def joined(mine, other, axis):
        return jnp.concatenate(
            [jnp.where(low_half, mine, other), jnp.where(low_half, other, mine)], axis=axis
        )

    def plus(*terms):
        return sum(v.astype(F32) for v in terms).astype(BF)

    def ring_up(v):
        chain = [v]
        for _ in range(ring - 1):
            chain.append(pp_up(chain[-1]))
        return chain[1:]

    def cut_rows(v, c, of=2):
        size = v.shape[0] // of
        return v[c * size : (c + 1) * size]

    class Weight:
        def __init__(self, mine, other):
            self.have = {(0, 0, 0): mine}
            self.other = other
            self.chunks = {}

        def prepare(self, mine=1, other=1):
            first = self.have[0, 0, 0]
            if mine > 1:
                for c in range(mine):
                    self.chunks["mine", c] = run(lambda v, c=c: cut_rows(v, c, mine), first)
            if other > 1:
                for c in range(other):
                    self.chunks["other", c] = run(lambda v, c=c: cut_rows(v, c, other), self.other)

        def get(self, key):
            if isinstance(self.have[key], list):
                first, *rest = self.have[key]
                self.have[key] = stack_rows(steps.begin(first), *rest) if rest else first
            return self.have[key]

        def swap(self, c=0, of=1):
            got = move(pp_zl, self.chunks["other", c] if of > 1 else self.other)
            self.chunks["swap", c] = got
            if c == of - 1:
                self.have[0, 0, 1] = [self.chunks["swap", i] for i in range(of)]

        def zh(self, source, c=0, of=1):
            if source == 1 and of > 1 and ("swap", of - 1) in self.chunks:
                v = self.chunks["swap", c]
            elif source == 0 and of > 1:
                v = self.chunks["mine", c]
            elif of > 1:
                v = cut_rows(self.get((0, 0, source)), c, of)
            else:
                v = self.get((0, 0, source))
            self.chunks[source, c] = move(ring_up, v)
            if c == of - 1:
                for k in range(ring - 1):
                    self.have[k + 1, 0, source] = [self.chunks[source, i][k] for i in range(of)]

        def y(self, source):
            self.have[0, 1, source] = move(pp_y, self.get((0, 0, source)))

        def yz(self, source):
            for k in range(1, ring):
                self.have[k, 1, source] = move(pp_y, self.get((k, 0, source)))

        def blocks(self):
            found, starts = [], []
            for k, j in pairs:
                for source in range(2):
                    found.append(self.get((k, j, source)))
                    starts.append((2 * (2 * k + j) + (zl if source == 0 else 1 - zl)) * (unit // 128))
            return found, jnp.stack(starts).astype(jnp.int32)

    def halves(v, axis):
        lower, upper = jnp.split(v, 2, axis=axis)
        return mine_of(lower, upper), mine_of(upper, lower)

    gains = jnp.stack([norm1_gain, norm2_gain])
    gain_chain = [joined(gains, pp_zl(gains), 1)]
    gain_chain = jnp.concatenate(gain_chain + ring_up(gain_chain[0]), axis=0)
    gain_other = pp_y(gain_chain)
    qkv_heads = (
        qkv_weight.reshape(unit, 3, 2 * heads, HEAD)
        .transpose(0, 2, 1, 3)
        .reshape(unit, 2 * heads * 3 * HEAD)
    )
    qkv_w = Weight(*halves(qkv_heads, 1))
    out_mine, out_other = halves(out_weight, 0)
    other_ids = move(pp_zl, segment_ids)
    steps.pending += [gain_other, gain_chain, qkv_w.have[0, 0, 0], qkv_w.other, out_other]
    close()

    gains = jnp.concatenate(
        [(gain_chain, gain_other)[j][2 * k : 2 * k + 2] for k, j in pairs], axis=1
    ).astype(F32)
    gain_one, gain_two = gains[0:1], gains[1:2]
    qkv_w.swap()
    qkv_w.y(0)
    qkv_w.zh(0)
    out_swapped = move(pp_zl, out_other)
    x = to_rel(steps.begin(hidden_in)).astype(F32)
    normed_one, inverse_one = norm_forward(x)
    a_one = (normed_one * gain_one).astype(BF)
    cot = to_rel(steps.begin(out_cotangent))
    steps.pending += [a_one, cot]
    close()

    qkv_w.zh(1)
    qkv_w.y(1)
    qkv_w.yz(0)
    az = move(pp_zl, a_one)
    ax = move(pp_x, a_one)
    out_block = run(lambda v: joined(v, out_swapped, 1), out_mine)

    def first_of(ids):
        return jnp.sum((ids < ids.reshape(sequence, 1)).astype(jnp.int32), axis=-1, keepdims=True)

    start_a, start_b = run(first_of, segment_ids), run(first_of, other_ids)
    up_w = Weight(*run(lambda v: halves(v, 1), up_weight))
    down_w = Weight(*run(lambda v: halves(v, 0), down_weight))
    up_w.prepare(mine=2, other=2)
    down_w.prepare(mine=2, other=2)
    close()

    def gather(v, *pieces):
        return run(lambda first, *rest: stack_rows(first, *rest), v, *pieces)

    one_a = gather(a_one, ax)
    qkv_w.yz(1)
    ad = move(pp_x, az)
    out_w = Weight(out_block, None)
    out_w.zh(0)
    one_a_far = move(pp_core, one_a)
    up_w.swap(0, 2)
    close()

    turn = jnp.full((1,), t, jnp.int32)
    head_index = t * 2 * heads + zl * heads + jnp.arange(heads)
    slopes = 2.0 ** (-8.0 * (head_index + 1).astype(F32) / H)
    two = 2 * piece

    def batch(near, far):
        return [(near, 0, two), (far, 0, two)]

    w_qkv, at_qkv = qkv_w.blocks()
    one_b = gather(az, ad)
    one_b_far = move(pp_core, one_b)
    up_w.zh(0, 0, 2)
    out_w.y(0)
    out_w.yz(0)
    cx_top = move(pp_x, cot[:half])
    up_w.swap(1, 2)
    one_b_rows = batch(one_b, one_b_far)
    one_a_rows = batch(one_a, one_a_far)
    qkv_a = run(lambda v: deep(batch(v, one_a_far), w_qkv, at_qkv, 0), one_a)
    qkv_b = run(lambda v: deep(batch(one_b, v), w_qkv, at_qkv, 0), one_b_far)
    close()

    def spec(cols):
        return pl.BlockSpec((2, 2, piece, cols), lambda h, *_: (0, 0, 0, h))

    start_spec = pl.BlockSpec((sequence, 1), lambda h, *_: (0, 0))
    lse_spec = pl.BlockSpec((1, sequence, 1), lambda h, *_: (h, 0, 0))
    block = pltpu.VMEM((sequence, HEAD), BF)
    wide = pltpu.VMEM((sequence, HEAD), F32)

    def attend(qkv, start):
        out, lse = pl.pallas_call(
            attention_forward,
            out_shape=(
                jax.ShapeDtypeStruct((2, 2, piece, width), BF),
                jax.ShapeDtypeStruct((heads, sequence, 1), F32),
            ),
            grid_spec=pltpu.PrefetchScalarGridSpec(
                num_scalar_prefetch=2,
                grid=(heads,),
                in_specs=[spec(3 * HEAD), start_spec],
                out_specs=[spec(HEAD), lse_spec],
                scratch_shapes=[block] * 4,
            ),
            compiler_params=params(1),
            cost_estimate=cost(sequence, sequence, 2 * heads * HEAD),
            name="attention_forward",
        )(turn, slopes, qkv.reshape(2, 2, piece, 3 * width), start)
        return out.reshape(sequence, width), lse

    def attend_back(grad, qkv, start, lse):
        out = pl.pallas_call(
            attention_backward,
            out_shape=jax.ShapeDtypeStruct((2, 2, piece, 3 * width), BF),
            grid_spec=pltpu.PrefetchScalarGridSpec(
                num_scalar_prefetch=2,
                grid=(heads,),
                in_specs=[spec(3 * HEAD), spec(HEAD), start_spec, lse_spec],
                out_specs=spec(3 * HEAD),
                scratch_shapes=[block] * 5 + [wide] * 2,
            ),
            compiler_params=params(1),
            cost_estimate=cost(sequence, sequence, 4 * heads * HEAD),
            name="attention_backward",
        )(
            turn,
            slopes,
            qkv.reshape(2, 2, piece, 3 * width),
            grad.reshape(2, 2, piece, width),
            start,
            lse,
        )
        return out.reshape(sequence, 3 * width)

    def core_sum(near, far):
        got = move(pp_core, far)
        near = steps.begin(near)
        return tuple(plus(near[i * piece : (i + 1) * piece], got[i * piece : (i + 1) * piece]) for i in range(2))

    w_out = [out_w.get((k, j, 0)) for k, j in pairs]
    at_out = jnp.arange(len(pairs), dtype=jnp.int32) * (2 * unit // 128)
    att_b, lse_b = run(attend, qkv_b, start_b)
    sums_b = run(broad, att_b, w_out, at_out, 0)
    up_w.zh(0, 1, 2)
    up_w.y(0)
    cz_top = move(pp_zl, cot[:half])
    cx_bottom = move(pp_x, cot[half:])
    close()

    ez, ed = core_sum(*sums_b)
    from_d = pp_x(ed)
    steps.pending += [ez, from_d]
    up_w.zh(1, 0, 2)
    up_w.yz(0)
    cz_bottom = move(pp_zl, cot[half:])
    att_a, lse_a = run(attend, qkv_a, start_a)
    sums_a = run(broad, att_a, w_out, at_out, 0)
    close()

    e00, ex = core_sum(*sums_a)
    from_x = pp_x(ex)
    steps.pending += [e00, from_x]
    from_z = move(pp_zl, plus(steps.begin(ez), from_d))
    up_w.zh(1, 1, 2)
    up_w.y(1)
    cz = gather(cz_top, cz_bottom)
    near_cot_a = gather(cot, cx_top, cx_bottom)
    close()

    resid = x + (steps.begin(e00).astype(F32) + from_x.astype(F32) + from_z.astype(F32))
    normed_two, inverse_two = norm_forward(resid)
    a_two = (normed_two * gain_two).astype(BF)
    far_cot_a = move(pp_core, near_cot_a)
    ax = move(pp_x, a_two)
    az = move(pp_zl, a_two)
    down_w.zh(0, 0, 2)
    up_w.yz(1)
    close()

    w_up, at_up = up_w.blocks()

    def lift(near, far):
        return deep(batch(near, far), w_up, at_up, 0, finish=gelu_and_slope, outs=2, cuts=2)

    two_a = gather(a_two, ax)
    ad = move(pp_x, az)
    two_a_far = move(pp_core, two_a)
    down_w.zh(0, 1, 2)
    down_w.y(0)
    down_w.swap(0, 2)
    act_a, slope_a = run(lambda v: lift(two_a, v), two_a_far)
    close()

    two_b = gather(az, ad)
    two_b_far = move(pp_core, two_b)
    down_w.yz(0)
    down_w.swap(1, 2)
    down_w.zh(1, 0, 2)
    cd = move(pp_x, cz)
    act_b, slope_b = run(lambda v: lift(two_b, v), two_b_far)
    close()

    class Sum:
        def __init__(self, axis, whole=False):
            self.whole = whole
            self.parts = {}
            self.got = {}
            self.sums = {}
            self.value = {}
            self.axis = axis

        def make(self, j, a_sides, b_sides):
            def go(first):
                (head, *others), *sides = a_sides
                head = (first, *head[1:])
                return gram([[head, *others], *sides], b_sides, blocks, self.axis)

            if self.whole:
                keys = [(k, j, 0) for k in far_first]
                blocks = [(2 * k + j, 2 * unit) for k, j, _ in keys]
            else:
                keys = [(k, j, l) for k in far_first for l in range(2)]
                blocks = [((2 * k + j) * 2 + l, unit) for k, j, l in keys]
            for key, v in zip(keys, run(go, a_sides[0][0][0])):
                self.parts[key] = v

        def y_far(self, l):
            for k in range(ring - 1, 0, -1):
                self.sums[k, l] = move(pp_y, self.parts[k, 1, l])

        def y_own(self, l):
            self.got[l] = move(pp_y, self.parts[0, 1, l])

        def cut(self, v, r, of):
            size = v.shape[1 - self.axis] // of
            return lax.slice_in_dim(v, r * size, (r + 1) * size, axis=1 - self.axis)

        def part(self, k, l, r, of):
            mine = steps.begin(self.parts[k, 0, l])
            return self.cut(mine, r, of), self.cut(self.sums[k, l], r, of)

        def zh(self, l, r=0, of=2):
            value = plus(*self.part(ring - 1, l, r, of))
            for k in range(ring - 2, 0, -1):
                value = plus(move(pp_down, value), *self.part(k, l, r, of))
            self.value[l, r] = move(pp_down, value)

        def ready(self, r=0, of=2):
            def go(value):
                if self.whole:
                    total = plus(value, self.parts[0, 0, 0], self.got[0])
                    first, second = jnp.split(total, 2, axis=self.axis)
                else:
                    first, second = (
                        plus(v, self.cut(self.parts[0, 0, l], r, of), self.cut(self.got[l], r, of))
                        for l, v in enumerate((value, self.value[1, r]))
                    )
                return mine_of(first, second), mine_of(second, first)

            self.value[2, r], self.value[3, r] = run(go, self.value[0, r])

        def zl(self, r=0):
            self.value[3, r] = move(pp_zl, self.value[3, r])

        def result(self, of=2):
            mine = [self.value[2, r] for r in range(of)]
            other = [self.value[3, r] for r in range(of)]
            if of == 1:
                return mine[0], other[0]
            return tuple(jnp.concatenate(v, axis=1 - self.axis) for v in (mine, other))

    def finished(make):
        out = make()
        steps.pending.append(out)
        return out

    down_g, up_g, out_g, qkv_g = Sum(1), Sum(0), Sum(1, True), Sum(0)
    near_cot_b = gather(cz, cd)
    far_cot_b = move(pp_core, near_cot_b)
    down_w.zh(1, 1, 2)
    down_w.y(1)
    cot_a, cot_b = batch(near_cot_a, far_cot_a), batch(near_cot_b, far_cot_b)
    acts = [[(act_a, 0, 2 * two)], [(act_b, 0, 2 * two)]]
    down_g.make(1, acts, [cot_a, cot_b])
    close()
    down_w.yz(1)
    down_g.make(0, acts, [cot_a, cot_b])
    close()

    w_down, at_down = down_w.blocks()

    def pull(rows, slope):
        return deep(
            rows,
            w_down,
            at_down,
            1,
            finish=lambda total, s: (total * s.astype(F32),),
            extra=(slope,),
            cuts=1,
        )

    down_g.y_far(0)
    du_b = run(lambda v: pull(cot_b, v), slope_b)
    sums_b = run(broad, du_b, w_up, at_up, 1)
    close()

    ez, ed = core_sum(*sums_b)
    from_d = pp_x(ed)
    steps.pending += [ez, from_d]
    down_g.zh(0, 0)
    down_g.zh(0, 1)
    down_g.y_far(1)
    down_g.y_own(0)
    du_a = run(lambda v: pull(cot_a, v), slope_a)
    sums_a = run(broad, du_a, w_up, at_up, 1)
    close()

    e00, ex = core_sum(*sums_a)
    from_x = pp_x(ex)
    steps.pending += [e00, from_x]
    from_z = move(pp_zl, plus(steps.begin(ez), from_d))
    down_g.zh(1, 0)
    down_g.y_own(1)
    two_rows = [batch(two_a, two_a_far), batch(two_b, two_b_far)]
    dus = [[(du_a, 0, 2 * two)], [(du_b, 0, 2 * two)]]
    up_g.make(1, two_rows, dus)
    up_g.make(0, two_rows, dus)
    close()

    grad_in_two = steps.begin(e00).astype(F32) + from_x.astype(F32) + from_z.astype(F32)
    grad_part, grad_gain_two = norm_backward(grad_in_two, normed_two, inverse_two, gain_two)
    grad_resid = cot.astype(F32) + grad_part
    grad_rows = grad_resid.astype(BF)
    ax = move(pp_x, grad_rows)
    az = move(pp_zl, grad_rows)
    down_g.zh(1, 1)
    up_g.y_far(0)
    out_b = run(broad, act_b, w_down, at_down, 0)
    out_a = run(broad, act_a, w_down, at_down, 0)
    close()

    grad_a = gather(grad_rows, ax)
    grad_a_far = move(pp_core, grad_a)
    ad = move(pp_x, az)
    up_g.zh(0, 0)
    up_g.y_far(1)
    o_b = core_sum(*out_b)
    steps.pending += o_b
    dov_a = run(lambda v: deep(batch(grad_a, v), w_out, at_out, 1), grad_a_far)
    proj_a = attend_back(dov_a, qkv_a, start_a, lse_a)
    steps.pending.append(proj_a)
    close()

    grad_b = gather(az, ad)
    grad_b_far = move(pp_core, grad_b)
    up_g.zh(1, 0)
    up_g.y_own(0)
    oz, od = o_b
    from_od = move(pp_x, od)
    o_a = core_sum(*out_a)
    steps.pending += o_a
    down_g.ready(0)
    down_g.ready(1)
    dov_b = run(lambda v: deep(batch(grad_b, v), w_out, at_out, 1), grad_b_far)
    proj_b = attend_back(dov_b, qkv_b, start_b, lse_b)
    steps.pending.append(proj_b)
    close()

    one_rows = [one_a_rows, one_b_rows]
    projs = [[(proj_a, 0, 2 * two)], [(proj_b, 0, 2 * two)]]
    o00, ox = o_a
    from_ox = move(pp_x, ox)
    from_oz = move(pp_zl, plus(steps.begin(oz), from_od))
    up_g.zh(0, 1)
    up_g.y_own(1)
    qkv_g.make(1, one_rows, projs)
    qkv_g.make(0, one_rows, projs)
    atts = [[(att_a, 0, 2 * two)], [(att_b, 0, 2 * two)]]
    grads = [batch(grad_a, grad_a_far), batch(grad_b, grad_b_far)]
    out_g.make(1, atts, grads)
    close()

    down_g.zl(0)
    down_g.zl(1)
    qkv_g.y_far(0)
    up_g.zh(1, 1)
    sums_b = run(broad, proj_b, w_qkv, at_qkv, 1)
    out_g.y_far(0)
    up_g.ready(0)
    out_g.make(0, atts, grads)
    block_out = run(
        lambda v: from_rel(
            (resid + (v.astype(F32) + from_ox.astype(F32) + from_oz.astype(F32))).astype(BF)
        ),
        o00,
    )
    close()

    ez, ed = core_sum(*sums_b)
    from_d = pp_x(ed)
    steps.pending += [ez, from_d]
    qkv_g.zh(0, 0, 1)
    qkv_g.y_far(1)
    up_g.zl(0)
    up_g.ready(1)
    up_g.zl(1)
    sums_a = run(broad, proj_a, w_qkv, at_qkv, 1)
    grad_down = finished(lambda: joined(steps.begin(down_g.result()[0]), down_g.result()[1], 0).astype(F32))
    close()

    e00, ex = core_sum(*sums_a)
    from_x = pp_x(ex)
    steps.pending += [e00, from_x]
    from_z = move(pp_zl, plus(steps.begin(ez), from_d))
    qkv_g.zh(1, 0, 1)
    qkv_g.y_own(0)
    qkv_g.y_own(1)
    close()

    out_g.y_own(0)
    out_g.zh(0, 0, 1)
    qkv_g.ready(0, 1)
    grad_up = finished(lambda: joined(steps.begin(up_g.result()[0]), up_g.result()[1], 1).astype(F32))
    qkv_g.value[3, 0] = pp_zl(qkv_g.value[3, 0])
    steps.pending.append(qkv_g.value[3, 0])
    grad_in_one = steps.begin(e00).astype(F32) + from_x.astype(F32) + from_z.astype(F32)
    grad_part, grad_gain_one = norm_backward(grad_in_one, normed_one, inverse_one, gain_one)
    grad_in = from_rel(grad_resid + grad_part)
    gain_grads = from_rel(jnp.stack([grad_gain_one, grad_gain_two]))
    for step in (pp_core, pp_x, pp_y):
        gain_grads = gain_grads + step(gain_grads)
    steps.pending += [grad_in, gain_grads]
    close()

    def parts_first(v):
        return v.reshape(unit, heads, 3, HEAD).transpose(0, 2, 1, 3).reshape(unit, 3, width)

    out_g.ready(0, 1)
    out_g.value[3, 0] = pp_zl(out_g.value[3, 0])
    mine, other = qkv_g.result(1)
    grad_qkv = finished(
        lambda: joined(parts_first(steps.begin(mine)), parts_first(other), 2).astype(F32)
    )
    gain_grads = steps.begin(gain_grads)
    gain_grads = gain_grads + pp_zl(gain_grads)
    moving = gain_grads
    for _ in range(ring - 1):
        moving = pp_up(moving)
        gain_grads = gain_grads + moving
    size = D // (n * tp)
    gain_grads = lax.dynamic_slice_in_dim(gain_grads, (f * tp + t) * size, size, axis=1)

    grad_out = joined(*out_g.result(1), 0).astype(F32)

    return (
        block_out,
        grad_in,
        gain_grads[0],
        gain_grads[1],
        grad_qkv,
        grad_out,
        grad_up,
        grad_down,
    )


def solution(mesh):
    return jax.shard_map(
        on_device,
        mesh=mesh,
        in_specs=(
            P(("fsdp", "tp"), None),
            P("fsdp", None),
            P("fsdp", None, "tp"),
            P("tp", "fsdp"),
            P("fsdp", "tp"),
            P("tp", "fsdp"),
            P("fsdp"),
            P("fsdp"),
            P(("fsdp", "tp"), None),
        ),
        out_specs=(
            P(("fsdp", "tp"), None),
            P(("fsdp", "tp"), None),
            P(("fsdp", "tp")),
            P(("fsdp", "tp")),
            P("fsdp", None, "tp"),
            P("tp", "fsdp"),
            P("fsdp", "tp"),
            P("tp", "fsdp"),
        ),
        check_vma=False,
    )
```

```python
import functools
import math

import jax
import jax.numpy as jnp
from jax import lax
from jax.experimental import pallas as pl
from jax.experimental.pallas import tpu as pltpu
from jax.sharding import PartitionSpec as P

D = 4096
H = 32
HEAD = D // H
REACH = 640
NORM_EPSILON = 1e-05
SQRT_HALF = 0.7071067811865476
INV_ROOT_TWO_PI = 0.3989422804014327
BF = jnp.bfloat16
F32 = jnp.float32
COVER = 0.05
VMEM = 56 << 20


def norm_forward(values_in):
    row_mean = jnp.mean(values_in, axis=-1, keepdims=True)
    centred = values_in - row_mean
    row_variance = jnp.mean(centred * centred, axis=-1, keepdims=True)
    inverse = lax.rsqrt(row_variance + NORM_EPSILON)
    return centred * inverse, inverse


def norm_backward(grad_out, normed, inverse, gain):
    grad_gain = jnp.sum(grad_out * normed, axis=0)
    scaled = grad_out * gain
    mean_one = jnp.mean(scaled, axis=-1, keepdims=True)
    mean_two = jnp.mean(scaled * normed, axis=-1, keepdims=True)
    return inverse * (scaled - mean_one - normed * mean_two), grad_gain


def gelu_and_slope(pre_act):
    part = 0.5 * (1.0 + lax.erf(pre_act * SQRT_HALF))
    slope = part + pre_act * jnp.exp(-0.5 * pre_act * pre_act) * INV_ROOT_TWO_PI
    return pre_act * part, slope


def dot(left, right, cl, cr):
    return lax.dot_general(left, right, (((cl,), (cr,)), ((), ())), preferred_element_type=F32)


class Steps:
    def __init__(self):
        self.token = jnp.zeros((1,), F32)
        self.pending = []
        self.first = True

    def begin(self, value):
        if self.first:
            return value
        return lax.optimization_barrier((value, self.token))[0]

    def move(self, how, value):
        out = how(self.begin(value))
        self.pending.append(out)
        return out

    def run(self, how, value, *more, **named):
        out = how(self.begin(value), *more, **named)
        self.pending += jax.tree.leaves(out)
        return out

    def close(self):
        self.token = lax.optimization_barrier((self.token, *self.pending))[0]
        self.pending = []
        self.first = False


def params(grid_dims):
    return pltpu.CompilerParams(
        dimension_semantics=("arbitrary",) * grid_dims, vmem_limit_bytes=VMEM
    )


def cost(m, n, k):
    return pl.CostEstimate(
        flops=int(2 * m * n * k * COVER), transcendentals=0, bytes_accessed=2 * (m * k + k * n + m * n)
    )


def tile(size, most):
    if size <= most:
        return size
    while size % most:
        most -= 128
    return most


def stack_rows(*pieces):
    rows = math.gcd(*(v.shape[0] for v in pieces))
    cols = pieces[0].shape[1]
    sizes = [v.shape[0] // rows for v in pieces]
    firsts = [sum(sizes[:i]) for i in range(len(pieces))]

    def body(*refs):
        step = pl.program_id(0)
        for ref, first, size in zip(refs, firsts, sizes):

            @pl.when((step >= first) & (step < first + size))
            def _(ref=ref):
                refs[-1][...] = ref[...]

    def spec(first, size):
        return pl.BlockSpec((rows, cols), lambda g: (jnp.clip(g - first, 0, size - 1), 0))

    return pl.pallas_call(
        body,
        out_shape=jax.ShapeDtypeStruct((sum(sizes) * rows, cols), pieces[0].dtype),
        grid=(sum(sizes),),
        in_specs=[spec(f, s) for f, s in zip(firsts, sizes)],
        out_specs=pl.BlockSpec((rows, cols), lambda g: (g, 0)),
        compiler_params=params(1),
        name="stack_rows",
    )(*pieces)


def gram(a_sides, b_sides, blocks, side):
    width = blocks[0][1]
    m = width if side == 0 else a_sides[0][0][0].shape[1]
    n = width if side == 1 else b_sides[0][0][0].shape[1]
    tm, tn = tile(m, 1024), tile(n, 1024)
    grid_m, grid_n = m // tm, n // tn
    count = len(blocks)
    per = grid_m * grid_n

    def at(g):
        p, r = g // per, g % per
        return p, r // grid_m, r % grid_m

    def a_spec(row, rows):
        def index_map(g, index):
            p, _, i = at(g)
            return row, (index[p] * grid_m + i if side == 0 else i)

        return pl.BlockSpec((rows, tm), index_map)

    def b_spec(row, rows):
        def index_map(g, index):
            p, j, _ = at(g)
            return row, (index[p] * grid_n + j if side == 1 else j)

        return pl.BlockSpec((rows, tn), index_map)

    def out_map(q):
        def at_q(g, index):
            r = jnp.clip(g - q * per, 0, per - 1)
            return r % grid_m, r // grid_m

        return at_q

    def body(index_ref, *refs):
        refs = list(refs)

        def take(batch):
            parts = [refs.pop(0)[...] for _ in batch]
            return parts[0] if len(parts) == 1 else jnp.concatenate(parts, axis=0)

        lefts = [take(batch) for batch in a_sides]
        rights = [take(batch) for batch in b_sides]
        total = None
        for left, right in zip(lefts, rights):
            part = dot(left, right, 0, 0)
            total = part if total is None else total + part
        total = total.astype(BF)
        p = pl.program_id(0) // per
        for q in range(count):

            @pl.when(p == q)
            def _(q=q):
                refs[q][...] = total

    flat_a = [piece for batch in a_sides for piece in batch]
    flat_b = [piece for batch in b_sides for piece in batch]
    depth = sum(piece[2] for piece in flat_a)
    return pl.pallas_call(
        body,
        out_shape=[jax.ShapeDtypeStruct((m, n), BF)] * count,
        grid_spec=pltpu.PrefetchScalarGridSpec(
            num_scalar_prefetch=1,
            grid=(count * per,),
            in_specs=[a_spec(row, rows) for _, row, rows in flat_a]
            + [b_spec(row, rows) for _, row, rows in flat_b],
            out_specs=[pl.BlockSpec((tm, tn), out_map(q)) for q in range(count)],
        ),
        compiler_params=params(1),
        cost_estimate=cost(m, n * count, depth),
        name="gram",
    )(
        jnp.array([b[0] for b in blocks], jnp.int32),
        *(piece[0] for piece in flat_a),
        *(piece[0] for piece in flat_b),
    )


def deep(pieces, blocks, starts, cr, finish=None, extra=(), outs=1, tn=512, cuts=1):
    sizes = [rows for _, _, rows in pieces]
    m, k = sum(sizes), pieces[0][0].shape[1]
    n = blocks[0].shape[1 - cr]
    count, heights = len(blocks), len(pieces)
    tn = tile(n, tn)
    work = []
    for i, rows in enumerate(sizes):
        for c in range(cuts):
            height = rows // cuts
            work.append((i, c * height, sum(sizes[:i]) + c * height, height))

    def body(starts_ref, *refs):
        a_refs, rest = refs[:heights], refs[heights:]

        def part(i, first, height):
            total = None
            for p in range(count):
                size = blocks[p].shape[cr]
                at = pl.multiple_of(starts_ref[p] * 128, 128)
                term = dot(a_refs[i][first : first + height, pl.ds(at, size)], rest[p][...], 1, cr)
                total = term if total is None else total + term
            return total

        def store(first, height, total):
            at = slice(first, first + height)
            values = (total,) if finish is None else finish(total, *(v[at, :] for v in rest[count:-outs]))
            for ref, value in zip(rest[-outs:], values):
                ref[at, :] = value.astype(BF)

        before = None
        for i, first, row, height in work:
            total = part(i, first, height)
            if before is not None:
                store(*before)
            before = (row, height, total)
        store(*before)

    def a_spec(row, rows):
        return pl.BlockSpec((rows, k), lambda j, *_: (row, 0), pipeline_mode=pl.Buffered(1))

    def w_spec(w):
        size = w.shape[cr]
        if cr == 0:
            return pl.BlockSpec((size, tn), lambda j, *_: (0, j))
        return pl.BlockSpec((tn, size), lambda j, *_: (j, 0))

    out = pl.BlockSpec((m, tn), lambda j, *_: (0, j))
    result = pl.pallas_call(
        body,
        out_shape=[jax.ShapeDtypeStruct((m, n), BF)] * outs,
        grid_spec=pltpu.PrefetchScalarGridSpec(
            num_scalar_prefetch=1,
            grid=(n // tn,),
            in_specs=[a_spec(row, rows) for _, row, rows in pieces]
            + [w_spec(w) for w in blocks]
            + [out] * len(extra),
            out_specs=[out] * outs,
        ),
        compiler_params=params(1),
        cost_estimate=cost(m, n, k),
        name="deep",
    )(starts, *(piece[0] for piece in pieces), *blocks, *extra)
    return result[0] if outs == 1 else result


def broad(a, blocks, starts, cr):
    m, k = a.shape
    n = sum(w.shape[1 - cr] for w in blocks)
    count = len(blocks)
    tm = tile(m // 2, 320)
    steps = m // 2 // tm

    def body(starts_ref, a_ref, *rest):
        for which in range(2):

            @pl.when(pl.program_id(0) // steps == which)
            def _(out=rest[count + which]):
                for p in range(count):
                    size = blocks[p].shape[1 - cr]
                    at = pl.multiple_of(starts_ref[p] * 128, 128)
                    out[:, pl.ds(at, size)] = dot(a_ref[...], rest[p][...], 1, cr).astype(BF)

    return pl.pallas_call(
        body,
        out_shape=[jax.ShapeDtypeStruct((m // 2, n), BF)] * 2,
        grid_spec=pltpu.PrefetchScalarGridSpec(
            num_scalar_prefetch=1,
            grid=(2 * steps,),
            in_specs=[pl.BlockSpec((tm, k), lambda i, *_: (i, 0))]
            + [pl.BlockSpec(w.shape, lambda i, *_: (0, 0), pipeline_mode=pl.Buffered(1)) for w in blocks],
            out_specs=[
                pl.BlockSpec((tm, n), lambda i, *_: (jnp.minimum(i, steps - 1), 0)),
                pl.BlockSpec((tm, n), lambda i, *_: (jnp.maximum(i - steps, 0), 0)),
            ],
        ),
        compiler_params=params(1),
        cost_estimate=cost(m, n, k),
        name="broad",
    )(starts, a, *blocks)


QB = 256


def window(first):
    low = max(0, first - REACH)
    return low, first + QB - low


def masked_scores(q, k, start, slope, first, low, width, scale):
    scores = dot(q, k, 1, 1)
    row = first + lax.broadcasted_iota(jnp.int32, (QB, width), 0)
    col = low + lax.broadcasted_iota(jnp.int32, (QB, width), 1)
    scores = scores * scale - slope * (row - col).astype(F32)
    return jnp.where((col >= start) & (col <= row), scores, -1e30)


def in_order(turn, visit):
    for i in range(4):
        rel = lax.bitwise_xor(jnp.int32(i), turn)
        visit(i, lax.bitwise_and(rel, 1), lax.shift_right_logical(rel, 1))


def attention_forward(turn_ref, slope_ref, qkv_ref, start_ref, o_ref, lse_ref, q_s, k_s, v_s, o_s):
    turn = turn_ref[0]
    slope = slope_ref[pl.program_id(0)]
    sequence = q_s.shape[0]
    piece = sequence // 4
    scale = 1.0 / math.sqrt(HEAD)

    def load(i, core, x):
        block = qkv_ref[core, x]
        for j, scratch in enumerate((q_s, k_s, v_s)):
            scratch[i * piece : (i + 1) * piece, :] = block[:, j * HEAD : (j + 1) * HEAD]

    in_order(turn, load)
    for first in range(0, sequence, QB):
        low, width = window(first)
        scores = masked_scores(
            q_s[first : first + QB, :],
            k_s[low : low + width, :],
            start_ref[first : first + QB, :],
            slope,
            first,
            low,
            width,
            scale,
        )
        peak = jnp.max(scores, axis=-1, keepdims=True)
        weights = jnp.exp(scores - peak)
        total = jnp.sum(weights, axis=-1, keepdims=True)
        lse_ref[0, first : first + QB, :] = peak + jnp.log(total)
        probs = (weights * (1.0 / total)).astype(BF)
        o_s[first : first + QB, :] = dot(probs, v_s[low : low + width, :], 1, 0).astype(BF)

    def store(i, core, x):
        o_ref[core, x] = o_s[i * piece : (i + 1) * piece, :]

    in_order(turn, store)


def attention_backward(
    turn_ref, slope_ref, qkv_ref, do_ref, start_ref, lse_ref, out_ref, q_s, k_s, v_s, do_s, dq_s, dk_s, dv_s
):
    turn = turn_ref[0]
    slope = slope_ref[pl.program_id(0)]
    sequence = q_s.shape[0]
    piece = sequence // 4
    scale = 1.0 / math.sqrt(HEAD)

    def load(i, core, x):
        rows = slice(i * piece, (i + 1) * piece)
        block = qkv_ref[core, x]
        for j, scratch in enumerate((q_s, k_s, v_s)):
            scratch[rows, :] = block[:, j * HEAD : (j + 1) * HEAD]
        do_s[rows, :] = do_ref[core, x]

    in_order(turn, load)
    dk_s[...] = jnp.zeros_like(dk_s)
    dv_s[...] = jnp.zeros_like(dv_s)
    for first in range(0, sequence, QB):
        low, width = window(first)
        keys = k_s[low : low + width, :]
        query = q_s[first : first + QB, :]
        grad = do_s[first : first + QB, :]
        scores = masked_scores(
            query, keys, start_ref[first : first + QB, :], slope, first, low, width, scale
        )
        probs = jnp.exp(scores - lse_ref[0, first : first + QB, :])
        grad_probs = dot(grad, v_s[low : low + width, :], 1, 1)
        delta = jnp.sum(probs * grad_probs, axis=-1, keepdims=True)
        grad_scores = (probs * (grad_probs - delta) * scale).astype(BF)
        dq_s[first : first + QB, :] = dot(grad_scores, keys, 1, 0).astype(BF)
        dk_s[low : low + width, :] += dot(grad_scores, query, 0, 0)
        dv_s[low : low + width, :] += dot(probs.astype(BF), grad, 0, 0)

    def store(i, core, x):
        rows = slice(i * piece, (i + 1) * piece)
        out_ref[core, x, :, 0:HEAD] = dq_s[rows, :]
        out_ref[core, x, :, HEAD : 2 * HEAD] = dk_s[rows, :].astype(BF)
        out_ref[core, x, :, 2 * HEAD : 3 * HEAD] = dv_s[rows, :].astype(BF)

    in_order(turn, store)


def on_device(
    hidden_in,
    segment_ids,
    qkv_weight,
    out_weight,
    up_weight,
    down_weight,
    norm1_gain,
    norm2_gain,
    out_cotangent,
):
    n = lax.axis_size("fsdp")
    tp = lax.axis_size("tp")
    ring = n // 4
    f = lax.axis_index("fsdp")
    t = lax.axis_index("tp")
    y, zl, zh = f & 1, (f >> 1) & 1, f >> 2
    low_half = zl == 0
    piece = hidden_in.shape[0]
    half = piece // 2
    sequence = piece * tp
    heads = H // tp // 2
    width = heads * HEAD
    unit = D // n
    pairs = [(k, j) for k in range(ring) for j in range(2)]
    far_first = range(ring - 1, -1, -1)
    steps = Steps()
    move, run, close = steps.move, steps.run, steps.close

    def over(axis, to, size):
        return lambda v: lax.ppermute(v, axis, [(i, to(i)) for i in range(size)])

    pp_core = over("tp", lambda i: i ^ 1, tp)
    pp_x = over("tp", lambda i: i ^ 2, tp)
    pp_zl = over("fsdp", lambda i: i ^ 2, n)
    pp_y = over("fsdp", lambda i: i ^ 1, n)
    pp_up = over("fsdp", lambda i: (i + 4) % n, n)
    pp_down = over("fsdp", lambda i: (i - 4) % n, n)

    def to_rel(v):
        cols = [v[..., b * unit : (b + 1) * unit] for b in range(n)]

        def pick(k, j, l):
            chosen = None
            for a in range(ring):
                both = jnp.where(y == j, cols[a * 4 + l * 2], cols[a * 4 + l * 2 + 1])
                chosen = both if chosen is None else jnp.where((zh - k) % ring == a, both, chosen)
            return chosen

        return jnp.concatenate([pick(k, j, l) for k, j in pairs for l in range(2)], axis=-1)

    def from_rel(v):
        cols = [v[..., b * unit : (b + 1) * unit] for b in range(n)]

        def pick(a, l, b):
            chosen = None
            for k in range(ring):
                both = jnp.where(y == b, cols[k * 4 + l], cols[k * 4 + 2 + l])
                chosen = both if chosen is None else jnp.where((zh - k) % ring == a, both, chosen)
            return chosen

        return jnp.concatenate(
            [pick(a, l, b) for a in range(ring) for l in range(2) for b in range(2)], axis=-1
        )

    def mine_of(first, second):
        return jnp.where(low_half, first, second)

    def joined(mine, other, axis):
        return jnp.concatenate(
            [jnp.where(low_half, mine, other), jnp.where(low_half, other, mine)], axis=axis
        )

    def plus(*terms):
        return sum(v.astype(F32) for v in terms).astype(BF)

    def ring_up(v):
        chain = [v]
        for _ in range(ring - 1):
            chain.append(pp_up(chain[-1]))
        return chain[1:]

    def cut_rows(v, c, of=2):
        size = v.shape[0] // of
        return v[c * size : (c + 1) * size]

    class Weight:
        def __init__(self, mine, other):
            self.have = {(0, 0, 0): mine}
            self.other = other
            self.chunks = {}

        def prepare(self, mine=1, other=1):
            first = self.have[0, 0, 0]
            if mine > 1:
                for c in range(mine):
                    self.chunks["mine", c] = run(lambda v, c=c: cut_rows(v, c, mine), first)
            if other > 1:
                for c in range(other):
                    self.chunks["other", c] = run(lambda v, c=c: cut_rows(v, c, other), self.other)

        def get(self, key):
            if isinstance(self.have[key], list):
                first, *rest = self.have[key]
                self.have[key] = stack_rows(steps.begin(first), *rest) if rest else first
            return self.have[key]

        def swap(self, c=0, of=1):
            got = move(pp_zl, self.chunks["other", c] if of > 1 else self.other)
            self.chunks["swap", c] = got
            if c == of - 1:
                self.have[0, 0, 1] = [self.chunks["swap", i] for i in range(of)]

        def zh(self, source, c=0, of=1):
            if source == 1 and of > 1 and ("other", c) in self.chunks:
                v = self.chunks["swap", c]
            elif source == 0 and of > 1:
                v = self.chunks["mine", c]
            elif of > 1:
                v = cut_rows(self.get((0, 0, source)), c, of)
            else:
                v = self.get((0, 0, source))
            self.chunks[source, c] = move(ring_up, v)
            if c == of - 1:
                for k in range(ring - 1):
                    self.have[k + 1, 0, source] = [self.chunks[source, i][k] for i in range(of)]

        def y(self, source):
            self.have[0, 1, source] = move(pp_y, self.get((0, 0, source)))

        def yz(self, source):
            for k in range(1, ring):
                self.have[k, 1, source] = move(pp_y, self.get((k, 0, source)))

        def blocks(self):
            found, starts = [], []
            for k, j in pairs:
                for source in range(2):
                    found.append(self.get((k, j, source)))
                    starts.append((2 * (2 * k + j) + (zl if source == 0 else 1 - zl)) * (unit // 128))
            return found, jnp.stack(starts).astype(jnp.int32)

    def halves(v, axis):
        lower, upper = jnp.split(v, 2, axis=axis)
        return mine_of(lower, upper), mine_of(upper, lower)

    gains = jnp.stack([norm1_gain, norm2_gain])
    gain_chain = [joined(gains, pp_zl(gains), 1)]
    gain_chain = jnp.concatenate(gain_chain + ring_up(gain_chain[0]), axis=0)
    qkv_heads = (
        qkv_weight.reshape(unit, 3, 2 * heads, HEAD)
        .transpose(0, 2, 1, 3)
        .reshape(unit, 2 * heads * 3 * HEAD)
    )
    qkv_w = Weight(*halves(qkv_heads, 1))
    out_mine, out_other = halves(out_weight, 0)
    other_ids = move(pp_zl, segment_ids)
    steps.pending += [gain_chain, qkv_w.have[0, 0, 0], qkv_w.other, out_other]
    close()

    gain_other = move(pp_y, gain_chain)
    gains = jnp.concatenate(
        [(gain_chain, gain_other)[j][2 * k : 2 * k + 2] for k, j in pairs], axis=1
    ).astype(F32)
    gain_one, gain_two = gains[0:1], gains[1:2]
    qkv_w.swap()
    qkv_w.y(0)
    qkv_w.zh(0)
    out_swapped = move(pp_zl, out_other)
    x = to_rel(steps.begin(hidden_in)).astype(F32)
    normed_one, inverse_one = norm_forward(x)
    a_one = (normed_one * gain_one).astype(BF)
    cot = to_rel(steps.begin(out_cotangent))
    steps.pending += [a_one, cot]
    close()

    qkv_w.zh(1)
    qkv_w.y(1)
    qkv_w.yz(0)
    az = move(pp_zl, a_one)
    ax = move(pp_x, a_one)
    out_block = run(lambda v: joined(v, out_swapped, 1), out_mine)

    def first_of(ids):
        return jnp.sum((ids < ids.reshape(sequence, 1)).astype(jnp.int32), axis=-1, keepdims=True)

    start_a, start_b = run(first_of, segment_ids), run(first_of, other_ids)
    up_w = Weight(*run(lambda v: halves(v, 1), up_weight))
    down_w = Weight(*run(lambda v: halves(v, 0), down_weight))
    up_w.prepare(mine=2, other=2)
    down_w.prepare(mine=2, other=2)
    close()

    def gather(v, *pieces):
        return run(lambda first, *rest: stack_rows(first, *rest), v, *pieces)

    one_a = gather(a_one, ax)
    qkv_w.yz(1)
    ad = move(pp_x, az)
    out_w = Weight(out_block, None)
    out_w.zh(0)
    one_a_far = move(pp_core, one_a)
    up_w.swap(0, 2)
    close()

    turn = jnp.full((1,), t, jnp.int32)
    head_index = t * 2 * heads + zl * heads + jnp.arange(heads)
    slopes = 2.0 ** (-8.0 * (head_index + 1).astype(F32) / H)
    two = 2 * piece

    def batch(*pieces):
        return [(v, 0, v.shape[0]) for v in pieces]

    w_qkv, at_qkv = qkv_w.blocks()
    one_b = gather(az, ad)
    one_b_far = move(pp_core, one_b)
    up_w.zh(0, 0, 2)
    out_w.y(0)
    out_w.yz(0)
    cx = move(pp_x, cot)
    cz_top = move(pp_zl, cot[:half])
    one_b_rows = batch(one_b, one_b_far)
    one_a_rows = batch(one_a, one_a_far)
    qkv_a = run(lambda v: deep(batch(v, one_a_far), w_qkv, at_qkv, 0), one_a)
    qkv_b = run(lambda v: deep(batch(one_b, v), w_qkv, at_qkv, 0), one_b_far)
    close()

    def spec(cols):
        return pl.BlockSpec((2, 2, piece, cols), lambda h, *_: (0, 0, 0, h))

    start_spec = pl.BlockSpec((sequence, 1), lambda h, *_: (0, 0))
    lse_spec = pl.BlockSpec((1, sequence, 1), lambda h, *_: (h, 0, 0))
    block = pltpu.VMEM((sequence, HEAD), BF)
    wide = pltpu.VMEM((sequence, HEAD), F32)

    def attend(qkv, start):
        out, lse = pl.pallas_call(
            attention_forward,
            out_shape=(
                jax.ShapeDtypeStruct((2, 2, piece, width), BF),
                jax.ShapeDtypeStruct((heads, sequence, 1), F32),
            ),
            grid_spec=pltpu.PrefetchScalarGridSpec(
                num_scalar_prefetch=2,
                grid=(heads,),
                in_specs=[spec(3 * HEAD), start_spec],
                out_specs=[spec(HEAD), lse_spec],
                scratch_shapes=[block] * 4,
            ),
            compiler_params=params(1),
            cost_estimate=cost(sequence, sequence, 2 * heads * HEAD),
            name="attention_forward",
        )(turn, slopes, qkv.reshape(2, 2, piece, 3 * width), start)
        return out.reshape(sequence, width), lse

    def attend_back(grad, qkv, start, lse):
        out = pl.pallas_call(
            attention_backward,
            out_shape=jax.ShapeDtypeStruct((2, 2, piece, 3 * width), BF),
            grid_spec=pltpu.PrefetchScalarGridSpec(
                num_scalar_prefetch=2,
                grid=(heads,),
                in_specs=[spec(3 * HEAD), spec(HEAD), start_spec, lse_spec],
                out_specs=spec(3 * HEAD),
                scratch_shapes=[block] * 5 + [wide] * 2,
            ),
            compiler_params=params(1),
            cost_estimate=cost(sequence, sequence, 4 * heads * HEAD),
            name="attention_backward",
        )(
            turn,
            slopes,
            qkv.reshape(2, 2, piece, 3 * width),
            grad.reshape(2, 2, piece, width),
            start,
            lse,
        )
        return out.reshape(sequence, 3 * width)

    def core_sum(near, far):
        got = move(pp_core, far)
        near = steps.begin(near)
        return tuple(plus(near[i * piece : (i + 1) * piece], got[i * piece : (i + 1) * piece]) for i in range(2))

    w_out = [out_w.get((k, j, 0)) for k, j in pairs]
    at_out = jnp.arange(len(pairs), dtype=jnp.int32) * (2 * unit // 128)
    att_b, lse_b = run(attend, qkv_b, start_b)
    sums_b = run(broad, att_b, w_out, at_out, 0)
    up_w.zh(0, 1, 2)
    up_w.y(0)
    cz_bottom = move(pp_zl, cot[half:])
    cd_top = move(pp_x, cz_top)
    near_cot_a = gather(cot, cx)
    far_cot_a = pp_core(near_cot_a)
    steps.pending.append(far_cot_a)
    close()

    ez, ed = core_sum(*sums_b)
    from_d = pp_x(ed)
    steps.pending += [ez, from_d]
    up_w.zh(1, 0, 2)
    up_w.yz(0)
    up_w.swap(1, 2)
    att_a, lse_a = run(attend, qkv_a, start_a)
    sums_a = run(broad, att_a, w_out, at_out, 0)
    close()

    e00, ex = core_sum(*sums_a)
    from_x = pp_x(ex)
    steps.pending += [e00, from_x]
    from_z = move(pp_zl, plus(steps.begin(ez), from_d))
    up_w.zh(1, 1, 2)
    up_w.y(1)
    close()

    resid = x + (steps.begin(e00).astype(F32) + from_x.astype(F32) + from_z.astype(F32))
    normed_two, inverse_two = norm_forward(resid)
    a_two = (normed_two * gain_two).astype(BF)
    a_two_far = move(pp_core, a_two)
    ax = move(pp_x, a_two)
    az = move(pp_zl, a_two)
    down_w.zh(0, 0, 2)
    up_w.yz(1)
    close()

    w_up, at_up = up_w.blocks()

    def lift(*pieces):
        return deep(batch(*pieces), w_up, at_up, 0, finish=gelu_and_slope, outs=2)

    ax_far = move(pp_core, ax)
    ad = move(pp_x, az)
    two_a = (a_two, ax, a_two_far, ax_far)
    down_w.zh(0, 1, 2)
    down_w.y(0)
    down_w.swap(0, 2)
    act_a, slope_a = run(lambda v: lift(a_two, ax, a_two_far, v), ax_far)
    close()

    az_far, ad_far = move(pp_core, az), move(pp_core, ad)
    two_b = (az, ad, az_far, ad_far)
    down_w.yz(0)
    down_w.swap(1, 2)
    down_w.zh(1, 0, 2)
    cd_bottom = move(pp_x, cz_bottom)
    act_b, slope_b = run(lambda v: lift(*two_b[:3], v), ad_far)
    close()

    class Sum:
        def __init__(self, axis, whole=False):
            self.whole = whole
            self.parts = {}
            self.got = {}
            self.sums = {}
            self.value = {}
            self.axis = axis

        def make(self, j, a_sides, b_sides):
            def go(first):
                (head, *others), *sides = a_sides
                head = (first, *head[1:])
                return gram([[head, *others], *sides], b_sides, blocks, self.axis)

            if self.whole:
                keys = [(k, j, 0) for k in far_first]
                blocks = [(2 * k + j, 2 * unit) for k, j, _ in keys]
            else:
                keys = [(k, j, l) for k in far_first for l in range(2)]
                blocks = [((2 * k + j) * 2 + l, unit) for k, j, l in keys]
            for key, v in zip(keys, run(go, a_sides[0][0][0])):
                self.parts[key] = v

        def y_far(self, l):
            for k in range(ring - 1, 0, -1):
                self.sums[k, l] = move(pp_y, self.parts[k, 1, l])

        def y_own(self, l):
            self.got[l] = move(pp_y, self.parts[0, 1, l])

        def cut(self, v, r, of):
            size = v.shape[1 - self.axis] // of
            return lax.slice_in_dim(v, r * size, (r + 1) * size, axis=1 - self.axis)

        def part(self, k, l, r, of):
            mine = steps.begin(self.parts[k, 0, l])
            return self.cut(mine, r, of), self.cut(self.sums[k, l], r, of)

        def zh(self, l, r=0, of=2):
            value = plus(*self.part(ring - 1, l, r, of))
            for k in range(ring - 2, 0, -1):
                value = plus(move(pp_down, value), *self.part(k, l, r, of))
            self.value[l, r] = move(pp_down, value)

        def ready(self, r=0, of=2):
            def go(value):
                if self.whole:
                    total = plus(value, self.parts[0, 0, 0], self.got[0])
                    first, second = jnp.split(total, 2, axis=self.axis)
                else:
                    first, second = (
                        plus(v, self.cut(self.parts[0, 0, l], r, of), self.cut(self.got[l], r, of))
                        for l, v in enumerate((value, self.value[1, r]))
                    )
                return mine_of(first, second), mine_of(second, first)

            self.value[2, r], self.value[3, r] = run(go, self.value[0, r])

        def zl(self, r=0):
            self.value[3, r] = move(pp_zl, self.value[3, r])

        def result(self, of=2):
            mine = [self.value[2, r] for r in range(of)]
            other = [self.value[3, r] for r in range(of)]
            if of == 1:
                return mine[0], other[0]
            return tuple(jnp.concatenate(v, axis=1 - self.axis) for v in (mine, other))

    def finished(make):
        out = make()
        steps.pending.append(out)
        return out

    near_cot_b = gather(cz_top, cz_bottom, cd_top, cd_bottom)
    far_cot_b = move(pp_core, near_cot_b)
    down_g, up_g, out_g, qkv_g = Sum(1), Sum(0), Sum(1, True), Sum(0)
    down_w.zh(1, 1, 2)
    down_w.y(1)
    cot_a, cot_b = batch(near_cot_a, far_cot_a), batch(near_cot_b, far_cot_b)
    acts = [[(act_a, 0, 2 * two)], [(act_b, 0, 2 * two)]]
    down_g.make(1, acts, [cot_a, cot_b])
    close()
    down_w.yz(1)
    down_g.make(0, acts, [cot_a, cot_b])
    close()

    w_down, at_down = down_w.blocks()

    def pull(rows, slope):
        return deep(
            rows,
            w_down,
            at_down,
            1,
            finish=lambda total, s: (total * s.astype(F32),),
            extra=(slope,),
            cuts=1,
        )

    down_g.y_far(0)
    du_b = run(lambda v: pull(cot_b, v), slope_b)
    sums_b = run(broad, du_b, w_up, at_up, 1)
    close()

    ez, ed = core_sum(*sums_b)
    from_d = pp_x(ed)
    steps.pending += [ez, from_d]
    down_g.zh(0, 0)
    down_g.zh(0, 1)
    down_g.y_far(1)
    down_g.y_own(0)
    du_a = run(lambda v: pull(cot_a, v), slope_a)
    sums_a = run(broad, du_a, w_up, at_up, 1)
    close()

    e00, ex = core_sum(*sums_a)
    from_x = pp_x(ex)
    steps.pending += [e00, from_x]
    from_z = move(pp_zl, plus(steps.begin(ez), from_d))
    down_g.zh(1, 0)
    down_g.y_own(1)
    two_rows = [batch(*two_a), batch(*two_b)]
    dus = [[(du_a, 0, 2 * two)], [(du_b, 0, 2 * two)]]
    up_g.make(1, two_rows, dus)
    up_g.make(0, two_rows, dus)
    close()

    grad_in_two = steps.begin(e00).astype(F32) + from_x.astype(F32) + from_z.astype(F32)
    grad_part, grad_gain_two = norm_backward(grad_in_two, normed_two, inverse_two, gain_two)
    grad_resid = cot.astype(F32) + grad_part
    grad_rows = grad_resid.astype(BF)
    grad_far = move(pp_core, grad_rows)
    ax = move(pp_x, grad_rows)
    az = move(pp_zl, grad_rows)
    down_g.zh(1, 1)
    up_g.y_far(0)
    down_g.ready(0)
    out_b = run(broad, act_b, w_down, at_down, 0)
    out_a = run(broad, act_a, w_down, at_down, 0)
    close()

    ax_far = move(pp_core, ax)
    grad_a = (grad_rows, ax, grad_far, ax_far)
    ad = move(pp_x, az)
    up_g.zh(0, 0)
    up_g.y_far(1)
    down_g.zl(0)
    o_b = core_sum(*out_b)
    steps.pending += o_b
    dov_a = run(lambda v: deep(batch(*grad_a[:3], v), w_out, at_out, 1), ax_far)
    proj_a = attend_back(dov_a, qkv_a, start_a, lse_a)
    steps.pending.append(proj_a)
    close()

    az_far, ad_far = move(pp_core, az), move(pp_core, ad)
    grad_b = (az, ad, az_far, ad_far)
    up_g.zh(1, 0)
    up_g.y_own(0)
    oz, od = o_b
    from_od = move(pp_x, od)
    o_a = core_sum(*out_a)
    steps.pending += o_a
    down_g.ready(1)
    dov_b = run(lambda v: deep(batch(*grad_b[:3], v), w_out, at_out, 1), ad_far)
    proj_b = attend_back(dov_b, qkv_b, start_b, lse_b)
    steps.pending.append(proj_b)
    close()

    one_rows = [one_a_rows, one_b_rows]
    projs = [[(proj_a, 0, 2 * two)], [(proj_b, 0, 2 * two)]]
    o00, ox = o_a
    from_ox = move(pp_x, ox)
    from_oz = move(pp_zl, plus(steps.begin(oz), from_od))
    up_g.zh(0, 1)
    up_g.y_own(1)
    qkv_g.make(1, one_rows, projs)
    qkv_g.make(0, one_rows, projs)
    atts = [[(att_a, 0, 2 * two)], [(att_b, 0, 2 * two)]]
    grads = [batch(*grad_a), batch(*grad_b)]
    out_g.make(1, atts, grads)
    close()

    down_g.zl(1)
    qkv_g.y_far(0)
    up_g.zh(1, 1)
    sums_b = run(broad, proj_b, w_qkv, at_qkv, 1)
    out_g.y_far(0)
    up_g.ready(0)
    out_g.make(0, atts, grads)
    block_out = run(
        lambda v: from_rel(
            (resid + (v.astype(F32) + from_ox.astype(F32) + from_oz.astype(F32))).astype(BF)
        ),
        o00,
    )
    close()

    ez, ed = core_sum(*sums_b)
    from_d = pp_x(ed)
    steps.pending += [ez, from_d]
    qkv_g.zh(0, 0, 1)
    qkv_g.y_far(1)
    up_g.zl(0)
    up_g.ready(1)
    sums_a = run(broad, proj_a, w_qkv, at_qkv, 1)
    grad_down = finished(lambda: joined(steps.begin(down_g.result()[0]), down_g.result()[1], 0).astype(F32))
    close()

    e00, ex = core_sum(*sums_a)
    from_x = pp_x(ex)
    steps.pending += [e00, from_x]
    from_z = move(pp_zl, plus(steps.begin(ez), from_d))
    qkv_g.zh(1, 0, 1)
    qkv_g.y_own(0)
    qkv_g.y_own(1)
    close()

    out_g.y_own(0)
    out_g.zh(0, 0, 1)
    up_g.zl(1)
    qkv_g.ready(0, 1)
    qkv_g.value[3, 0] = pp_zl(qkv_g.value[3, 0])
    steps.pending.append(qkv_g.value[3, 0])
    grad_in_one = steps.begin(e00).astype(F32) + from_x.astype(F32) + from_z.astype(F32)
    grad_part, grad_gain_one = norm_backward(grad_in_one, normed_one, inverse_one, gain_one)
    grad_in = from_rel(grad_resid + grad_part)
    gain_grads = from_rel(jnp.stack([grad_gain_one, grad_gain_two]))
    for step in (pp_core, pp_x, pp_y):
        gain_grads = gain_grads + step(gain_grads)
    steps.pending += [grad_in, gain_grads]
    close()

    def parts_first(v):
        return v.reshape(unit, heads, 3, HEAD).transpose(0, 2, 1, 3).reshape(unit, 3, width)

    out_g.ready(0, 1)
    out_g.value[3, 0] = pp_zl(out_g.value[3, 0])
    grad_up = joined(steps.begin(up_g.result()[0]), up_g.result()[1], 1).astype(F32)
    mine, other = qkv_g.result(1)
    grad_qkv = finished(
        lambda: joined(parts_first(steps.begin(mine)), parts_first(other), 2).astype(F32)
    )
    gain_grads = steps.begin(gain_grads)
    gain_grads = gain_grads + pp_zl(gain_grads)
    moving = gain_grads
    for _ in range(ring - 1):
        moving = pp_up(moving)
        gain_grads = gain_grads + moving
    size = D // (n * tp)
    gain_grads = lax.dynamic_slice_in_dim(gain_grads, (f * tp + t) * size, size, axis=1)

    grad_out = joined(*out_g.result(1), 0).astype(F32)

    return (
        block_out,
        grad_in,
        gain_grads[0],
        gain_grads[1],
        grad_qkv,
        grad_out,
        grad_up,
        grad_down,
    )


def solution(mesh):
    return jax.shard_map(
        on_device,
        mesh=mesh,
        in_specs=(
            P(("fsdp", "tp"), None),
            P("fsdp", None),
            P("fsdp", None, "tp"),
            P("tp", "fsdp"),
            P("fsdp", "tp"),
            P("tp", "fsdp"),
            P("fsdp"),
            P("fsdp"),
            P(("fsdp", "tp"), None),
        ),
        out_specs=(
            P(("fsdp", "tp"), None),
            P(("fsdp", "tp"), None),
            P(("fsdp", "tp")),
            P(("fsdp", "tp")),
            P("fsdp", None, "tp"),
            P("tp", "fsdp"),
            P("fsdp", "tp"),
            P("tp", "fsdp"),
        ),
        check_vma=False,
    )
```

```python
import functools
import math

import jax
import jax.numpy as jnp
from jax import lax
from jax.experimental import pallas as pl
from jax.experimental.pallas import tpu as pltpu
from jax.sharding import PartitionSpec as P

D = 4096
H = 32
HEAD = D // H
REACH = 640
NORM_EPSILON = 1e-05
SQRT_HALF = 0.7071067811865476
INV_ROOT_TWO_PI = 0.3989422804014327
BF = jnp.bfloat16
F32 = jnp.float32
COVER = 0.05
VMEM = 56 << 20


def norm_forward(values_in):
    row_mean = jnp.mean(values_in, axis=-1, keepdims=True)
    centred = values_in - row_mean
    row_variance = jnp.mean(centred * centred, axis=-1, keepdims=True)
    inverse = lax.rsqrt(row_variance + NORM_EPSILON)
    return centred * inverse, inverse


def norm_backward(grad_out, normed, inverse, gain):
    grad_gain = jnp.sum(grad_out * normed, axis=0)
    scaled = grad_out * gain
    mean_one = jnp.mean(scaled, axis=-1, keepdims=True)
    mean_two = jnp.mean(scaled * normed, axis=-1, keepdims=True)
    return inverse * (scaled - mean_one - normed * mean_two), grad_gain


def gelu_and_slope(pre_act):
    part = 0.5 * (1.0 + lax.erf(pre_act * SQRT_HALF))
    slope = part + pre_act * jnp.exp(-0.5 * pre_act * pre_act) * INV_ROOT_TWO_PI
    return pre_act * part, slope


def dot(left, right, cl, cr):
    return lax.dot_general(left, right, (((cl,), (cr,)), ((), ())), preferred_element_type=F32)


class Steps:
    def __init__(self):
        self.token = jnp.zeros((1,), F32)
        self.pending = []
        self.first = True

    def begin(self, value):
        if self.first:
            return value
        return lax.optimization_barrier((value, self.token))[0]

    def move(self, how, value):
        out = how(self.begin(value))
        self.pending.append(out)
        return out

    def run(self, how, value, *more, **named):
        out = how(self.begin(value), *more, **named)
        self.pending += jax.tree.leaves(out)
        return out

    def close(self):
        self.token = lax.optimization_barrier((self.token, *self.pending))[0]
        self.pending = []
        self.first = False


def params(grid_dims):
    return pltpu.CompilerParams(
        dimension_semantics=("arbitrary",) * grid_dims, vmem_limit_bytes=VMEM
    )


def cost(m, n, k):
    return pl.CostEstimate(
        flops=int(2 * m * n * k * COVER), transcendentals=0, bytes_accessed=2 * (m * k + k * n + m * n)
    )


def tile(size, most):
    if size <= most:
        return size
    while size % most:
        most -= 128
    return most


def stack_rows(*pieces):
    rows = math.gcd(*(v.shape[0] for v in pieces))
    cols = pieces[0].shape[1]
    sizes = [v.shape[0] // rows for v in pieces]
    firsts = [sum(sizes[:i]) for i in range(len(pieces))]

    def body(*refs):
        step = pl.program_id(0)
        for ref, first, size in zip(refs, firsts, sizes):

            @pl.when((step >= first) & (step < first + size))
            def _(ref=ref):
                refs[-1][...] = ref[...]

    def spec(first, size):
        return pl.BlockSpec((rows, cols), lambda g: (jnp.clip(g - first, 0, size - 1), 0))

    return pl.pallas_call(
        body,
        out_shape=jax.ShapeDtypeStruct((sum(sizes) * rows, cols), pieces[0].dtype),
        grid=(sum(sizes),),
        in_specs=[spec(f, s) for f, s in zip(firsts, sizes)],
        out_specs=pl.BlockSpec((rows, cols), lambda g: (g, 0)),
        compiler_params=params(1),
        name="stack_rows",
    )(*pieces)


def gram(a_sides, b_sides, blocks, side):
    width = blocks[0][1]
    m = width if side == 0 else a_sides[0][0][0].shape[1]
    n = width if side == 1 else b_sides[0][0][0].shape[1]
    tm, tn = tile(m, 1024), tile(n, 1024)
    grid_m, grid_n = m // tm, n // tn
    count = len(blocks)
    per = grid_m * grid_n

    def at(g):
        p, r = g // per, g % per
        return p, r // grid_m, r % grid_m

    def a_spec(row, rows):
        def index_map(g, index):
            p, _, i = at(g)
            return row, (index[p] * grid_m + i if side == 0 else i)

        return pl.BlockSpec((rows, tm), index_map)

    def b_spec(row, rows):
        def index_map(g, index):
            p, j, _ = at(g)
            return row, (index[p] * grid_n + j if side == 1 else j)

        return pl.BlockSpec((rows, tn), index_map)

    def out_map(q):
        def at_q(g, index):
            r = jnp.clip(g - q * per, 0, per - 1)
            return r % grid_m, r // grid_m

        return at_q

    def body(index_ref, *refs):
        refs = list(refs)

        def take(batch):
            parts = [refs.pop(0)[...] for _ in batch]
            return parts[0] if len(parts) == 1 else jnp.concatenate(parts, axis=0)

        lefts = [take(batch) for batch in a_sides]
        rights = [take(batch) for batch in b_sides]
        total = None
        for left, right in zip(lefts, rights):
            part = dot(left, right, 0, 0)
            total = part if total is None else total + part
        total = total.astype(BF)
        p = pl.program_id(0) // per
        for q in range(count):

            @pl.when(p == q)
            def _(q=q):
                refs[q][...] = total

    flat_a = [piece for batch in a_sides for piece in batch]
    flat_b = [piece for batch in b_sides for piece in batch]
    depth = sum(piece[2] for piece in flat_a)
    return pl.pallas_call(
        body,
        out_shape=[jax.ShapeDtypeStruct((m, n), BF)] * count,
        grid_spec=pltpu.PrefetchScalarGridSpec(
            num_scalar_prefetch=1,
            grid=(count * per,),
            in_specs=[a_spec(row, rows) for _, row, rows in flat_a]
            + [b_spec(row, rows) for _, row, rows in flat_b],
            out_specs=[pl.BlockSpec((tm, tn), out_map(q)) for q in range(count)],
        ),
        compiler_params=params(1),
        cost_estimate=cost(m, n * count, depth),
        name="gram",
    )(
        jnp.array([b[0] for b in blocks], jnp.int32),
        *(piece[0] for piece in flat_a),
        *(piece[0] for piece in flat_b),
    )


def deep(pieces, blocks, starts, cr, finish=None, extra=(), outs=1, tn=512, cuts=1):
    sizes = [rows for _, _, rows in pieces]
    m, k = sum(sizes), pieces[0][0].shape[1]
    n = blocks[0].shape[1 - cr]
    count, heights = len(blocks), len(pieces)
    tn = tile(n, tn)
    work = []
    for i, rows in enumerate(sizes):
        for c in range(cuts):
            height = rows // cuts
            work.append((i, c * height, sum(sizes[:i]) + c * height, height))

    def body(starts_ref, *refs):
        a_refs, rest = refs[:heights], refs[heights:]

        def part(i, first, height):
            total = None
            for p in range(count):
                size = blocks[p].shape[cr]
                at = pl.multiple_of(starts_ref[p] * 128, 128)
                term = dot(a_refs[i][first : first + height, pl.ds(at, size)], rest[p][...], 1, cr)
                total = term if total is None else total + term
            return total

        def store(first, height, total):
            at = slice(first, first + height)
            values = (total,) if finish is None else finish(total, *(v[at, :] for v in rest[count:-outs]))
            for ref, value in zip(rest[-outs:], values):
                ref[at, :] = value.astype(BF)

        before = None
        for i, first, row, height in work:
            total = part(i, first, height)
            if before is not None:
                store(*before)
            before = (row, height, total)
        store(*before)

    def a_spec(row, rows):
        return pl.BlockSpec((rows, k), lambda j, *_: (row, 0), pipeline_mode=pl.Buffered(1))

    def w_spec(w):
        size = w.shape[cr]
        if cr == 0:
            return pl.BlockSpec((size, tn), lambda j, *_: (0, j))
        return pl.BlockSpec((tn, size), lambda j, *_: (j, 0))

    out = pl.BlockSpec((m, tn), lambda j, *_: (0, j))
    result = pl.pallas_call(
        body,
        out_shape=[jax.ShapeDtypeStruct((m, n), BF)] * outs,
        grid_spec=pltpu.PrefetchScalarGridSpec(
            num_scalar_prefetch=1,
            grid=(n // tn,),
            in_specs=[a_spec(row, rows) for _, row, rows in pieces]
            + [w_spec(w) for w in blocks]
            + [out] * len(extra),
            out_specs=[out] * outs,
        ),
        compiler_params=params(1),
        cost_estimate=cost(m, n, k),
        name="deep",
    )(starts, *(piece[0] for piece in pieces), *blocks, *extra)
    return result[0] if outs == 1 else result


def broad(a, blocks, starts, cr):
    m, k = a.shape
    n = sum(w.shape[1 - cr] for w in blocks)
    count = len(blocks)
    tm = tile(m // 2, 320)
    steps = m // 2 // tm

    def body(starts_ref, a_ref, *rest):
        for which in range(2):

            @pl.when(pl.program_id(0) // steps == which)
            def _(out=rest[count + which]):
                for p in range(count):
                    size = blocks[p].shape[1 - cr]
                    at = pl.multiple_of(starts_ref[p] * 128, 128)
                    out[:, pl.ds(at, size)] = dot(a_ref[...], rest[p][...], 1, cr).astype(BF)

    return pl.pallas_call(
        body,
        out_shape=[jax.ShapeDtypeStruct((m // 2, n), BF)] * 2,
        grid_spec=pltpu.PrefetchScalarGridSpec(
            num_scalar_prefetch=1,
            grid=(2 * steps,),
            in_specs=[pl.BlockSpec((tm, k), lambda i, *_: (i, 0))]
            + [pl.BlockSpec(w.shape, lambda i, *_: (0, 0), pipeline_mode=pl.Buffered(1)) for w in blocks],
            out_specs=[
                pl.BlockSpec((tm, n), lambda i, *_: (jnp.minimum(i, steps - 1), 0)),
                pl.BlockSpec((tm, n), lambda i, *_: (jnp.maximum(i - steps, 0), 0)),
            ],
        ),
        compiler_params=params(1),
        cost_estimate=cost(m, n, k),
        name="broad",
    )(starts, a, *blocks)


QB = 256


def window(first):
    low = max(0, first - REACH)
    return low, first + QB - low


def masked_scores(q, k, start, slope, first, low, width, scale):
    scores = dot(q, k, 1, 1)
    row = first + lax.broadcasted_iota(jnp.int32, (QB, width), 0)
    col = low + lax.broadcasted_iota(jnp.int32, (QB, width), 1)
    scores = scores * scale - slope * (row - col).astype(F32)
    return jnp.where((col >= start) & (col <= row), scores, -1e30)


def in_order(turn, visit):
    for i in range(4):
        rel = lax.bitwise_xor(jnp.int32(i), turn)
        visit(i, lax.bitwise_and(rel, 1), lax.shift_right_logical(rel, 1))


def attention_forward(turn_ref, slope_ref, qkv_ref, start_ref, o_ref, lse_ref, q_s, k_s, v_s, o_s):
    turn = turn_ref[0]
    slope = slope_ref[pl.program_id(0)]
    sequence = q_s.shape[0]
    piece = sequence // 4
    scale = 1.0 / math.sqrt(HEAD)

    def load(i, core, x):
        block = qkv_ref[core, x]
        for j, scratch in enumerate((q_s, k_s, v_s)):
            scratch[i * piece : (i + 1) * piece, :] = block[:, j * HEAD : (j + 1) * HEAD]

    in_order(turn, load)
    for first in range(0, sequence, QB):
        low, width = window(first)
        scores = masked_scores(
            q_s[first : first + QB, :],
            k_s[low : low + width, :],
            start_ref[first : first + QB, :],
            slope,
            first,
            low,
            width,
            scale,
        )
        peak = jnp.max(scores, axis=-1, keepdims=True)
        weights = jnp.exp(scores - peak)
        total = jnp.sum(weights, axis=-1, keepdims=True)
        lse_ref[0, first : first + QB, :] = peak + jnp.log(total)
        probs = (weights * (1.0 / total)).astype(BF)
        o_s[first : first + QB, :] = dot(probs, v_s[low : low + width, :], 1, 0).astype(BF)

    def store(i, core, x):
        o_ref[core, x] = o_s[i * piece : (i + 1) * piece, :]

    in_order(turn, store)


def attention_backward(
    turn_ref, slope_ref, qkv_ref, do_ref, start_ref, lse_ref, out_ref, q_s, k_s, v_s, do_s, dq_s, dk_s, dv_s
):
    turn = turn_ref[0]
    slope = slope_ref[pl.program_id(0)]
    sequence = q_s.shape[0]
    piece = sequence // 4
    scale = 1.0 / math.sqrt(HEAD)

    def load(i, core, x):
        rows = slice(i * piece, (i + 1) * piece)
        block = qkv_ref[core, x]
        for j, scratch in enumerate((q_s, k_s, v_s)):
            scratch[rows, :] = block[:, j * HEAD : (j + 1) * HEAD]
        do_s[rows, :] = do_ref[core, x]

    in_order(turn, load)
    dk_s[...] = jnp.zeros_like(dk_s)
    dv_s[...] = jnp.zeros_like(dv_s)
    for first in range(0, sequence, QB):
        low, width = window(first)
        keys = k_s[low : low + width, :]
        query = q_s[first : first + QB, :]
        grad = do_s[first : first + QB, :]
        scores = masked_scores(
            query, keys, start_ref[first : first + QB, :], slope, first, low, width, scale
        )
        probs = jnp.exp(scores - lse_ref[0, first : first + QB, :])
        grad_probs = dot(grad, v_s[low : low + width, :], 1, 1)
        delta = jnp.sum(probs * grad_probs, axis=-1, keepdims=True)
        grad_scores = (probs * (grad_probs - delta) * scale).astype(BF)
        dq_s[first : first + QB, :] = dot(grad_scores, keys, 1, 0).astype(BF)
        dk_s[low : low + width, :] += dot(grad_scores, query, 0, 0)
        dv_s[low : low + width, :] += dot(probs.astype(BF), grad, 0, 0)

    def store(i, core, x):
        rows = slice(i * piece, (i + 1) * piece)
        out_ref[core, x, :, 0:HEAD] = dq_s[rows, :]
        out_ref[core, x, :, HEAD : 2 * HEAD] = dk_s[rows, :].astype(BF)
        out_ref[core, x, :, 2 * HEAD : 3 * HEAD] = dv_s[rows, :].astype(BF)

    in_order(turn, store)


def on_device(
    hidden_in,
    segment_ids,
    qkv_weight,
    out_weight,
    up_weight,
    down_weight,
    norm1_gain,
    norm2_gain,
    out_cotangent,
):
    n = lax.axis_size("fsdp")
    tp = lax.axis_size("tp")
    ring = n // 4
    f = lax.axis_index("fsdp")
    t = lax.axis_index("tp")
    y, zl, zh = f & 1, (f >> 1) & 1, f >> 2
    low_half = zl == 0
    piece = hidden_in.shape[0]
    half = piece // 2
    sequence = piece * tp
    heads = H // tp // 2
    width = heads * HEAD
    unit = D // n
    pairs = [(k, j) for k in range(ring) for j in range(2)]
    far_first = range(ring - 1, -1, -1)
    steps = Steps()
    move, run, close = steps.move, steps.run, steps.close

    def over(axis, to, size):
        return lambda v: lax.ppermute(v, axis, [(i, to(i)) for i in range(size)])

    pp_core = over("tp", lambda i: i ^ 1, tp)
    pp_x = over("tp", lambda i: i ^ 2, tp)
    pp_zl = over("fsdp", lambda i: i ^ 2, n)
    pp_y = over("fsdp", lambda i: i ^ 1, n)
    pp_up = over("fsdp", lambda i: (i + 4) % n, n)
    pp_down = over("fsdp", lambda i: (i - 4) % n, n)

    def to_rel(v):
        cols = [v[..., b * unit : (b + 1) * unit] for b in range(n)]

        def pick(k, j, l):
            chosen = None
            for a in range(ring):
                both = jnp.where(y == j, cols[a * 4 + l * 2], cols[a * 4 + l * 2 + 1])
                chosen = both if chosen is None else jnp.where((zh - k) % ring == a, both, chosen)
            return chosen

        return jnp.concatenate([pick(k, j, l) for k, j in pairs for l in range(2)], axis=-1)

    def from_rel(v):
        cols = [v[..., b * unit : (b + 1) * unit] for b in range(n)]

        def pick(a, l, b):
            chosen = None
            for k in range(ring):
                both = jnp.where(y == b, cols[k * 4 + l], cols[k * 4 + 2 + l])
                chosen = both if chosen is None else jnp.where((zh - k) % ring == a, both, chosen)
            return chosen

        return jnp.concatenate(
            [pick(a, l, b) for a in range(ring) for l in range(2) for b in range(2)], axis=-1
        )

    def mine_of(first, second):
        return jnp.where(low_half, first, second)

    def joined(mine, other, axis):
        return jnp.concatenate(
            [jnp.where(low_half, mine, other), jnp.where(low_half, other, mine)], axis=axis
        )

    def plus(*terms):
        return sum(v.astype(F32) for v in terms).astype(BF)

    def ring_up(v):
        chain = [v]
        for _ in range(ring - 1):
            chain.append(pp_up(chain[-1]))
        return chain[1:]

    def cut_rows(v, c, of=2):
        size = v.shape[0] // of
        return v[c * size : (c + 1) * size]

    class Weight:
        def __init__(self, mine, other):
            self.have = {(0, 0, 0): mine}
            self.other = other
            self.chunks = {}

        def prepare(self, mine=1, other=1):
            first = self.have[0, 0, 0]
            if mine > 1:
                for c in range(mine):
                    self.chunks["mine", c] = run(lambda v, c=c: cut_rows(v, c, mine), first)
            if other > 1:
                for c in range(other):
                    self.chunks["other", c] = run(lambda v, c=c: cut_rows(v, c, other), self.other)

        def get(self, key):
            if isinstance(self.have[key], list):
                first, *rest = self.have[key]
                self.have[key] = stack_rows(steps.begin(first), *rest) if rest else first
            return self.have[key]

        def swap(self, c=0, of=1):
            got = move(pp_zl, self.chunks["other", c] if of > 1 else self.other)
            self.chunks["swap", c] = got
            if c == of - 1:
                self.have[0, 0, 1] = [self.chunks["swap", i] for i in range(of)]

        def zh(self, source, c=0, of=1):
            if source == 1 and of > 1 and ("other", c) in self.chunks:
                v = self.chunks["swap", c]
            elif source == 0 and of > 1:
                v = self.chunks["mine", c]
            elif of > 1:
                v = cut_rows(self.get((0, 0, source)), c, of)
            else:
                v = self.get((0, 0, source))
            self.chunks[source, c] = move(ring_up, v)
            if c == of - 1:
                for k in range(ring - 1):
                    self.have[k + 1, 0, source] = [self.chunks[source, i][k] for i in range(of)]

        def y(self, source):
            self.have[0, 1, source] = move(pp_y, self.get((0, 0, source)))

        def yz(self, source):
            for k in range(1, ring):
                self.have[k, 1, source] = move(pp_y, self.get((k, 0, source)))

        def blocks(self):
            found, starts = [], []
            for k, j in pairs:
                for source in range(2):
                    found.append(self.get((k, j, source)))
                    starts.append((2 * (2 * k + j) + (zl if source == 0 else 1 - zl)) * (unit // 128))
            return found, jnp.stack(starts).astype(jnp.int32)

    def halves(v, axis):
        lower, upper = jnp.split(v, 2, axis=axis)
        return mine_of(lower, upper), mine_of(upper, lower)

    gains = jnp.stack([norm1_gain, norm2_gain])
    gain_chain = [joined(gains, pp_zl(gains), 1)]
    gain_chain = jnp.concatenate(gain_chain + ring_up(gain_chain[0]), axis=0)
    qkv_heads = (
        qkv_weight.reshape(unit, 3, 2 * heads, HEAD)
        .transpose(0, 2, 1, 3)
        .reshape(unit, 2 * heads * 3 * HEAD)
    )
    qkv_w = Weight(*halves(qkv_heads, 1))
    out_mine, out_other = halves(out_weight, 0)
    other_ids = move(pp_zl, segment_ids)
    steps.pending += [gain_chain, qkv_w.have[0, 0, 0], qkv_w.other, out_other]
    close()

    gain_other = move(pp_y, gain_chain)
    gains = jnp.concatenate(
        [(gain_chain, gain_other)[j][2 * k : 2 * k + 2] for k, j in pairs], axis=1
    ).astype(F32)
    gain_one, gain_two = gains[0:1], gains[1:2]
    qkv_w.swap()
    qkv_w.y(0)
    qkv_w.zh(0)
    out_swapped = move(pp_zl, out_other)
    x = to_rel(steps.begin(hidden_in)).astype(F32)
    normed_one, inverse_one = norm_forward(x)
    a_one = (normed_one * gain_one).astype(BF)
    cot = to_rel(steps.begin(out_cotangent))
    steps.pending += [a_one, cot]
    close()

    qkv_w.zh(1)
    qkv_w.y(1)
    qkv_w.yz(0)
    az = move(pp_zl, a_one)
    ax = move(pp_x, a_one)
    out_block = run(lambda v: joined(v, out_swapped, 1), out_mine)

    def first_of(ids):
        return jnp.sum((ids < ids.reshape(sequence, 1)).astype(jnp.int32), axis=-1, keepdims=True)

    start_a, start_b = run(first_of, segment_ids), run(first_of, other_ids)
    up_w = Weight(*run(lambda v: halves(v, 1), up_weight))
    down_w = Weight(*run(lambda v: halves(v, 0), down_weight))
    up_w.prepare(mine=2, other=2)
    down_w.prepare(mine=2, other=2)
    close()

    def gather(v, *pieces):
        return run(lambda first, *rest: stack_rows(first, *rest), v, *pieces)

    one_a = gather(a_one, ax)
    qkv_w.yz(1)
    ad = move(pp_x, az)
    out_w = Weight(out_block, None)
    out_w.zh(0)
    one_a_far = move(pp_core, one_a)
    up_w.swap(0, 2)
    close()

    turn = jnp.full((1,), t, jnp.int32)
    head_index = t * 2 * heads + zl * heads + jnp.arange(heads)
    slopes = 2.0 ** (-8.0 * (head_index + 1).astype(F32) / H)
    two = 2 * piece

    def batch(*pieces):
        return [(v, 0, v.shape[0]) for v in pieces]

    w_qkv, at_qkv = qkv_w.blocks()
    one_b = (az, ad, move(pp_core, az), move(pp_core, ad))
    up_w.zh(0, 0, 2)
    out_w.y(0)
    out_w.yz(0)
    cx = move(pp_x, cot)
    cz_top = move(pp_zl, cot[:half])
    one_b_rows = batch(*one_b)
    one_a_rows = batch(one_a, one_a_far)
    qkv_a = run(lambda v: deep(batch(v, one_a_far), w_qkv, at_qkv, 0), one_a)
    qkv_b = run(lambda v: deep(batch(*one_b[:3], v), w_qkv, at_qkv, 0), one_b[3])
    close()

    def spec(cols):
        return pl.BlockSpec((2, 2, piece, cols), lambda h, *_: (0, 0, 0, h))

    start_spec = pl.BlockSpec((sequence, 1), lambda h, *_: (0, 0))
    lse_spec = pl.BlockSpec((1, sequence, 1), lambda h, *_: (h, 0, 0))
    block = pltpu.VMEM((sequence, HEAD), BF)
    wide = pltpu.VMEM((sequence, HEAD), F32)

    def attend(qkv, start):
        out, lse = pl.pallas_call(
            attention_forward,
            out_shape=(
                jax.ShapeDtypeStruct((2, 2, piece, width), BF),
                jax.ShapeDtypeStruct((heads, sequence, 1), F32),
            ),
            grid_spec=pltpu.PrefetchScalarGridSpec(
                num_scalar_prefetch=2,
                grid=(heads,),
                in_specs=[spec(3 * HEAD), start_spec],
                out_specs=[spec(HEAD), lse_spec],
                scratch_shapes=[block] * 4,
            ),
            compiler_params=params(1),
            cost_estimate=cost(sequence, sequence, 2 * heads * HEAD),
            name="attention_forward",
        )(turn, slopes, qkv.reshape(2, 2, piece, 3 * width), start)
        return out.reshape(sequence, width), lse

    def attend_back(grad, qkv, start, lse):
        out = pl.pallas_call(
            attention_backward,
            out_shape=jax.ShapeDtypeStruct((2, 2, piece, 3 * width), BF),
            grid_spec=pltpu.PrefetchScalarGridSpec(
                num_scalar_prefetch=2,
                grid=(heads,),
                in_specs=[spec(3 * HEAD), spec(HEAD), start_spec, lse_spec],
                out_specs=spec(3 * HEAD),
                scratch_shapes=[block] * 5 + [wide] * 2,
            ),
            compiler_params=params(1),
            cost_estimate=cost(sequence, sequence, 4 * heads * HEAD),
            name="attention_backward",
        )(
            turn,
            slopes,
            qkv.reshape(2, 2, piece, 3 * width),
            grad.reshape(2, 2, piece, width),
            start,
            lse,
        )
        return out.reshape(sequence, 3 * width)

    def core_sum(near, far):
        got = move(pp_core, far)
        near = steps.begin(near)
        return tuple(plus(near[i * piece : (i + 1) * piece], got[i * piece : (i + 1) * piece]) for i in range(2))

    w_out = [out_w.get((k, j, 0)) for k, j in pairs]
    at_out = jnp.arange(len(pairs), dtype=jnp.int32) * (2 * unit // 128)
    att_b, lse_b = run(attend, qkv_b, start_b)
    sums_b = run(broad, att_b, w_out, at_out, 0)
    up_w.zh(0, 1, 2)
    up_w.y(0)
    cz_bottom = move(pp_zl, cot[half:])
    cd_top = move(pp_x, cz_top)
    near_cot_a = gather(cot, cx)
    far_cot_a = pp_core(near_cot_a)
    steps.pending.append(far_cot_a)
    close()

    ez, ed = core_sum(*sums_b)
    from_d = pp_x(ed)
    steps.pending += [ez, from_d]
    up_w.zh(1, 0, 2)
    up_w.yz(0)
    up_w.swap(1, 2)
    att_a, lse_a = run(attend, qkv_a, start_a)
    sums_a = run(broad, att_a, w_out, at_out, 0)
    close()

    e00, ex = core_sum(*sums_a)
    from_x = pp_x(ex)
    steps.pending += [e00, from_x]
    from_z = move(pp_zl, plus(steps.begin(ez), from_d))
    up_w.zh(1, 1, 2)
    up_w.y(1)
    close()

    resid = x + (steps.begin(e00).astype(F32) + from_x.astype(F32) + from_z.astype(F32))
    normed_two, inverse_two = norm_forward(resid)
    a_two = (normed_two * gain_two).astype(BF)
    a_two_far = move(pp_core, a_two)
    ax = move(pp_x, a_two)
    az = move(pp_zl, a_two)
    down_w.zh(0, 0, 2)
    up_w.yz(1)
    close()

    w_up, at_up = up_w.blocks()

    def lift(*pieces):
        return deep(batch(*pieces), w_up, at_up, 0, finish=gelu_and_slope, outs=2)

    ax_far = move(pp_core, ax)
    ad = move(pp_x, az)
    two_a = (a_two, ax, a_two_far, ax_far)
    down_w.zh(0, 1, 2)
    down_w.y(0)
    down_w.swap(0, 2)
    act_a, slope_a = run(lambda v: lift(a_two, ax, a_two_far, v), ax_far)
    close()

    az_far, ad_far = move(pp_core, az), move(pp_core, ad)
    two_b = (az, ad, az_far, ad_far)
    down_w.yz(0)
    down_w.swap(1, 2)
    down_w.zh(1, 0, 2)
    cd_bottom = move(pp_x, cz_bottom)
    cot_b_most = gather(cz_top, cz_bottom, cd_top)
    act_b, slope_b = run(lambda v: lift(*two_b[:3], v), ad_far)
    close()

    class Sum:
        def __init__(self, axis, whole=False):
            self.whole = whole
            self.parts = {}
            self.got = {}
            self.sums = {}
            self.value = {}
            self.axis = axis

        def make(self, j, a_sides, b_sides):
            def go(first):
                (head, *others), *sides = a_sides
                head = (first, *head[1:])
                return gram([[head, *others], *sides], b_sides, blocks, self.axis)

            if self.whole:
                keys = [(k, j, 0) for k in far_first]
                blocks = [(2 * k + j, 2 * unit) for k, j, _ in keys]
            else:
                keys = [(k, j, l) for k in far_first for l in range(2)]
                blocks = [((2 * k + j) * 2 + l, unit) for k, j, l in keys]
            for key, v in zip(keys, run(go, a_sides[0][0][0])):
                self.parts[key] = v

        def y_far(self, l):
            for k in range(ring - 1, 0, -1):
                self.sums[k, l] = move(pp_y, self.parts[k, 1, l])

        def y_own(self, l):
            self.got[l] = move(pp_y, self.parts[0, 1, l])

        def cut(self, v, r, of):
            size = v.shape[1 - self.axis] // of
            return lax.slice_in_dim(v, r * size, (r + 1) * size, axis=1 - self.axis)

        def part(self, k, l, r, of):
            mine = steps.begin(self.parts[k, 0, l])
            return self.cut(mine, r, of), self.cut(self.sums[k, l], r, of)

        def zh(self, l, r=0, of=2):
            value = plus(*self.part(ring - 1, l, r, of))
            for k in range(ring - 2, 0, -1):
                value = plus(move(pp_down, value), *self.part(k, l, r, of))
            self.value[l, r] = move(pp_down, value)

        def ready(self, r=0, of=2):
            def go(value):
                if self.whole:
                    total = plus(value, self.parts[0, 0, 0], self.got[0])
                    first, second = jnp.split(total, 2, axis=self.axis)
                else:
                    first, second = (
                        plus(v, self.cut(self.parts[0, 0, l], r, of), self.cut(self.got[l], r, of))
                        for l, v in enumerate((value, self.value[1, r]))
                    )
                return mine_of(first, second), mine_of(second, first)

            self.value[2, r], self.value[3, r] = run(go, self.value[0, r])

        def zl(self, r=0):
            self.value[3, r] = move(pp_zl, self.value[3, r])

        def result(self, of=2):
            mine = [self.value[2, r] for r in range(of)]
            other = [self.value[3, r] for r in range(of)]
            if of == 1:
                return mine[0], other[0]
            return tuple(jnp.concatenate(v, axis=1 - self.axis) for v in (mine, other))

    def finished(make):
        out = make()
        steps.pending.append(out)
        return out

    cot_b_parts = (cot_b_most, cd_bottom, move(pp_core, cot_b_most), move(pp_core, cd_bottom))
    down_g, up_g, out_g, qkv_g = Sum(1), Sum(0), Sum(1, True), Sum(0)
    down_w.zh(1, 1, 2)
    down_w.y(1)
    cot_a, cot_b = batch(near_cot_a, far_cot_a), batch(*cot_b_parts)
    acts = [[(act_a, 0, 2 * two)], [(act_b, 0, 2 * two)]]
    down_g.make(1, acts, [cot_a, cot_b])
    close()
    down_w.yz(1)
    down_g.make(0, acts, [cot_a, cot_b])
    cot_b_near = gather(cot_b_parts[0], cot_b_parts[1])
    cot_b_far = gather(cot_b_parts[2], cot_b_parts[3])
    close()

    w_down, at_down = down_w.blocks()

    def pull(rows, slope):
        return deep(
            rows,
            w_down,
            at_down,
            1,
            finish=lambda total, s: (total * s.astype(F32),),
            extra=(slope,),
            cuts=1,
        )

    down_g.y_far(0)
    du_b = run(lambda v: pull(batch(cot_b_near, cot_b_far), v), slope_b)
    sums_b = run(broad, du_b, w_up, at_up, 1)
    close()

    ez, ed = core_sum(*sums_b)
    from_d = pp_x(ed)
    steps.pending += [ez, from_d]
    down_g.zh(0, 0)
    down_g.zh(0, 1)
    down_g.y_far(1)
    down_g.y_own(0)
    du_a = run(lambda v: pull(cot_a, v), slope_a)
    sums_a = run(broad, du_a, w_up, at_up, 1)
    close()

    e00, ex = core_sum(*sums_a)
    from_x = pp_x(ex)
    steps.pending += [e00, from_x]
    from_z = move(pp_zl, plus(steps.begin(ez), from_d))
    down_g.zh(1, 0)
    down_g.y_own(1)
    two_rows = [batch(*two_a), batch(*two_b)]
    dus = [[(du_a, 0, 2 * two)], [(du_b, 0, 2 * two)]]
    up_g.make(1, two_rows, dus)
    up_g.make(0, two_rows, dus)
    close()

    grad_in_two = steps.begin(e00).astype(F32) + from_x.astype(F32) + from_z.astype(F32)
    grad_part, grad_gain_two = norm_backward(grad_in_two, normed_two, inverse_two, gain_two)
    grad_resid = cot.astype(F32) + grad_part
    grad_rows = grad_resid.astype(BF)
    grad_far = move(pp_core, grad_rows)
    ax = move(pp_x, grad_rows)
    az = move(pp_zl, grad_rows)
    down_g.zh(1, 1)
    up_g.y_far(0)
    down_g.ready(0)
    out_b = run(broad, act_b, w_down, at_down, 0)
    out_a = run(broad, act_a, w_down, at_down, 0)
    close()

    ax_far = move(pp_core, ax)
    grad_a = (grad_rows, ax, grad_far, ax_far)
    ad = move(pp_x, az)
    up_g.zh(0, 0)
    up_g.y_far(1)
    down_g.zl(0)
    o_b = core_sum(*out_b)
    steps.pending += o_b
    dov_a = run(lambda v: deep(batch(*grad_a[:3], v), w_out, at_out, 1), ax_far)
    proj_a = attend_back(dov_a, qkv_a, start_a, lse_a)
    steps.pending.append(proj_a)
    close()

    az_far, ad_far = move(pp_core, az), move(pp_core, ad)
    grad_b = (az, ad, az_far, ad_far)
    up_g.zh(1, 0)
    up_g.y_own(0)
    oz, od = o_b
    from_od = move(pp_x, od)
    o_a = core_sum(*out_a)
    steps.pending += o_a
    down_g.ready(1)
    dov_b = run(lambda v: deep(batch(*grad_b[:3], v), w_out, at_out, 1), ad_far)
    proj_b = attend_back(dov_b, qkv_b, start_b, lse_b)
    steps.pending.append(proj_b)
    close()

    one_rows = [one_a_rows, one_b_rows]
    projs = [[(proj_a, 0, 2 * two)], [(proj_b, 0, 2 * two)]]
    o00, ox = o_a
    from_ox = move(pp_x, ox)
    from_oz = move(pp_zl, plus(steps.begin(oz), from_od))
    up_g.zh(0, 1)
    up_g.y_own(1)
    qkv_g.make(1, one_rows, projs)
    qkv_g.make(0, one_rows, projs)
    atts = [[(att_a, 0, 2 * two)], [(att_b, 0, 2 * two)]]
    grads = [batch(*grad_a), batch(*grad_b)]
    out_g.make(1, atts, grads)
    close()

    down_g.zl(1)
    qkv_g.y_far(0)
    up_g.zh(1, 1)
    sums_b = run(broad, proj_b, w_qkv, at_qkv, 1)
    out_g.y_far(0)
    up_g.ready(0)
    out_g.make(0, atts, grads)
    block_out = run(
        lambda v: from_rel(
            (resid + (v.astype(F32) + from_ox.astype(F32) + from_oz.astype(F32))).astype(BF)
        ),
        o00,
    )
    close()

    ez, ed = core_sum(*sums_b)
    from_d = pp_x(ed)
    steps.pending += [ez, from_d]
    qkv_g.zh(0, 0, 1)
    qkv_g.y_far(1)
    up_g.zl(0)
    up_g.ready(1)
    sums_a = run(broad, proj_a, w_qkv, at_qkv, 1)
    grad_down = finished(lambda: joined(steps.begin(down_g.result()[0]), down_g.result()[1], 0).astype(F32))
    close()

    e00, ex = core_sum(*sums_a)
    from_x = pp_x(ex)
    steps.pending += [e00, from_x]
    from_z = move(pp_zl, plus(steps.begin(ez), from_d))
    qkv_g.zh(1, 0, 1)
    qkv_g.y_own(0)
    qkv_g.y_own(1)
    close()

    out_g.y_own(0)
    out_g.zh(0, 0, 1)
    up_g.zl(1)
    qkv_g.ready(0, 1)
    qkv_g.value[3, 0] = pp_zl(qkv_g.value[3, 0])
    steps.pending.append(qkv_g.value[3, 0])
    grad_in_one = steps.begin(e00).astype(F32) + from_x.astype(F32) + from_z.astype(F32)
    grad_part, grad_gain_one = norm_backward(grad_in_one, normed_one, inverse_one, gain_one)
    grad_in = from_rel(grad_resid + grad_part)
    gain_grads = from_rel(jnp.stack([grad_gain_one, grad_gain_two]))
    for step in (pp_core, pp_x, pp_y):
        gain_grads = gain_grads + step(gain_grads)
    steps.pending += [grad_in, gain_grads]
    close()

    def parts_first(v):
        return v.reshape(unit, heads, 3, HEAD).transpose(0, 2, 1, 3).reshape(unit, 3, width)

    out_g.ready(0, 1)
    out_g.value[3, 0] = pp_zl(out_g.value[3, 0])
    grad_up = joined(steps.begin(up_g.result()[0]), up_g.result()[1], 1).astype(F32)
    mine, other = qkv_g.result(1)
    grad_qkv = finished(
        lambda: joined(parts_first(steps.begin(mine)), parts_first(other), 2).astype(F32)
    )
    gain_grads = steps.begin(gain_grads)
    gain_grads = gain_grads + pp_zl(gain_grads)
    moving = gain_grads
    for _ in range(ring - 1):
        moving = pp_up(moving)
        gain_grads = gain_grads + moving
    size = D // (n * tp)
    gain_grads = lax.dynamic_slice_in_dim(gain_grads, (f * tp + t) * size, size, axis=1)

    grad_out = joined(*out_g.result(1), 0).astype(F32)

    return (
        block_out,
        grad_in,
        gain_grads[0],
        gain_grads[1],
        grad_qkv,
        grad_out,
        grad_up,
        grad_down,
    )


def solution(mesh):
    return jax.shard_map(
        on_device,
        mesh=mesh,
        in_specs=(
            P(("fsdp", "tp"), None),
            P("fsdp", None),
            P("fsdp", None, "tp"),
            P("tp", "fsdp"),
            P("fsdp", "tp"),
            P("tp", "fsdp"),
            P("fsdp"),
            P("fsdp"),
            P(("fsdp", "tp"), None),
        ),
        out_specs=(
            P(("fsdp", "tp"), None),
            P(("fsdp", "tp"), None),
            P(("fsdp", "tp")),
            P(("fsdp", "tp")),
            P("fsdp", None, "tp"),
            P("tp", "fsdp"),
            P("fsdp", "tp"),
            P("tp", "fsdp"),
        ),
        check_vma=False,
    )
```

```python
import functools
import math

import jax
import jax.numpy as jnp
from jax import lax
from jax.experimental import pallas as pl
from jax.experimental.pallas import tpu as pltpu
from jax.sharding import PartitionSpec as P

D = 4096
H = 32
HEAD = D // H
REACH = 640
NORM_EPSILON = 1e-05
SQRT_HALF = 0.7071067811865476
INV_ROOT_TWO_PI = 0.3989422804014327
BF = jnp.bfloat16
F32 = jnp.float32
COVER = 0.05
VMEM = 56 << 20


def norm_forward(values_in):
    row_mean = jnp.mean(values_in, axis=-1, keepdims=True)
    centred = values_in - row_mean
    row_variance = jnp.mean(centred * centred, axis=-1, keepdims=True)
    inverse = lax.rsqrt(row_variance + NORM_EPSILON)
    return centred * inverse, inverse


def norm_backward(grad_out, normed, inverse, gain):
    grad_gain = jnp.sum(grad_out * normed, axis=0)
    scaled = grad_out * gain
    mean_one = jnp.mean(scaled, axis=-1, keepdims=True)
    mean_two = jnp.mean(scaled * normed, axis=-1, keepdims=True)
    return inverse * (scaled - mean_one - normed * mean_two), grad_gain


def gelu_and_slope(pre_act):
    part = 0.5 * (1.0 + lax.erf(pre_act * SQRT_HALF))
    slope = part + pre_act * jnp.exp(-0.5 * pre_act * pre_act) * INV_ROOT_TWO_PI
    return pre_act * part, slope


def dot(left, right, cl, cr):
    return lax.dot_general(left, right, (((cl,), (cr,)), ((), ())), preferred_element_type=F32)


class Steps:
    def __init__(self):
        self.token = jnp.zeros((1,), F32)
        self.pending = []
        self.first = True

    def begin(self, value):
        if self.first:
            return value
        return lax.optimization_barrier((value, self.token))[0]

    def move(self, how, value):
        out = how(self.begin(value))
        self.pending.append(out)
        return out

    def run(self, how, value, *more, **named):
        out = how(self.begin(value), *more, **named)
        self.pending += jax.tree.leaves(out)
        return out

    def close(self):
        self.token = lax.optimization_barrier((self.token, *self.pending))[0]
        self.pending = []
        self.first = False


def params(grid_dims):
    return pltpu.CompilerParams(
        dimension_semantics=("arbitrary",) * grid_dims, vmem_limit_bytes=VMEM
    )


def cost(m, n, k):
    return pl.CostEstimate(
        flops=int(2 * m * n * k * COVER), transcendentals=0, bytes_accessed=2 * (m * k + k * n + m * n)
    )


def tile(size, most):
    if size <= most:
        return size
    while size % most:
        most -= 128
    return most


def stack_rows(*pieces):
    rows = math.gcd(*(v.shape[0] for v in pieces))
    cols = pieces[0].shape[1]
    sizes = [v.shape[0] // rows for v in pieces]
    firsts = [sum(sizes[:i]) for i in range(len(pieces))]

    def body(*refs):
        step = pl.program_id(0)
        for ref, first, size in zip(refs, firsts, sizes):

            @pl.when((step >= first) & (step < first + size))
            def _(ref=ref):
                refs[-1][...] = ref[...]

    def spec(first, size):
        return pl.BlockSpec((rows, cols), lambda g: (jnp.clip(g - first, 0, size - 1), 0))

    return pl.pallas_call(
        body,
        out_shape=jax.ShapeDtypeStruct((sum(sizes) * rows, cols), pieces[0].dtype),
        grid=(sum(sizes),),
        in_specs=[spec(f, s) for f, s in zip(firsts, sizes)],
        out_specs=pl.BlockSpec((rows, cols), lambda g: (g, 0)),
        compiler_params=params(1),
        name="stack_rows",
    )(*pieces)


def gram(a_sides, b_sides, blocks, side):
    width = blocks[0][1]
    m = width if side == 0 else a_sides[0][0][0].shape[1]
    n = width if side == 1 else b_sides[0][0][0].shape[1]
    tm, tn = tile(m, 1024), tile(n, 1024)
    grid_m, grid_n = m // tm, n // tn
    count = len(blocks)
    per = grid_m * grid_n

    def at(g):
        p, r = g // per, g % per
        return p, r // grid_m, r % grid_m

    def a_spec(row, rows):
        def index_map(g, index):
            p, _, i = at(g)
            return row, (index[p] * grid_m + i if side == 0 else i)

        return pl.BlockSpec((rows, tm), index_map)

    def b_spec(row, rows):
        def index_map(g, index):
            p, j, _ = at(g)
            return row, (index[p] * grid_n + j if side == 1 else j)

        return pl.BlockSpec((rows, tn), index_map)

    def out_map(q):
        def at_q(g, index):
            r = jnp.clip(g - q * per, 0, per - 1)
            return r % grid_m, r // grid_m

        return at_q

    def body(index_ref, *refs):
        refs = list(refs)

        def take(batch):
            parts = [refs.pop(0)[...] for _ in batch]
            return parts[0] if len(parts) == 1 else jnp.concatenate(parts, axis=0)

        lefts = [take(batch) for batch in a_sides]
        rights = [take(batch) for batch in b_sides]
        total = None
        for left, right in zip(lefts, rights):
            part = dot(left, right, 0, 0)
            total = part if total is None else total + part
        total = total.astype(BF)
        p = pl.program_id(0) // per
        for q in range(count):

            @pl.when(p == q)
            def _(q=q):
                refs[q][...] = total

    flat_a = [piece for batch in a_sides for piece in batch]
    flat_b = [piece for batch in b_sides for piece in batch]
    depth = sum(piece[2] for piece in flat_a)
    return pl.pallas_call(
        body,
        out_shape=[jax.ShapeDtypeStruct((m, n), BF)] * count,
        grid_spec=pltpu.PrefetchScalarGridSpec(
            num_scalar_prefetch=1,
            grid=(count * per,),
            in_specs=[a_spec(row, rows) for _, row, rows in flat_a]
            + [b_spec(row, rows) for _, row, rows in flat_b],
            out_specs=[pl.BlockSpec((tm, tn), out_map(q)) for q in range(count)],
        ),
        compiler_params=params(1),
        cost_estimate=cost(m, n * count, depth),
        name="gram",
    )(
        jnp.array([b[0] for b in blocks], jnp.int32),
        *(piece[0] for piece in flat_a),
        *(piece[0] for piece in flat_b),
    )


def deep(pieces, blocks, starts, cr, finish=None, extra=(), outs=1, tn=512, cuts=1):
    sizes = [rows for _, _, rows in pieces]
    m, k = sum(sizes), pieces[0][0].shape[1]
    n = blocks[0].shape[1 - cr]
    count, heights = len(blocks), len(pieces)
    tn = tile(n, tn)
    work = []
    for i, rows in enumerate(sizes):
        for c in range(cuts):
            height = rows // cuts
            work.append((i, c * height, sum(sizes[:i]) + c * height, height))

    def body(starts_ref, *refs):
        a_refs, rest = refs[:heights], refs[heights:]

        def part(i, first, height):
            total = None
            for p in range(count):
                size = blocks[p].shape[cr]
                at = pl.multiple_of(starts_ref[p] * 128, 128)
                term = dot(a_refs[i][first : first + height, pl.ds(at, size)], rest[p][...], 1, cr)
                total = term if total is None else total + term
            return total

        def store(first, height, total):
            at = slice(first, first + height)
            values = (total,) if finish is None else finish(total, *(v[at, :] for v in rest[count:-outs]))
            for ref, value in zip(rest[-outs:], values):
                ref[at, :] = value.astype(BF)

        before = None
        for i, first, row, height in work:
            total = part(i, first, height)
            if before is not None:
                store(*before)
            before = (row, height, total)
        store(*before)

    def a_spec(row, rows):
        return pl.BlockSpec((rows, k), lambda j, *_: (row, 0), pipeline_mode=pl.Buffered(1))

    def w_spec(w):
        size = w.shape[cr]
        if cr == 0:
            return pl.BlockSpec((size, tn), lambda j, *_: (0, j))
        return pl.BlockSpec((tn, size), lambda j, *_: (j, 0))

    out = pl.BlockSpec((m, tn), lambda j, *_: (0, j))
    result = pl.pallas_call(
        body,
        out_shape=[jax.ShapeDtypeStruct((m, n), BF)] * outs,
        grid_spec=pltpu.PrefetchScalarGridSpec(
            num_scalar_prefetch=1,
            grid=(n // tn,),
            in_specs=[a_spec(row, rows) for _, row, rows in pieces]
            + [w_spec(w) for w in blocks]
            + [out] * len(extra),
            out_specs=[out] * outs,
        ),
        compiler_params=params(1),
        cost_estimate=cost(m, n, k),
        name="deep",
    )(starts, *(piece[0] for piece in pieces), *blocks, *extra)
    return result[0] if outs == 1 else result


def broad(a, blocks, starts, cr):
    m, k = a.shape
    n = sum(w.shape[1 - cr] for w in blocks)
    count = len(blocks)
    tm = tile(m // 2, 320)
    steps = m // 2 // tm

    def body(starts_ref, a_ref, *rest):
        for which in range(2):

            @pl.when(pl.program_id(0) // steps == which)
            def _(out=rest[count + which]):
                for p in range(count):
                    size = blocks[p].shape[1 - cr]
                    at = pl.multiple_of(starts_ref[p] * 128, 128)
                    out[:, pl.ds(at, size)] = dot(a_ref[...], rest[p][...], 1, cr).astype(BF)

    return pl.pallas_call(
        body,
        out_shape=[jax.ShapeDtypeStruct((m // 2, n), BF)] * 2,
        grid_spec=pltpu.PrefetchScalarGridSpec(
            num_scalar_prefetch=1,
            grid=(2 * steps,),
            in_specs=[pl.BlockSpec((tm, k), lambda i, *_: (i, 0))]
            + [pl.BlockSpec(w.shape, lambda i, *_: (0, 0), pipeline_mode=pl.Buffered(1)) for w in blocks],
            out_specs=[
                pl.BlockSpec((tm, n), lambda i, *_: (jnp.minimum(i, steps - 1), 0)),
                pl.BlockSpec((tm, n), lambda i, *_: (jnp.maximum(i - steps, 0), 0)),
            ],
        ),
        compiler_params=params(1),
        cost_estimate=cost(m, n, k),
        name="broad",
    )(starts, a, *blocks)


QB = 256


def window(first):
    low = max(0, first - REACH)
    return low, first + QB - low


def masked_scores(q, k, start, slope, first, low, width, scale):
    scores = dot(q, k, 1, 1)
    row = first + lax.broadcasted_iota(jnp.int32, (QB, width), 0)
    col = low + lax.broadcasted_iota(jnp.int32, (QB, width), 1)
    scores = scores * scale - slope * (row - col).astype(F32)
    return jnp.where((col >= start) & (col <= row), scores, -1e30)


def in_order(turn, visit):
    for i in range(4):
        rel = lax.bitwise_xor(jnp.int32(i), turn)
        visit(i, lax.bitwise_and(rel, 1), lax.shift_right_logical(rel, 1))


def attention_forward(turn_ref, slope_ref, qkv_ref, start_ref, o_ref, lse_ref, q_s, k_s, v_s, o_s):
    turn = turn_ref[0]
    slope = slope_ref[pl.program_id(0)]
    sequence = q_s.shape[0]
    piece = sequence // 4
    scale = 1.0 / math.sqrt(HEAD)

    def load(i, core, x):
        block = qkv_ref[core, x]
        for j, scratch in enumerate((q_s, k_s, v_s)):
            scratch[i * piece : (i + 1) * piece, :] = block[:, j * HEAD : (j + 1) * HEAD]

    in_order(turn, load)
    for first in range(0, sequence, QB):
        low, width = window(first)
        scores = masked_scores(
            q_s[first : first + QB, :],
            k_s[low : low + width, :],
            start_ref[first : first + QB, :],
            slope,
            first,
            low,
            width,
            scale,
        )
        peak = jnp.max(scores, axis=-1, keepdims=True)
        weights = jnp.exp(scores - peak)
        total = jnp.sum(weights, axis=-1, keepdims=True)
        lse_ref[0, first : first + QB, :] = peak + jnp.log(total)
        probs = (weights * (1.0 / total)).astype(BF)
        o_s[first : first + QB, :] = dot(probs, v_s[low : low + width, :], 1, 0).astype(BF)

    def store(i, core, x):
        o_ref[core, x] = o_s[i * piece : (i + 1) * piece, :]

    in_order(turn, store)


def attention_backward(
    turn_ref, slope_ref, qkv_ref, do_ref, start_ref, lse_ref, out_ref, q_s, k_s, v_s, do_s, dq_s, dk_s, dv_s
):
    turn = turn_ref[0]
    slope = slope_ref[pl.program_id(0)]
    sequence = q_s.shape[0]
    piece = sequence // 4
    scale = 1.0 / math.sqrt(HEAD)

    def load(i, core, x):
        rows = slice(i * piece, (i + 1) * piece)
        block = qkv_ref[core, x]
        for j, scratch in enumerate((q_s, k_s, v_s)):
            scratch[rows, :] = block[:, j * HEAD : (j + 1) * HEAD]
        do_s[rows, :] = do_ref[core, x]

    in_order(turn, load)
    dk_s[...] = jnp.zeros_like(dk_s)
    dv_s[...] = jnp.zeros_like(dv_s)
    for first in range(0, sequence, QB):
        low, width = window(first)
        keys = k_s[low : low + width, :]
        query = q_s[first : first + QB, :]
        grad = do_s[first : first + QB, :]
        scores = masked_scores(
            query, keys, start_ref[first : first + QB, :], slope, first, low, width, scale
        )
        probs = jnp.exp(scores - lse_ref[0, first : first + QB, :])
        grad_probs = dot(grad, v_s[low : low + width, :], 1, 1)
        delta = jnp.sum(probs * grad_probs, axis=-1, keepdims=True)
        grad_scores = (probs * (grad_probs - delta) * scale).astype(BF)
        dq_s[first : first + QB, :] = dot(grad_scores, keys, 1, 0).astype(BF)
        dk_s[low : low + width, :] += dot(grad_scores, query, 0, 0)
        dv_s[low : low + width, :] += dot(probs.astype(BF), grad, 0, 0)

    def store(i, core, x):
        rows = slice(i * piece, (i + 1) * piece)
        out_ref[core, x, :, 0:HEAD] = dq_s[rows, :]
        out_ref[core, x, :, HEAD : 2 * HEAD] = dk_s[rows, :].astype(BF)
        out_ref[core, x, :, 2 * HEAD : 3 * HEAD] = dv_s[rows, :].astype(BF)

    in_order(turn, store)


def on_device(
    hidden_in,
    segment_ids,
    qkv_weight,
    out_weight,
    up_weight,
    down_weight,
    norm1_gain,
    norm2_gain,
    out_cotangent,
):
    n = lax.axis_size("fsdp")
    tp = lax.axis_size("tp")
    ring = n // 4
    f = lax.axis_index("fsdp")
    t = lax.axis_index("tp")
    y, zl, zh = f & 1, (f >> 1) & 1, f >> 2
    low_half = zl == 0
    piece = hidden_in.shape[0]
    half = piece // 2
    sequence = piece * tp
    heads = H // tp // 2
    width = heads * HEAD
    unit = D // n
    pairs = [(k, j) for k in range(ring) for j in range(2)]
    far_first = range(ring - 1, -1, -1)
    steps = Steps()
    move, run, close = steps.move, steps.run, steps.close

    def over(axis, to, size):
        return lambda v: lax.ppermute(v, axis, [(i, to(i)) for i in range(size)])

    pp_core = over("tp", lambda i: i ^ 1, tp)
    pp_x = over("tp", lambda i: i ^ 2, tp)
    pp_zl = over("fsdp", lambda i: i ^ 2, n)
    pp_y = over("fsdp", lambda i: i ^ 1, n)
    pp_up = over("fsdp", lambda i: (i + 4) % n, n)
    pp_down = over("fsdp", lambda i: (i - 4) % n, n)

    def to_rel(v):
        cols = [v[..., b * unit : (b + 1) * unit] for b in range(n)]

        def pick(k, j, l):
            chosen = None
            for a in range(ring):
                both = jnp.where(y == j, cols[a * 4 + l * 2], cols[a * 4 + l * 2 + 1])
                chosen = both if chosen is None else jnp.where((zh - k) % ring == a, both, chosen)
            return chosen

        return jnp.concatenate([pick(k, j, l) for k, j in pairs for l in range(2)], axis=-1)

    def from_rel(v):
        cols = [v[..., b * unit : (b + 1) * unit] for b in range(n)]

        def pick(a, l, b):
            chosen = None
            for k in range(ring):
                both = jnp.where(y == b, cols[k * 4 + l], cols[k * 4 + 2 + l])
                chosen = both if chosen is None else jnp.where((zh - k) % ring == a, both, chosen)
            return chosen

        return jnp.concatenate(
            [pick(a, l, b) for a in range(ring) for l in range(2) for b in range(2)], axis=-1
        )

    def mine_of(first, second):
        return jnp.where(low_half, first, second)

    def joined(mine, other, axis):
        return jnp.concatenate(
            [jnp.where(low_half, mine, other), jnp.where(low_half, other, mine)], axis=axis
        )

    def plus(*terms):
        return sum(v.astype(F32) for v in terms).astype(BF)

    def ring_up(v):
        chain = [v]
        for _ in range(ring - 1):
            chain.append(pp_up(chain[-1]))
        return chain[1:]

    def cut_rows(v, c, of=2):
        size = v.shape[0] // of
        return v[c * size : (c + 1) * size]

    class Weight:
        def __init__(self, mine, other):
            self.have = {(0, 0, 0): mine}
            self.other = other
            self.chunks = {}

        def prepare(self, mine=1, other=1):
            first = self.have[0, 0, 0]
            if mine > 1:
                for c in range(mine):
                    self.chunks["mine", c] = run(lambda v, c=c: cut_rows(v, c, mine), first)
            if other > 1:
                for c in range(other):
                    self.chunks["other", c] = run(lambda v, c=c: cut_rows(v, c, other), self.other)

        def get(self, key):
            if isinstance(self.have[key], list):
                first, *rest = self.have[key]
                self.have[key] = stack_rows(steps.begin(first), *rest) if rest else first
            return self.have[key]

        def swap(self, c=0, of=1):
            got = move(pp_zl, self.chunks["other", c] if of > 1 else self.other)
            self.chunks["swap", c] = got
            if c == of - 1:
                self.have[0, 0, 1] = [self.chunks["swap", i] for i in range(of)]

        def zh(self, source, c=0, of=1):
            if source == 1 and of > 1 and ("other", c) in self.chunks:
                v = self.chunks["swap", c]
            elif source == 0 and of > 1:
                v = self.chunks["mine", c]
            elif of > 1:
                v = cut_rows(self.get((0, 0, source)), c, of)
            else:
                v = self.get((0, 0, source))
            self.chunks[source, c] = move(ring_up, v)
            if c == of - 1:
                for k in range(ring - 1):
                    self.have[k + 1, 0, source] = [self.chunks[source, i][k] for i in range(of)]

        def y(self, source):
            self.have[0, 1, source] = move(pp_y, self.get((0, 0, source)))

        def yz(self, source):
            for k in range(1, ring):
                self.have[k, 1, source] = move(pp_y, self.get((k, 0, source)))

        def blocks(self):
            found, starts = [], []
            for k, j in pairs:
                for source in range(2):
                    found.append(self.get((k, j, source)))
                    starts.append((2 * (2 * k + j) + (zl if source == 0 else 1 - zl)) * (unit // 128))
            return found, jnp.stack(starts).astype(jnp.int32)

    def halves(v, axis):
        lower, upper = jnp.split(v, 2, axis=axis)
        return mine_of(lower, upper), mine_of(upper, lower)

    gains = jnp.stack([norm1_gain, norm2_gain])
    gain_chain = [joined(gains, pp_zl(gains), 1)]
    gain_chain = jnp.concatenate(gain_chain + ring_up(gain_chain[0]), axis=0)
    qkv_heads = (
        qkv_weight.reshape(unit, 3, 2 * heads, HEAD)
        .transpose(0, 2, 1, 3)
        .reshape(unit, 2 * heads * 3 * HEAD)
    )
    qkv_w = Weight(*halves(qkv_heads, 1))
    out_mine, out_other = halves(out_weight, 0)
    other_ids = move(pp_zl, segment_ids)
    steps.pending += [gain_chain, qkv_w.have[0, 0, 0], qkv_w.other, out_other]
    close()

    gain_other = move(pp_y, gain_chain)
    gains = jnp.concatenate(
        [(gain_chain, gain_other)[j][2 * k : 2 * k + 2] for k, j in pairs], axis=1
    ).astype(F32)
    gain_one, gain_two = gains[0:1], gains[1:2]
    qkv_w.swap()
    qkv_w.y(0)
    qkv_w.zh(0)
    out_swapped = move(pp_zl, out_other)
    x = to_rel(steps.begin(hidden_in)).astype(F32)
    normed_one, inverse_one = norm_forward(x)
    a_one = (normed_one * gain_one).astype(BF)
    cot = to_rel(steps.begin(out_cotangent))
    steps.pending += [a_one, cot]
    close()

    qkv_w.zh(1)
    qkv_w.y(1)
    qkv_w.yz(0)
    az = move(pp_zl, a_one)
    ax = move(pp_x, a_one)
    out_block = run(lambda v: joined(v, out_swapped, 1), out_mine)

    def first_of(ids):
        return jnp.sum((ids < ids.reshape(sequence, 1)).astype(jnp.int32), axis=-1, keepdims=True)

    start_a, start_b = run(first_of, segment_ids), run(first_of, other_ids)
    up_w = Weight(*run(lambda v: halves(v, 1), up_weight))
    down_w = Weight(*run(lambda v: halves(v, 0), down_weight))
    up_w.prepare(mine=2, other=2)
    down_w.prepare(mine=2, other=2)
    close()

    def gather(v, *pieces):
        return run(lambda first, *rest: stack_rows(first, *rest), v, *pieces)

    one_a = gather(a_one, ax)
    qkv_w.yz(1)
    ad = move(pp_x, az)
    out_w = Weight(out_block, None)
    out_w.zh(0)
    one_a_far = move(pp_core, one_a)
    up_w.swap(0, 2)
    close()

    turn = jnp.full((1,), t, jnp.int32)
    head_index = t * 2 * heads + zl * heads + jnp.arange(heads)
    slopes = 2.0 ** (-8.0 * (head_index + 1).astype(F32) / H)
    two = 2 * piece

    def batch(*pieces):
        return [(v, 0, v.shape[0]) for v in pieces]

    w_qkv, at_qkv = qkv_w.blocks()
    one_b = (az, ad, move(pp_core, az), move(pp_core, ad))
    up_w.zh(0, 0, 2)
    out_w.y(0)
    out_w.yz(0)
    cx = move(pp_x, cot)
    cz_top = move(pp_zl, cot[:half])
    one_b_rows = batch(*one_b)
    one_a_rows = batch(one_a, one_a_far)
    qkv_a = run(lambda v: deep(batch(v, one_a_far), w_qkv, at_qkv, 0), one_a)
    qkv_b = run(lambda v: deep(batch(*one_b[:3], v), w_qkv, at_qkv, 0), one_b[3])
    close()

    def spec(cols):
        return pl.BlockSpec((2, 2, piece, cols), lambda h, *_: (0, 0, 0, h))

    start_spec = pl.BlockSpec((sequence, 1), lambda h, *_: (0, 0))
    lse_spec = pl.BlockSpec((1, sequence, 1), lambda h, *_: (h, 0, 0))
    block = pltpu.VMEM((sequence, HEAD), BF)
    wide = pltpu.VMEM((sequence, HEAD), F32)

    def attend(qkv, start):
        out, lse = pl.pallas_call(
            attention_forward,
            out_shape=(
                jax.ShapeDtypeStruct((2, 2, piece, width), BF),
                jax.ShapeDtypeStruct((heads, sequence, 1), F32),
            ),
            grid_spec=pltpu.PrefetchScalarGridSpec(
                num_scalar_prefetch=2,
                grid=(heads,),
                in_specs=[spec(3 * HEAD), start_spec],
                out_specs=[spec(HEAD), lse_spec],
                scratch_shapes=[block] * 4,
            ),
            compiler_params=params(1),
            cost_estimate=cost(sequence, sequence, 2 * heads * HEAD),
            name="attention_forward",
        )(turn, slopes, qkv.reshape(2, 2, piece, 3 * width), start)
        return out.reshape(sequence, width), lse

    def attend_back(grad, qkv, start, lse):
        out = pl.pallas_call(
            attention_backward,
            out_shape=jax.ShapeDtypeStruct((2, 2, piece, 3 * width), BF),
            grid_spec=pltpu.PrefetchScalarGridSpec(
                num_scalar_prefetch=2,
                grid=(heads,),
                in_specs=[spec(3 * HEAD), spec(HEAD), start_spec, lse_spec],
                out_specs=spec(3 * HEAD),
                scratch_shapes=[block] * 5 + [wide] * 2,
            ),
            compiler_params=params(1),
            cost_estimate=cost(sequence, sequence, 4 * heads * HEAD),
            name="attention_backward",
        )(
            turn,
            slopes,
            qkv.reshape(2, 2, piece, 3 * width),
            grad.reshape(2, 2, piece, width),
            start,
            lse,
        )
        return out.reshape(sequence, 3 * width)

    def core_sum(near, far):
        got = move(pp_core, far)
        near = steps.begin(near)
        return tuple(plus(near[i * piece : (i + 1) * piece], got[i * piece : (i + 1) * piece]) for i in range(2))

    w_out = [out_w.get((k, j, 0)) for k, j in pairs]
    at_out = jnp.arange(len(pairs), dtype=jnp.int32) * (2 * unit // 128)
    att_b, lse_b = run(attend, qkv_b, start_b)
    sums_b = run(broad, att_b, w_out, at_out, 0)
    up_w.zh(0, 1, 2)
    up_w.y(0)
    cz_bottom = move(pp_zl, cot[half:])
    cd_top = move(pp_x, cz_top)
    close()

    ez, ed = core_sum(*sums_b)
    from_d = pp_x(ed)
    steps.pending += [ez, from_d]
    up_w.zh(1, 0, 2)
    up_w.yz(0)
    up_w.swap(1, 2)
    att_a, lse_a = run(attend, qkv_a, start_a)
    sums_a = run(broad, att_a, w_out, at_out, 0)
    close()

    e00, ex = core_sum(*sums_a)
    from_x = pp_x(ex)
    steps.pending += [e00, from_x]
    from_z = move(pp_zl, plus(steps.begin(ez), from_d))
    up_w.zh(1, 1, 2)
    up_w.y(1)
    near_cot_a = gather(cot, cx)
    close()

    resid = x + (steps.begin(e00).astype(F32) + from_x.astype(F32) + from_z.astype(F32))
    normed_two, inverse_two = norm_forward(resid)
    a_two = (normed_two * gain_two).astype(BF)
    a_two_far = move(pp_core, a_two)
    ax = move(pp_x, a_two)
    az = move(pp_zl, a_two)
    down_w.zh(0, 0, 2)
    up_w.yz(1)
    close()

    w_up, at_up = up_w.blocks()

    def lift(*pieces):
        return deep(batch(*pieces), w_up, at_up, 0, finish=gelu_and_slope, outs=2)

    ax_far = move(pp_core, ax)
    ad = move(pp_x, az)
    two_a = (a_two, ax, a_two_far, ax_far)
    down_w.zh(0, 1, 2)
    down_w.y(0)
    down_w.swap(0, 2)
    far_cot_a = move(pp_core, near_cot_a)
    act_a, slope_a = run(lambda v: lift(a_two, ax, a_two_far, v), ax_far)
    close()

    az_far, ad_far = move(pp_core, az), move(pp_core, ad)
    two_b = (az, ad, az_far, ad_far)
    down_w.yz(0)
    down_w.swap(1, 2)
    down_w.zh(1, 0, 2)
    cd_bottom = move(pp_x, cz_bottom)
    cot_b_most = gather(cz_top, cz_bottom, cd_top)
    act_b, slope_b = run(lambda v: lift(*two_b[:3], v), ad_far)
    close()

    class Sum:
        def __init__(self, axis, whole=False):
            self.whole = whole
            self.parts = {}
            self.got = {}
            self.sums = {}
            self.value = {}
            self.axis = axis

        def make(self, j, a_sides, b_sides):
            def go(first):
                (head, *others), *sides = a_sides
                head = (first, *head[1:])
                return gram([[head, *others], *sides], b_sides, blocks, self.axis)

            if self.whole:
                keys = [(k, j, 0) for k in far_first]
                blocks = [(2 * k + j, 2 * unit) for k, j, _ in keys]
            else:
                keys = [(k, j, l) for k in far_first for l in range(2)]
                blocks = [((2 * k + j) * 2 + l, unit) for k, j, l in keys]
            for key, v in zip(keys, run(go, a_sides[0][0][0])):
                self.parts[key] = v

        def y_far(self, l):
            for k in range(ring - 1, 0, -1):
                self.sums[k, l] = move(pp_y, self.parts[k, 1, l])

        def y_own(self, l):
            self.got[l] = move(pp_y, self.parts[0, 1, l])

        def cut(self, v, r, of):
            size = v.shape[1 - self.axis] // of
            return lax.slice_in_dim(v, r * size, (r + 1) * size, axis=1 - self.axis)

        def part(self, k, l, r, of):
            mine = steps.begin(self.parts[k, 0, l])
            return self.cut(mine, r, of), self.cut(self.sums[k, l], r, of)

        def zh(self, l, r=0, of=2):
            value = plus(*self.part(ring - 1, l, r, of))
            for k in range(ring - 2, 0, -1):
                value = plus(move(pp_down, value), *self.part(k, l, r, of))
            self.value[l, r] = move(pp_down, value)

        def ready(self, r=0, of=2):
            def go(value):
                if self.whole:
                    total = plus(value, self.parts[0, 0, 0], self.got[0])
                    first, second = jnp.split(total, 2, axis=self.axis)
                else:
                    first, second = (
                        plus(v, self.cut(self.parts[0, 0, l], r, of), self.cut(self.got[l], r, of))
                        for l, v in enumerate((value, self.value[1, r]))
                    )
                return mine_of(first, second), mine_of(second, first)

            self.value[2, r], self.value[3, r] = run(go, self.value[0, r])

        def zl(self, r=0):
            self.value[3, r] = move(pp_zl, self.value[3, r])

        def result(self, of=2):
            mine = [self.value[2, r] for r in range(of)]
            other = [self.value[3, r] for r in range(of)]
            if of == 1:
                return mine[0], other[0]
            return tuple(jnp.concatenate(v, axis=1 - self.axis) for v in (mine, other))

    def finished(make):
        out = make()
        steps.pending.append(out)
        return out

    cot_b_parts = (cot_b_most, cd_bottom, move(pp_core, cot_b_most), move(pp_core, cd_bottom))
    down_g, up_g, out_g, qkv_g = Sum(1), Sum(0), Sum(1, True), Sum(0)
    down_w.zh(1, 1, 2)
    down_w.y(1)
    cot_a, cot_b = batch(near_cot_a, far_cot_a), batch(*cot_b_parts)
    acts = [[(act_a, 0, 2 * two)], [(act_b, 0, 2 * two)]]
    down_g.make(1, acts, [cot_a, cot_b])
    close()
    down_w.yz(1)
    down_g.make(0, acts, [cot_a, cot_b])
    cot_b_near = gather(cot_b_parts[0], cot_b_parts[1])
    cot_b_far = gather(cot_b_parts[2], cot_b_parts[3])
    close()

    w_down, at_down = down_w.blocks()

    def pull(rows, slope):
        return deep(
            rows,
            w_down,
            at_down,
            1,
            finish=lambda total, s: (total * s.astype(F32),),
            extra=(slope,),
            cuts=1,
        )

    down_g.y_far(0)
    du_b = run(lambda v: pull(batch(cot_b_near, cot_b_far), v), slope_b)
    sums_b = run(broad, du_b, w_up, at_up, 1)
    close()

    ez, ed = core_sum(*sums_b)
    from_d = pp_x(ed)
    steps.pending += [ez, from_d]
    down_g.zh(0, 0)
    down_g.zh(0, 1)
    down_g.y_far(1)
    down_g.y_own(0)
    du_a = run(lambda v: pull(cot_a, v), slope_a)
    sums_a = run(broad, du_a, w_up, at_up, 1)
    close()

    e00, ex = core_sum(*sums_a)
    from_x = pp_x(ex)
    steps.pending += [e00, from_x]
    from_z = move(pp_zl, plus(steps.begin(ez), from_d))
    down_g.zh(1, 0)
    down_g.y_own(1)
    two_rows = [batch(*two_a), batch(*two_b)]
    dus = [[(du_a, 0, 2 * two)], [(du_b, 0, 2 * two)]]
    up_g.make(1, two_rows, dus)
    up_g.make(0, two_rows, dus)
    close()

    grad_in_two = steps.begin(e00).astype(F32) + from_x.astype(F32) + from_z.astype(F32)
    grad_part, grad_gain_two = norm_backward(grad_in_two, normed_two, inverse_two, gain_two)
    grad_resid = cot.astype(F32) + grad_part
    grad_rows = grad_resid.astype(BF)
    grad_far = move(pp_core, grad_rows)
    ax = move(pp_x, grad_rows)
    az = move(pp_zl, grad_rows)
    down_g.zh(1, 1)
    up_g.y_far(0)
    down_g.ready(0)
    out_b = run(broad, act_b, w_down, at_down, 0)
    out_a = run(broad, act_a, w_down, at_down, 0)
    close()

    ax_far = move(pp_core, ax)
    grad_a = (grad_rows, ax, grad_far, ax_far)
    ad = move(pp_x, az)
    up_g.zh(0, 0)
    up_g.y_far(1)
    down_g.zl(0)
    o_b = core_sum(*out_b)
    steps.pending += o_b
    dov_a = run(lambda v: deep(batch(*grad_a[:3], v), w_out, at_out, 1), ax_far)
    proj_a = attend_back(dov_a, qkv_a, start_a, lse_a)
    steps.pending.append(proj_a)
    close()

    az_far, ad_far = move(pp_core, az), move(pp_core, ad)
    grad_b = (az, ad, az_far, ad_far)
    up_g.zh(1, 0)
    up_g.y_own(0)
    oz, od = o_b
    from_od = move(pp_x, od)
    o_a = core_sum(*out_a)
    steps.pending += o_a
    down_g.ready(1)
    dov_b = run(lambda v: deep(batch(*grad_b[:3], v), w_out, at_out, 1), ad_far)
    proj_b = attend_back(dov_b, qkv_b, start_b, lse_b)
    steps.pending.append(proj_b)
    close()

    one_rows = [one_a_rows, one_b_rows]
    projs = [[(proj_a, 0, 2 * two)], [(proj_b, 0, 2 * two)]]
    o00, ox = o_a
    from_ox = move(pp_x, ox)
    from_oz = move(pp_zl, plus(steps.begin(oz), from_od))
    up_g.zh(0, 1)
    up_g.y_own(1)
    qkv_g.make(1, one_rows, projs)
    qkv_g.make(0, one_rows, projs)
    atts = [[(att_a, 0, 2 * two)], [(att_b, 0, 2 * two)]]
    grads = [batch(*grad_a), batch(*grad_b)]
    out_g.make(1, atts, grads)
    close()

    down_g.zl(1)
    qkv_g.y_far(0)
    up_g.zh(1, 1)
    sums_b = run(broad, proj_b, w_qkv, at_qkv, 1)
    out_g.y_far(0)
    up_g.ready(0)
    out_g.make(0, atts, grads)
    block_out = run(
        lambda v: from_rel(
            (resid + (v.astype(F32) + from_ox.astype(F32) + from_oz.astype(F32))).astype(BF)
        ),
        o00,
    )
    close()

    ez, ed = core_sum(*sums_b)
    from_d = pp_x(ed)
    steps.pending += [ez, from_d]
    qkv_g.zh(0, 0, 1)
    qkv_g.y_far(1)
    up_g.zl(0)
    up_g.ready(1)
    sums_a = run(broad, proj_a, w_qkv, at_qkv, 1)
    grad_down = finished(lambda: joined(steps.begin(down_g.result()[0]), down_g.result()[1], 0).astype(F32))
    close()

    e00, ex = core_sum(*sums_a)
    from_x = pp_x(ex)
    steps.pending += [e00, from_x]
    from_z = move(pp_zl, plus(steps.begin(ez), from_d))
    qkv_g.zh(1, 0, 1)
    qkv_g.y_own(0)
    qkv_g.y_own(1)
    close()

    out_g.y_own(0)
    out_g.zh(0, 0, 1)
    up_g.zl(1)
    qkv_g.ready(0, 1)
    qkv_g.value[3, 0] = pp_zl(qkv_g.value[3, 0])
    steps.pending.append(qkv_g.value[3, 0])
    grad_in_one = steps.begin(e00).astype(F32) + from_x.astype(F32) + from_z.astype(F32)
    grad_part, grad_gain_one = norm_backward(grad_in_one, normed_one, inverse_one, gain_one)
    grad_in = from_rel(grad_resid + grad_part)
    gain_grads = from_rel(jnp.stack([grad_gain_one, grad_gain_two]))
    for step in (pp_core, pp_x, pp_y):
        gain_grads = gain_grads + step(gain_grads)
    steps.pending += [grad_in, gain_grads]
    close()

    def parts_first(v):
        return v.reshape(unit, heads, 3, HEAD).transpose(0, 2, 1, 3).reshape(unit, 3, width)

    out_g.ready(0, 1)
    out_g.value[3, 0] = pp_zl(out_g.value[3, 0])
    grad_up = joined(steps.begin(up_g.result()[0]), up_g.result()[1], 1).astype(F32)
    mine, other = qkv_g.result(1)
    grad_qkv = finished(
        lambda: joined(parts_first(steps.begin(mine)), parts_first(other), 2).astype(F32)
    )
    gain_grads = steps.begin(gain_grads)
    gain_grads = gain_grads + pp_zl(gain_grads)
    moving = gain_grads
    for _ in range(ring - 1):
        moving = pp_up(moving)
        gain_grads = gain_grads + moving
    size = D // (n * tp)
    gain_grads = lax.dynamic_slice_in_dim(gain_grads, (f * tp + t) * size, size, axis=1)

    grad_out = joined(*out_g.result(1), 0).astype(F32)

    return (
        block_out,
        grad_in,
        gain_grads[0],
        gain_grads[1],
        grad_qkv,
        grad_out,
        grad_up,
        grad_down,
    )


def solution(mesh):
    return jax.shard_map(
        on_device,
        mesh=mesh,
        in_specs=(
            P(("fsdp", "tp"), None),
            P("fsdp", None),
            P("fsdp", None, "tp"),
            P("tp", "fsdp"),
            P("fsdp", "tp"),
            P("tp", "fsdp"),
            P("fsdp"),
            P("fsdp"),
            P(("fsdp", "tp"), None),
        ),
        out_specs=(
            P(("fsdp", "tp"), None),
            P(("fsdp", "tp"), None),
            P(("fsdp", "tp")),
            P(("fsdp", "tp")),
            P("fsdp", None, "tp"),
            P("tp", "fsdp"),
            P("fsdp", "tp"),
            P("tp", "fsdp"),
        ),
        check_vma=False,
    )
```
